256 devices in a mesh: seq: 8 (over x, core), exp: 32 (over z, y).
Axes of the slice: x: 4, y: 4, z: 8, core: 2. Of those that a mesh axis runs over, the one named last changes fastest.
Arguments:
- queries: bfloat16 [32, 1024, 2048], P('exp', 'seq'), may hold values from -14 to 14
- keys: bfloat16 [32, 1024, 2048], P('exp', 'seq'), may hold values from -6 to 6
- values: bfloat16 [32, 1024, 2048], P('exp', 'seq'), may hold values from -6 to 6
- out_grad: bfloat16 [32, 1024, 2048], P('exp', 'seq'), may hold values from -6 to 6
- norm_gain: float32 [2048], replicated, may hold values from 0.5 to 1.5
- gate_values: float32 [32, 1024, 2], P('exp', 'seq'), may hold values from 0.2 to 1
- expert_ids: int32 [32, 1024, 2], P('exp', 'seq'), may hold values from 0 to 63, all different within a row; in each aligned block of 128 rows (0 to 127, 128 to 255, ..., all dimensions but the last counted through in order) at most 5 rows name the same one
- tile_offsets: int32 [32, 16, 3], P('exp', 'seq'), may hold values from -2 to 2, as said below
- gate_weight: bfloat16 [32, 8, 2048, 512], P('exp', 'seq'), may hold values from -0.125 to 0.125
- up_weight: bfloat16 [32, 8, 2048, 512], P('exp', 'seq'), may hold values from -0.125 to 0.125
- down_weight: bfloat16 [32, 8, 512, 2048], P('exp', 'seq'), may hold values from -0.125 to 0.125
Outputs:
- key_grad: bfloat16 [32, 1024, 2048], P('exp', 'seq')
- value_grad: bfloat16 [32, 1024, 2048], P('exp', 'seq')
The draws below stay inside these ranges and needn't reach their ends.
Inputs may be any that keep to these rules, and one draw needn't show every extreme that they name: `expert_ids`: a token's two ids differ; the tokens of one index pair (one device) name one expert at most 5 times. `tile_offsets`: each row holds 3 different offsets, the first of them 0.
All inputs are finite; a program needn't handle non-finite values.
Results may differ from the reference program's by a relative error of at most 0.013.
Values may be sent and summed in bfloat16 or wider, within the bound.
No kernel may reach another device: no remote copies, remote signals or barrier semaphores. Data moves between devices by JAX's collectives and lax.ppermute only.
A program may use at most 128 MiB of HBM per device.

```python
import math
import jax
import jax.numpy as jnp
import numpy as np
from jax import lax

HEADS = 16
HEAD_DIM = 128
FF = 2048
TILE = 64
NBR = 3
TOK_DEV = 128
D = 2048
SAMPLES = 32
SEQLEN = 1024
NTILES = 16
EXPERTS = 64
FF_PART = 512
CAP = 5
N_SEQ = 8
N_EXP = 32


def paired_fields(key):
    shape = (SAMPLES, SEQLEN, D)
    key_base = jnp.clip(jax.random.normal(jax.random.fold_in(key, 11), shape, jnp.float32), -6.0, 6.0)
    query_base = jnp.clip(jax.random.normal(jax.random.fold_in(key, 12), shape, jnp.float32), -6.0, 6.0)
    return (key_base, query_base)


def draw_queries(key, part):
    return paired_fields(key)[1].astype(jnp.bfloat16)


def draw_keys(key, part):
    return paired_fields(key)[0].astype(jnp.bfloat16)


def draw_tile_offsets(key, part):
    scores = jax.random.randint(jax.random.fold_in(key, 21), (SAMPLES, NTILES, 4), 0, 1 << 20) * 4
    scores = scores + jnp.arange(4, dtype=jnp.int32)
    ranking = jnp.argsort(scores, axis=-1)
    candidates = jnp.array([-2, -1, 1, 2], jnp.int32)
    picked = candidates[ranking[..., :NBR - 1]]
    return jnp.concatenate([jnp.zeros((SAMPLES, NTILES, 1), jnp.int32), picked], axis=-1)


def steps_of(own_key, dims, shards, low, largest):
    gain = 1.0
    for dim, shards_of in shards:
        heights = jax.random.uniform(jax.random.fold_in(jax.random.fold_in(own_key, 6), dim), (shards_of,), jnp.float32, low / len(shards), largest / len(shards))
        gain = gain * jnp.repeat(jnp.exp(heights), dims[dim] // shards_of).reshape((-1,) + (1,) * (len(dims) - 1 - dim))
    return gain


def deal_out(key, own, number, rows, number_of, top, bound, slope):
    sequence = jax.random.permutation(key, number_of)
    crowded, usual = load_shares(number_of, rows * top, bound, slope, True), load_shares(number_of, rows * top, bound, slope, False)
    places = jnp.arange(number_of)

    def named(tallies, turn):
        used = int((tallies > 0).sum())
        fixed = max(1, used // 4)
        moved = fixed + (places - fixed + turn * (used - fixed)) % max(1, number_of - fixed)
        return jnp.zeros((number_of,), jnp.int32).at[sequence[jnp.where(places < fixed, places, moved)]].set(jnp.asarray(tallies, jnp.int32))

    tallies = jnp.where(number % 4 == 0, named(crowded, number // 4), named(usual, number - number // 4 - 1))
    mixed = jax.random.permutation(jax.random.fold_in(own, 3), number_of)
    donor, receiver = mixed[0:number_of // 2 * 2:2], mixed[1:number_of // 2 * 2:2]
    room = jnp.minimum(tallies[donor] - 1, bound - tallies[receiver]) // 2
    room = jnp.where((donor == sequence[0]) | (receiver == sequence[0]) | (tallies[receiver] == 0), 0, jnp.maximum(room, 0))
    moved = jax.random.randint(jax.random.fold_in(own, 4), (number_of // 2,), 0, 1 << 20) % (room + 1)
    tallies = tallies.at[donor].add(-moved).at[receiver].add(moved)
    labels = jnp.searchsorted(jnp.cumsum(tallies), jnp.arange(rows * top), side="right").astype(jnp.int32)
    grid = labels.reshape(top, rows).T
    grid = grid[jax.random.permutation(jax.random.fold_in(own, 1), rows)]
    turn = jax.random.randint(jax.random.fold_in(own, 2), (rows, 1), 0, top)
    return jnp.take_along_axis(grid, (jnp.arange(top)[None, :] + turn) % top, axis=1)


def load_shares(count, total, limit, lean, full):
    loads = [(1 << 20) // math.isqrt(rank ** lean) + 1 for rank in range(1, count + 1)]
    largest = limit if full else min(limit, max(-(-total // count), total * loads[0] // sum(loads)))
    least = 1 if total - largest >= count - 1 else 0
    counts, spare = [largest] + [least] * (count - 1), total - largest - least * (count - 1)
    while spare > 0:
        movable = [i for i in range(1, count) if counts[i] < largest] or [i for i in range(1, count) if counts[i] < limit]
        pool, remaining = sum([loads[i] for i in movable]), spare
        for i in movable:
            addition = min(limit - counts[i], max(1, remaining * loads[i] // pool), spare)
            counts[i] = counts[i] + addition
            spare = spare - addition
    return np.array(counts)


def scatter_about(rng, dims, scale, most, cuts=(), kind=jnp.bfloat16):
    factor_of = steps_of(rng, dims, cuts, -0.22, 0.18) if cuts else 1.0
    result = jax.random.normal(rng, dims, jnp.float32) * scale * factor_of
    return jnp.minimum(jnp.maximum(result, -most), most).astype(kind)


def setup_inputs(seed: int = 0) -> dict:
    splits = jax.random.split(jax.random.key(seed), 12)
    queries = draw_queries(jax.random.fold_in(splits[11], 71), 0)
    keys = draw_keys(jax.random.fold_in(splits[11], 71), 0)
    values = scatter_about(splits[2], (SAMPLES, SEQLEN, D), 1.0, 6.0, ((0, 32), (1, 8)))
    out_grad = scatter_about(splits[3], (SAMPLES, SEQLEN, D), 1.0, 6.0, ((0, 32), (1, 8)))
    norm_gain = jnp.clip(1.0 + 0.1 * jax.random.normal(splits[4], (D,), jnp.float32), 0.5, 1.5)
    gate_values = jnp.clip(jnp.exp(math.log(1.0) - 1.609438 * jax.random.uniform(splits[5], (SAMPLES, SEQLEN, 2), jnp.float32) ** steps_of(splits[5], (SAMPLES, SEQLEN, 2), ((0, 32), (1, 8)), -0.2, 0.2)), 0.2, 1.0)
    expert_ids_keys = jax.random.split(jax.random.fold_in(splits[6], 1), SAMPLES * SEQLEN // TOK_DEV)
    expert_ids_turns = jax.random.permutation(jax.random.fold_in(splits[6], 3), SAMPLES * SEQLEN // TOK_DEV)
    expert_ids = jax.vmap(lambda own, number: deal_out(jax.random.fold_in(splits[6], 2), own, number, TOK_DEV, EXPERTS, 2, CAP, 2))(expert_ids_keys, expert_ids_turns).reshape((SAMPLES, SEQLEN, 2))
    tile_offsets = draw_tile_offsets(jax.random.fold_in(splits[11], 71), 0)
    gate_weight = scatter_about(splits[8], (N_EXP, N_SEQ, D, FF_PART), D ** -0.5, 0.125, ((0, 32), (1, 8)))
    up_weight = scatter_about(splits[9], (N_EXP, N_SEQ, D, FF_PART), D ** -0.5, 0.125, ((0, 32), (1, 8)))
    down_weight = scatter_about(splits[10], (N_EXP, N_SEQ, FF_PART, D), FF ** -0.5, 0.125, ((0, 32), (1, 8)))
    return {"queries": queries, "keys": keys, "values": values, "out_grad": out_grad, "norm_gain": norm_gain, "gate_values": gate_values, "expert_ids": expert_ids, "tile_offsets": tile_offsets, "gate_weight": gate_weight, "up_weight": up_weight, "down_weight": down_weight}


epsilon = 1e-06

def barrier_round(value):
    return lax.optimization_barrier(value.astype(jnp.bfloat16)).astype(jnp.float32)

def window_operands(query_s, key_s, value_s, offsets):
    tile_total = query_s.shape[0] // TILE
    tile_ids = jnp.arange(tile_total, dtype=jnp.int32)[:, None] + offsets.astype(jnp.int32)
    valid = (tile_ids >= 0) & (tile_ids < tile_total)
    clipped = jnp.clip(tile_ids, 0, tile_total - 1).astype(jnp.int32)
    tile_shape = (tile_total, TILE, HEADS, HEAD_DIM)
    window_shape = (tile_total, NBR * TILE, HEADS, HEAD_DIM)
    query_t = query_s.reshape(tile_shape).astype(jnp.float32)
    key_t = key_s.reshape(tile_shape).astype(jnp.float32)[clipped].reshape(window_shape)
    value_t = value_s.reshape(tile_shape).astype(jnp.float32)[clipped].reshape(window_shape)
    key_mask = jnp.repeat(valid, TILE, axis=1)
    return (query_t, key_t, value_t, key_mask, clipped)

def attention_weights(query_t, key_t, key_mask):
    scores = jnp.einsum('tqhd,tkhd->thqk', query_t, key_t) * HEAD_DIM ** (-0.5)
    scores = jnp.where(key_mask[:, None, None, :], scores, -jnp.inf)
    row_max = lax.optimization_barrier(jnp.max(scores, axis=-1, keepdims=True))
    raised = jnp.exp(scores - row_max)
    return raised / lax.optimization_barrier(jnp.sum(raised, axis=-1, keepdims=True))

def forward_sample(operands):
    query_s, key_s, value_s, offsets = operands
    query_t, key_t, value_t, key_mask, clipped = window_operands(query_s, key_s, value_s, offsets)
    weights_b = barrier_round(attention_weights(query_t, key_t, key_mask))
    attn_out = jnp.einsum('thqk,tkhd->tqhd', weights_b, value_t)
    return attn_out.reshape(query_s.shape[0], HEADS * HEAD_DIM)

def backward_sample(operands):
    query_s, key_s, value_s, offsets, grad_s = operands
    query_t, key_t, value_t, key_mask, clipped = window_operands(query_s, key_s, value_s, offsets)
    tile_total = query_t.shape[0]
    weights_f = attention_weights(query_t, key_t, key_mask)
    weights_b = barrier_round(weights_f)
    grad_t = grad_s.astype(jnp.float32).reshape(tile_total, TILE, HEADS, HEAD_DIM)
    prob_grad = jnp.einsum('tqhd,tkhd->thqk', grad_t, value_t)
    inner_sum = lax.optimization_barrier(jnp.sum(weights_f * prob_grad, axis=-1, keepdims=True))
    score_grad = barrier_round(weights_f * (prob_grad - inner_sum))
    key_part = jnp.einsum('thqk,tqhd->tkhd', score_grad, query_t) * HEAD_DIM ** (-0.5)
    value_part = jnp.einsum('thqk,tqhd->tkhd', weights_b, grad_t)
    flat_ids = clipped.reshape(-1)
    part_shape = (tile_total * NBR, TILE, HEADS, HEAD_DIM)
    tile_shape = (tile_total, TILE, HEADS, HEAD_DIM)
    key_sum = jnp.zeros(tile_shape, jnp.float32).at[flat_ids].add(key_part.reshape(part_shape))
    value_sum = jnp.zeros(tile_shape, jnp.float32).at[flat_ids].add(value_part.reshape(part_shape))
    out_shape = (query_s.shape[0], HEADS * HEAD_DIM)
    return (key_sum.reshape(out_shape).astype(jnp.bfloat16), value_sum.reshape(out_shape).astype(jnp.bfloat16))

def expert_part(rows_in, rows_grad, gate_w, up_w, down_w):
    gate_proj = jnp.dot(rows_in, gate_w, preferred_element_type=jnp.float32)
    up_proj = jnp.dot(rows_in, up_w, preferred_element_type=jnp.float32)
    hidden_grad = jnp.dot(rows_grad, down_w.T, preferred_element_type=jnp.float32)
    sig = jax.nn.sigmoid(gate_proj)
    grad_up = (hidden_grad * gate_proj * sig).astype(jnp.bfloat16)
    grad_gate = (hidden_grad * up_proj * sig * (1.0 + gate_proj * (1.0 - sig))).astype(jnp.bfloat16)
    total = jnp.dot(grad_gate, gate_w.T, preferred_element_type=jnp.float32)
    total = total + jnp.dot(grad_up, up_w.T, preferred_element_type=jnp.float32)
    return total

def reference(queries, keys, values, out_grad, norm_gain, gate_values, expert_ids, tile_offsets, gate_weight, up_weight, down_weight):
    width = HEADS * HEAD_DIM
    attn_out = lax.map(forward_sample, (queries, keys, values, tile_offsets))
    inv_rms = lax.rsqrt(lax.optimization_barrier(jnp.mean(attn_out * attn_out, axis=-1, keepdims=True)) + epsilon)
    unit = attn_out * inv_rms
    normed = (unit * norm_gain).astype(jnp.bfloat16)
    tokens_total = SAMPLES * SEQLEN
    group = N_SEQ // 2
    max_rows = N_SEQ * N_EXP * CAP
    flat_experts = expert_ids.reshape(-1).astype(jnp.int32)
    one_hot = (flat_experts[:, None] == jnp.arange(EXPERTS, dtype=jnp.int32)[None, :]).astype(jnp.int32)
    rank_index = lax.optimization_barrier(jnp.sum(jnp.cumsum(one_hot, axis=0) * one_hot, axis=1)) - 1
    slot_index = (flat_experts * max_rows + rank_index).astype(jnp.int32)
    owner = jnp.full((EXPERTS * max_rows,), -1, jnp.int32)
    owner = owner.at[slot_index].set(jnp.arange(tokens_total * 2, dtype=jnp.int32)).reshape(EXPERTS, max_rows)
    normed_flat = normed.reshape(tokens_total, width)
    grad_flat = out_grad.reshape(tokens_total, width)
    gate_all = gate_weight.reshape(EXPERTS, group, width, FF_PART)
    up_all = up_weight.reshape(EXPERTS, group, width, FF_PART)
    down_all = down_weight.reshape(EXPERTS, group, FF_PART, width)

    def expert_rows(operands):
        gate_w, up_w, down_w, owner_row = operands
        live = owner_row >= 0
        token = jnp.where(live, owner_row // 2, 0).astype(jnp.int32)
        rows_in = jnp.where(live[:, None], normed_flat[token], jnp.zeros((), jnp.bfloat16))
        rows_grad = jnp.where(live[:, None], grad_flat[token], jnp.zeros((), jnp.bfloat16))
        total = jnp.zeros((max_rows, width), jnp.float32)
        for part in range(group):
            total = total + barrier_round(expert_part(rows_in, rows_grad, gate_w[part], up_w[part], down_w[part]))
        return total.astype(jnp.bfloat16)
    returned = lax.map(expert_rows, (gate_all, up_all, down_all, owner))
    route_grad = returned.reshape(EXPERTS * max_rows, width)[slot_index]
    route_grad = route_grad.reshape(SAMPLES, SEQLEN, 2, width).astype(jnp.float32)
    normed_grad = lax.optimization_barrier(jnp.sum(gate_values[..., None] * route_grad, axis=2))
    scaled = normed_grad * norm_gain
    attn_grad = out_grad.astype(jnp.float32) + inv_rms * (scaled - unit * lax.optimization_barrier(jnp.mean(scaled * unit, axis=-1, keepdims=True)))
    attn_grad_b = attn_grad.astype(jnp.bfloat16)
    key_grad, value_grad = lax.map(backward_sample, (queries, keys, values, tile_offsets, attn_grad_b))
    return (key_grad, value_grad)
```

```python
import jax
import jax.numpy as jnp
import numpy as np
from jax import lax
from jax.experimental import pallas as pl
from jax.experimental.pallas import tpu as pltpu
from jax.sharding import PartitionSpec as P

HEAD_DIM = 128
TILE = 64
NBR = 3
CAP = 5
PIECES = 8
GROUP = 8
EPSILON = 1e-06
MICRO = 1 << 30
F32 = jnp.float32
BF16 = jnp.bfloat16

CELL = PIECES * CAP
CHUNK = GROUP * CELL
ROWS = GROUP * CAP


def shuffle_matrix():
    out = np.zeros((CHUNK, CHUNK), np.float32)
    for d in range(GROUP):
        for q in range(PIECES):
            for r in range(CAP):
                out[d * CELL + q * CAP + r, q * ROWS + d * CAP + r] = 1.0
    return out


def dot(a, b):
    return jnp.dot(a, b, preferred_element_type=F32)


def dot_nt(a, b):
    return lax.dot_general(a, b, (((1,), (1,)), ((), ())), preferred_element_type=F32)


def dot_tn(a, b):
    return lax.dot_general(a, b, (((0,), (0,)), ((), ())), preferred_element_type=F32)


def to_wire(rows_ref, base, perm, chunk, piece):
    start = base + chunk * ROWS
    stacked = jnp.concatenate(
        [rows_ref[start : start + ROWS, q * piece : (q + 1) * piece] for q in range(PIECES)], axis=0
    )
    return dot(perm, stacked.astype(BF16)).astype(BF16)


def from_wire(block_ref, rows_ref, base, perm_t, chunks, piece):
    if not isinstance(block_ref, list):
        block_ref = [block_ref[c * CHUNK : (c + 1) * CHUNK, :] for c in range(chunks)]
    for pair in range(chunks // 2):
        low = dot(perm_t, block_ref[2 * pair])
        high = dot(perm_t, block_ref[2 * pair + 1])
        start = base + 2 * pair * ROWS
        for q in range(PIECES):
            both = jnp.concatenate(
                [low[q * ROWS : (q + 1) * ROWS], high[q * ROWS : (q + 1) * ROWS]], axis=0
            )
            rows_ref[start : start + 2 * ROWS, q * piece : (q + 1) * piece] = both.astype(BF16)


def slot_rows(ids_ref, half, experts):
    tokens = ids_ref.shape[1]
    first = ids_ref[0:1, :]
    second = ids_ref[1:2, :]
    names = lax.broadcasted_iota(jnp.int32, (experts, tokens), 0)
    hot0 = (names == first).astype(F32)
    hot1 = (names == second).astype(F32)
    before = (
        lax.broadcasted_iota(jnp.int32, (tokens, tokens), 0)
        < lax.broadcasted_iota(jnp.int32, (tokens, tokens), 1)
    ).astype(F32).astype(BF16)
    seen0 = dot(hot0.astype(BF16), before)
    seen1 = dot(hot1.astype(BF16), before) + jnp.sum(hot0, axis=1, keepdims=True)
    rank0 = jnp.sum(hot0 * seen0, axis=0, keepdims=True).astype(jnp.int32)
    rank1 = jnp.sum(hot1 * seen1, axis=0, keepdims=True).astype(jnp.int32)
    slots = (experts // 2) * CAP
    slot0 = ((first & 1) ^ half) * slots + (first >> 1) * CAP + rank0
    slot1 = ((second & 1) ^ half) * slots + (second >> 1) * CAP + rank1
    return slot0, slot1


def slot_cols(ids_ref, half, experts):
    tokens = ids_ref.shape[0]
    first = ids_ref[:, 0:1]
    second = ids_ref[:, 1:2]
    names = lax.broadcasted_iota(jnp.int32, (tokens, experts), 1)
    hot0 = (names == first).astype(F32)
    hot1 = (names == second).astype(F32)
    before = (
        lax.broadcasted_iota(jnp.int32, (tokens, tokens), 1)
        < lax.broadcasted_iota(jnp.int32, (tokens, tokens), 0)
    ).astype(F32).astype(BF16)
    seen0 = dot(before, hot0.astype(BF16))
    seen1 = dot(before, hot1.astype(BF16)) + jnp.sum(hot0, axis=0, keepdims=True)
    rank0 = jnp.sum(hot0 * seen0, axis=1, keepdims=True).astype(jnp.int32)
    rank1 = jnp.sum(hot1 * seen1, axis=1, keepdims=True).astype(jnp.int32)
    slots = (experts // 2) * CAP
    slot0 = ((first & 1) ^ half) * slots + (first >> 1) * CAP + rank0
    slot1 = ((second & 1) ^ half) * slots + (second >> 1) * CAP + rank1
    return slot0, slot1


def place_rows(ids_ref, half, experts, x, rows_ref):
    slot0, slot1 = slot_rows(ids_ref, half, experts)
    places = lax.broadcasted_iota(jnp.int32, (rows_ref.shape[0], x.shape[0]), 0)
    hot = ((places == slot0) | (places == slot1)).astype(F32).astype(BF16)
    rows_ref[...] = dot(hot, x)


def send_rows(seq_ref, ids_ref, x, perm_ref, out_ref, rows_ref):
    columns = out_ref.shape[0]
    piece = out_ref.shape[3]
    place_rows(ids_ref, seq_ref[0] // 4, 2 * columns, x, rows_ref)
    perm = perm_ref[...]
    for rel in range(2):
        for chunk in range(columns // GROUP):
            block = to_wire(rows_ref, rel * columns * CAP, perm, chunk, piece)
            out_ref[chunk * GROUP : (chunk + 1) * GROUP, rel] = block.reshape(GROUP, CELL, piece)


def grad_kernel(seq_ref, ids_ref, x_ref, perm_ref, out_ref, rows_ref):
    send_rows(seq_ref, ids_ref, x_ref[...], perm_ref, out_ref, rows_ref)


def tile_places(seq_ref, offs_ref, tile, tiles, total):
    places = []
    valid = []
    for m in range(NBR):
        off = offs_ref[tile, m]
        places.append(pl.multiple_of((tile + 2 + off) * TILE, TILE))
        where = seq_ref[0] * tiles + tile + off
        valid.append((where >= 0) & (where < total))
    return places, valid


def fill_halo(dst_ref, left_ref, own_ref, right_ref):
    count = own_ref.shape[0]
    dst_ref[0:count, :] = left_ref[...]
    dst_ref[count : 2 * count, :] = own_ref[...]
    dst_ref[2 * count : 3 * count, :] = right_ref[...]


def forward_kernel(
    seq_ref, offs_ref, ids_ref, q_ref, kl_ref, k_ref, kr_ref, vl_ref, v_ref, vr_ref, gain_ref,
    perm_ref, wts_ref, unit_ref, inv_ref, sent_ref, kx_ref, vx_ref, out_ref, rows_ref, total_tiles,
):
    fill_halo(kx_ref, kl_ref, k_ref, kr_ref)
    fill_halo(vx_ref, vl_ref, v_ref, vr_ref)
    count, width = q_ref.shape
    heads = width // HEAD_DIM
    tiles = count // TILE
    scale = HEAD_DIM ** (-0.5)
    lane = lax.broadcasted_iota(jnp.int32, (TILE, NBR * TILE), 1) // TILE
    spots = []
    biases = []
    for t in range(tiles):
        places, valid = tile_places(seq_ref, offs_ref, t, tiles, total_tiles)
        bias = jnp.zeros((TILE, NBR * TILE), F32)
        for m in range(NBR):
            lost = jnp.where(valid[m], 0.0, -jnp.inf).astype(F32)
            bias = jnp.where(lane == m, lost, bias)
        spots.append(places)
        biases.append(bias)

    def one_head(h):
        lanes = pl.ds(pl.multiple_of(h * HEAD_DIM, HEAD_DIM), HEAD_DIM)
        for t in range(tiles):
            rows = slice(t * TILE, (t + 1) * TILE)
            k3 = jnp.concatenate([kx_ref[pl.ds(p, TILE), lanes] for p in spots[t]], axis=0)
            v3 = jnp.concatenate([vx_ref[pl.ds(p, TILE), lanes] for p in spots[t]], axis=0)
            scores = dot_nt(q_ref[rows, lanes], k3) * scale + biases[t]
            raised = jnp.exp(scores - jnp.max(scores, axis=-1, keepdims=True))
            weights = raised / jnp.sum(raised, axis=-1, keepdims=True)
            wts_ref[t * heads + h] = weights
            out_ref[rows, lanes] = dot(weights.astype(BF16), v3)

    def body(step, carry):
        for u in range(4):
            one_head(step * 4 + u)
        return carry

    lax.fori_loop(0, heads // 4, body, 0)
    out = out_ref[...]
    inv = lax.rsqrt(jnp.mean(out * out, axis=-1, keepdims=True) + EPSILON)
    unit = out * inv
    unit_ref[...] = unit
    inv_ref[...] = jnp.broadcast_to(inv, inv_ref.shape)
    normed = (unit * gain_ref[...]).astype(BF16)
    send_rows(seq_ref, ids_ref, normed, perm_ref, sent_ref, rows_ref)


def hidden_kernel(
    g0_ref, g1_ref, g2_ref, g3_ref, perm_t_ref, down0_ref, down1_ref, o0_ref, o1_ref, o2_ref,
    rows_ref, w_ref, sems,
):
    copies = [
        pltpu.make_async_copy(src, w_ref.at[i], sems.at[i])
        for i, src in enumerate((down0_ref, down1_ref))
    ]
    for copy in copies:
        copy.start()
    piece = g0_ref.shape[1]
    chunks = g0_ref.shape[0] // CHUNK
    slots = chunks * ROWS
    perm_t = perm_t_ref[...]
    for b, block in enumerate((g0_ref, g1_ref, g2_ref, g3_ref)):
        from_wire(block, rows_ref, b * slots, perm_t, chunks, piece)
    part = down0_ref.shape[0]
    for i, copy in enumerate(copies):
        copy.wait()
        cols = slice(i * part, (i + 1) * part)
        both = dot_nt(rows_ref[...], w_ref[i])
        o0_ref[:, cols] = both[:slots]
        o1_ref[:, cols] = both[slots : 3 * slots]
        o2_ref[:, cols] = both[3 * slots :]


def expert_kernel(*refs, blocks):
    ins = refs[:blocks]
    hg_ref, perm_ref, perm_t_ref = refs[blocks : blocks + 3]
    weights = refs[blocks + 3 : blocks + 7]
    outs = refs[blocks + 7 : 2 * blocks + 7]
    rows_ref, w_ref, act_ref, total_ref, sems = refs[2 * blocks + 7 :]
    copies = [pltpu.make_async_copy(src, w_ref.at[i], sems.at[i]) for i, src in enumerate(weights)]
    for copy in copies:
        copy.start()
    piece = ins[0].shape[1]
    chunks = ins[0].shape[0] // CHUNK
    perm_t = perm_t_ref[...]
    for b, block in enumerate(ins):
        from_wire(block, rows_ref, b * chunks * ROWS, perm_t, chunks, piece)
    part = w_ref.shape[2]
    for i in range(2):
        copies[2 * i].wait()
        gate_proj = dot(rows_ref[...], w_ref[2 * i])
        copies[2 * i + 1].wait()
        up_proj = dot(rows_ref[...], w_ref[2 * i + 1])
        hidden = hg_ref[:, i * part : (i + 1) * part]
        sig = jax.nn.sigmoid(gate_proj)
        act_ref[2 * i + 1] = (hidden * gate_proj * sig).astype(BF16)
        act_ref[2 * i] = (hidden * up_proj * sig * (1.0 + gate_proj * (1.0 - sig))).astype(BF16)
    width = total_ref.shape[1]
    for n in range(width // 512):
        cols = slice(n * 512, (n + 1) * 512)
        total = dot_nt(act_ref[0], w_ref[0, cols, :])
        for i in range(1, 4):
            total = total + dot_nt(act_ref[i], w_ref[i, cols, :])
        total_ref[:, cols] = total
    perm = perm_ref[...]
    for b, dst in enumerate(outs):
        for chunk in range(chunks):
            block = to_wire(total_ref, b * chunks * ROWS, perm, chunk, piece)
            dst[chunk * CHUNK : (chunk + 1) * CHUNK, :] = block


def backward_kernel(
    seq_ref, offs_ref, ids_ref, gates_ref, home_ref, grad_ref, unit_ref, inv_ref, q_ref,
    vl_ref, v_ref, vr_ref, wts_ref, gain_ref, perm_t_ref, k_out_ref, v_out_ref, left_ref,
    right_ref, vx_ref, rows_ref, ag_ref, ka_ref, va_ref, total_tiles,
):
    count, width = q_ref.shape
    heads = width // HEAD_DIM
    tiles = count // TILE
    scale = HEAD_DIM ** (-0.5)
    fill_halo(vx_ref, vl_ref, v_ref, vr_ref)
    ka_ref[...] = jnp.zeros_like(ka_ref)
    va_ref[...] = jnp.zeros_like(va_ref)
    columns, _, _, piece = home_ref.shape
    chunks = columns // GROUP
    perm_t = perm_t_ref[...]
    for rel in range(2):
        blocks = [
            home_ref[c * GROUP : (c + 1) * GROUP, rel].reshape(CHUNK, piece) for c in range(chunks)
        ]
        from_wire(blocks, rows_ref, rel * chunks * ROWS, perm_t, chunks, piece)
    slot0, slot1 = slot_cols(ids_ref, seq_ref[0] // 4, 2 * columns)
    places = lax.broadcasted_iota(jnp.int32, (count, rows_ref.shape[0]), 1)
    mix = jnp.where(places == slot0, gates_ref[:, 0:1], 0.0)
    mix = jnp.where(places == slot1, gates_ref[:, 1:2], mix)
    high = mix.astype(BF16)
    low = (mix - high.astype(F32)).astype(BF16)
    normed_grad = dot(high, rows_ref[...]) + dot(low, rows_ref[...])
    scaled = normed_grad * gain_ref[...]
    unit = unit_ref[...]
    inner = jnp.mean(scaled * unit, axis=-1, keepdims=True)
    attn_grad = grad_ref[...].astype(F32) + inv_ref[:, 0:1] * (scaled - unit * inner)
    ag_ref[...] = attn_grad.astype(BF16)
    spots = [tile_places(seq_ref, offs_ref, t, tiles, total_tiles)[0] for t in range(tiles)]

    def one_head(h):
        lanes = pl.ds(pl.multiple_of(h * HEAD_DIM, HEAD_DIM), HEAD_DIM)
        for t in range(tiles):
            rows = slice(t * TILE, (t + 1) * TILE)
            v3 = jnp.concatenate([vx_ref[pl.ds(p, TILE), lanes] for p in spots[t]], axis=0)
            ag = ag_ref[rows, lanes]
            weights = wts_ref[t * heads + h]
            prob_grad = dot_nt(ag, v3)
            sums = jnp.sum(weights * prob_grad, axis=-1, keepdims=True)
            score_grad = (weights * (prob_grad - sums)).astype(BF16)
            key_part = dot_tn(score_grad, q_ref[rows, lanes]) * scale
            value_part = dot_tn(weights.astype(BF16), ag)
            for m in range(NBR):
                at = pl.ds(spots[t][m], TILE)
                ka_ref[at, lanes] += key_part[m * TILE : (m + 1) * TILE]
                va_ref[at, lanes] += value_part[m * TILE : (m + 1) * TILE]

    def body(step, carry):
        for u in range(4):
            one_head(step * 4 + u)
        return carry

    lax.fori_loop(0, heads // 4, body, 0)
    k_out_ref[...] = ka_ref[count : 2 * count, :]
    v_out_ref[...] = va_ref[count : 2 * count, :]
    left_ref[0] = ka_ref[0:count, :].astype(BF16)
    left_ref[1] = va_ref[0:count, :].astype(BF16)
    right_ref[0] = ka_ref[2 * count : 3 * count, :].astype(BF16)
    right_ref[1] = va_ref[2 * count : 3 * count, :].astype(BF16)


def call(body, outs, kinds, scratch, name, flops):
    spaces = {"s": pltpu.SMEM, "v": pltpu.VMEM, "a": pl.ANY}
    return pl.pallas_call(
        body,
        out_shape=outs,
        in_specs=[pl.BlockSpec(memory_space=spaces[kind]) for kind in kinds],
        out_specs=jax.tree.map(lambda _: pl.BlockSpec(memory_space=pltpu.VMEM), outs),
        scratch_shapes=scratch,
        compiler_params=pltpu.CompilerParams(vmem_limit_bytes=56 * 1024 * 1024),
        cost_estimate=pl.CostEstimate(flops=flops, transcendentals=0, bytes_accessed=1 << 20),
        name=name,
    )


def shape(dims, kind):
    return jax.ShapeDtypeStruct(dims, kind)


def on_device(
    queries, keys, values, out_grad, norm_gain, gate_values, expert_ids, tile_offsets, gate_weight,
    up_weight, down_weight,
):
    count, width = queries.shape[1:]
    heads = width // HEAD_DIM
    tiles = count // TILE
    seq_count = lax.axis_size("seq")
    columns = lax.axis_size("exp")
    total_tiles = tiles * seq_count
    piece = width // PIECES
    slots = columns * CAP
    seq = lax.axis_index("seq").astype(jnp.int32).reshape(1)
    ids = expert_ids[0]
    ids_t = ids.T
    gain = norm_gain.reshape(1, width)
    perm = jnp.asarray(shuffle_matrix(), BF16)
    perm_t = jnp.asarray(shuffle_matrix().T, BF16)
    q, k, v, grad = queries[0], keys[0], values[0], out_grad[0]
    gate, up, down = gate_weight[0, 0], up_weight[0, 0], down_weight[0, 0]
    wire = (columns, 2, CELL, piece)
    flat = (columns * CELL, piece)

    up_by = [(i, i + 1) for i in range(seq_count - 1)]
    down_by = [(i + 1, i) for i in range(seq_count - 1)]

    def swap(x, bits):
        return lax.ppermute(x, "seq", [(i, i ^ bits) for i in range(seq_count)])

    def exchange(x):
        return lax.all_to_all(x, "exp", split_axis=0, concat_axis=0, tiled=True)

    kl, kr = lax.ppermute(k, "seq", up_by), lax.ppermute(k, "seq", down_by)
    vl, vr = lax.ppermute(v, "seq", up_by), lax.ppermute(v, "seq", down_by)

    barrier = lax.optimization_barrier
    sent_grad = call(
        grad_kernel, shape(wire, BF16), "svvv", [pltpu.VMEM((2 * slots, width), F32)],
        "place_grad", 4 * MICRO,
    )(seq, ids_t, grad, perm)
    got_grad = exchange(sent_grad)
    gate_s, up_s, down_s = swap(gate, 1), swap(up, 1), swap(down, 1)

    q_after, _ = barrier((q, sent_grad))
    wts, unit, inv, sent = call(
        lambda *refs: forward_kernel(*refs, total_tiles=total_tiles),
        (
            shape((tiles * heads, TILE, NBR * TILE), F32),
            shape((count, width), F32),
            shape((count, HEAD_DIM), F32),
            shape(wire, BF16),
        ),
        "ssv" + "v" * 9,
        [
            pltpu.VMEM((3 * count, width), BF16),
            pltpu.VMEM((3 * count, width), BF16),
            pltpu.VMEM((count, width), F32),
            pltpu.VMEM((2 * slots, width), F32),
        ],
        "attention", 16 * MICRO,
    )(seq, tile_offsets[0], ids_t, q_after, kl, k, kr, vl, v, vr, gain, perm)

    sent, got_grad = barrier((sent, got_grad))
    got = exchange(sent)
    g0, grad_oth = got_grad[:, 0].reshape(flat), got_grad[:, 1].reshape(flat)
    g1, g2, g3 = swap(grad_oth, 6), swap(g0, 2), swap(grad_oth, 4)
    got, g1, g2, g3 = barrier((got, g1, g2, g3))
    n0, oth = got[:, 0].reshape(flat), got[:, 1].reshape(flat)
    n1, n2 = swap(oth, 6), swap(n0, 2)

    part = down.shape[0]
    hidden = call(
        hidden_kernel,
        tuple(shape((m * slots, 2 * part), F32) for m in (1, 2, 1)),
        "vvvvvaa",
        [
            pltpu.VMEM((4 * slots, width), BF16),
            pltpu.VMEM((2, part, width), BF16),
            pltpu.SemaphoreType.DMA((2,)),
        ],
        "hidden", 8 * MICRO,
    )(g0, g1, g2, g3, perm_t, down, down_s)

    def expert(ins, hg, micros):
        blocks = len(ins)
        return call(
            lambda *refs: expert_kernel(*refs, blocks=blocks),
            (shape(flat, BF16),) * blocks,
            "v" * (blocks + 3) + "aaaa",
            [
                pltpu.VMEM((blocks * slots, width), BF16),
                pltpu.VMEM((4, width, part), BF16),
                pltpu.VMEM((4, blocks * slots, part), BF16),
                pltpu.VMEM((blocks * slots, width), F32),
                pltpu.SemaphoreType.DMA((4,)),
            ],
            "expert", micros * MICRO,
        )(*ins, hg, perm, perm_t, gate, up, gate_s, up_s)

    (p0,) = expert((n0,), hidden[0], 7)
    p0, n1, n2, oth = barrier((p0, n1, n2, oth))
    n3 = swap(oth, 4)
    p1, p2 = expert((n1, n2), hidden[1], 11)
    (p3,) = expert((n3,), hidden[2], 7)
    h1, h2 = swap(p1, 6), swap(p2, 2)
    h3 = swap(p3, 4)
    own = (p0.astype(F32) + h2.astype(F32)).astype(BF16).reshape(columns, 1, CELL, piece)
    oth = (h1.astype(F32) + h3.astype(F32)).astype(BF16).reshape(columns, 1, CELL, piece)
    home = exchange(jnp.concatenate([own, oth], axis=1))

    k_own, v_own, left, right = call(
        lambda *refs: backward_kernel(*refs, total_tiles=total_tiles),
        (
            shape((count, width), F32),
            shape((count, width), F32),
            shape((2, count, width), BF16),
            shape((2, count, width), BF16),
        ),
        "ss" + "v" * 13,
        [
            pltpu.VMEM((3 * count, width), BF16),
            pltpu.VMEM((2 * slots, width), BF16),
            pltpu.VMEM((count, width), BF16),
            pltpu.VMEM((3 * count, width), F32),
            pltpu.VMEM((3 * count, width), F32),
        ],
        "attention_grad", 13 * MICRO,
    )(
        seq, tile_offsets[0], ids, gate_values[0], home, grad, unit, inv, q, vl, v, vr, wts, gain,
        perm_t,
    )
    from_right = lax.ppermute(left, "seq", down_by).astype(F32)
    from_left = lax.ppermute(right, "seq", up_by).astype(F32)
    key_out = (k_own + from_right[0] + from_left[0]).astype(BF16)
    value_out = (v_own + from_right[1] + from_left[1]).astype(BF16)
    return (key_out[None], value_out[None])


def solution(mesh):
    rows = P("exp", "seq", None)
    weights = P("exp", "seq", None, None)
    return jax.shard_map(
        on_device,
        mesh=mesh,
        in_specs=(rows, rows, rows, rows, P(), rows, rows, rows, weights, weights, weights),
        out_specs=(rows, rows),
        check_vma=False,
    )
```

```python
import jax
import jax.numpy as jnp
import numpy as np
from jax import lax
from jax.experimental import pallas as pl
from jax.experimental.pallas import tpu as pltpu
from jax.sharding import PartitionSpec as P

HEAD_DIM = 128
TILE = 64
NBR = 3
CAP = 5
PIECES = 8
GROUP = 8
EPSILON = 1e-06
ATTN = 24
MICRO = 1 << 30
F32 = jnp.float32
BF16 = jnp.bfloat16

CELL = PIECES * CAP
CHUNK = GROUP * CELL
ROWS = GROUP * CAP


def shuffle_matrix():
    out = np.zeros((CHUNK, CHUNK), np.float32)
    for d in range(GROUP):
        for q in range(PIECES):
            for r in range(CAP):
                out[d * CELL + q * CAP + r, q * ROWS + d * CAP + r] = 1.0
    return out


def dot(a, b):
    return jnp.dot(a, b, preferred_element_type=F32)


def dot_nt(a, b):
    return lax.dot_general(a, b, (((1,), (1,)), ((), ())), preferred_element_type=F32)


def dot_tn(a, b):
    return lax.dot_general(a, b, (((0,), (0,)), ((), ())), preferred_element_type=F32)


def to_wire(rows_ref, base, perm, chunk, piece):
    start = base + chunk * ROWS
    stacked = jnp.concatenate(
        [rows_ref[start : start + ROWS, q * piece : (q + 1) * piece] for q in range(PIECES)], axis=0
    )
    return dot(perm, stacked.astype(BF16)).astype(BF16)


def from_wire(block_ref, rows_ref, base, perm_t, chunks, piece):
    if not isinstance(block_ref, list):
        block_ref = [block_ref[c * CHUNK : (c + 1) * CHUNK, :] for c in range(chunks)]
    for pair in range(chunks // 2):
        low = dot(perm_t, block_ref[2 * pair])
        high = dot(perm_t, block_ref[2 * pair + 1])
        start = base + 2 * pair * ROWS
        for q in range(PIECES):
            both = jnp.concatenate(
                [low[q * ROWS : (q + 1) * ROWS], high[q * ROWS : (q + 1) * ROWS]], axis=0
            )
            rows_ref[start : start + 2 * ROWS, q * piece : (q + 1) * piece] = both.astype(BF16)


def slot_rows(ids_ref, half, experts):
    tokens = ids_ref.shape[1]
    first = ids_ref[0:1, :]
    second = ids_ref[1:2, :]
    names = lax.broadcasted_iota(jnp.int32, (experts, tokens), 0)
    hot0 = (names == first).astype(F32)
    hot1 = (names == second).astype(F32)
    before = (
        lax.broadcasted_iota(jnp.int32, (tokens, tokens), 0)
        < lax.broadcasted_iota(jnp.int32, (tokens, tokens), 1)
    ).astype(F32).astype(BF16)
    seen0 = dot(hot0.astype(BF16), before)
    seen1 = dot(hot1.astype(BF16), before) + jnp.sum(hot0, axis=1, keepdims=True)
    rank0 = jnp.sum(hot0 * seen0, axis=0, keepdims=True).astype(jnp.int32)
    rank1 = jnp.sum(hot1 * seen1, axis=0, keepdims=True).astype(jnp.int32)
    slots = (experts // 2) * CAP
    slot0 = ((first & 1) ^ half) * slots + (first >> 1) * CAP + rank0
    slot1 = ((second & 1) ^ half) * slots + (second >> 1) * CAP + rank1
    return slot0, slot1


def place_rows(ids_ref, half, experts, x, rows_ref):
    slot0, slot1 = slot_rows(ids_ref, half, experts)
    places = lax.broadcasted_iota(jnp.int32, (rows_ref.shape[0], x.shape[0]), 0)
    hot = ((places == slot0) | (places == slot1)).astype(F32).astype(BF16)
    rows_ref[...] = dot(hot, x)


def send_rows(seq_ref, ids_ref, x, perm_ref, out_ref, rows_ref):
    columns = out_ref.shape[0]
    piece = out_ref.shape[3]
    place_rows(ids_ref, seq_ref[0] // 4, 2 * columns, x, rows_ref)
    perm = perm_ref[...]
    for rel in range(2):
        for chunk in range(columns // GROUP):
            block = to_wire(rows_ref, rel * columns * CAP, perm, chunk, piece)
            out_ref[chunk * GROUP : (chunk + 1) * GROUP, rel] = block.reshape(GROUP, CELL, piece)


def grad_kernel(
    seq_ref, ids_ref, x_ref, perm_ref, k_ref, v_ref, out_ref, pair_ref, rows_ref, sems
):
    copies = [
        pltpu.make_async_copy(src, pair_ref.at[i], sems.at[i])
        for i, src in enumerate((k_ref, v_ref))
    ]
    for copy in copies:
        copy.start()
    send_rows(seq_ref, ids_ref, x_ref[...], perm_ref, out_ref, rows_ref)
    for copy in copies:
        copy.wait()


def tile_places(seq_ref, offs_ref, tile, tiles, total):
    places = []
    valid = []
    for m in range(NBR):
        off = offs_ref[tile, m]
        places.append(pl.multiple_of((tile + 2 + off) * TILE, TILE))
        where = seq_ref[0] * tiles + tile + off
        valid.append((where >= 0) & (where < total))
    return places, valid


def halo_copies(dst_ref, left_ref, own_ref, right_ref, which, sems, first):
    count = own_ref.shape[0]
    return [
        pltpu.make_async_copy(src, dst_ref.at[i * count : (i + 1) * count], sems.at[first + i])
        for i, src in enumerate((left_ref.at[which], own_ref, right_ref.at[which]))
    ]


def forward_kernel(
    seq_ref, offs_ref, ids_ref, q_ref, left_ref, k_ref, v_ref, right_ref, gain_ref, perm_ref,
    wts_ref, unit_ref, inv_ref, sent_ref, kx_ref, vx_ref, out_ref, rows_ref, sems, total_tiles,
):
    copies = halo_copies(kx_ref, left_ref, k_ref, right_ref, 0, sems, 0)
    copies += halo_copies(vx_ref, left_ref, v_ref, right_ref, 1, sems, NBR)
    for copy in copies:
        copy.start()
    count, width = q_ref.shape
    heads = width // HEAD_DIM
    tiles = count // TILE
    scale = HEAD_DIM ** (-0.5)
    lane = lax.broadcasted_iota(jnp.int32, (TILE, NBR * TILE), 1) // TILE
    spots = []
    biases = []
    for t in range(tiles):
        places, valid = tile_places(seq_ref, offs_ref, t, tiles, total_tiles)
        bias = jnp.zeros((TILE, NBR * TILE), F32)
        for m in range(NBR):
            lost = jnp.where(valid[m], 0.0, -jnp.inf).astype(F32)
            bias = jnp.where(lane == m, lost, bias)
        spots.append(places)
        biases.append(bias)

    for copy in copies:
        copy.wait()

    def one_head(h):
        lanes = pl.ds(pl.multiple_of(h * HEAD_DIM, HEAD_DIM), HEAD_DIM)
        for t in range(tiles):
            rows = slice(t * TILE, (t + 1) * TILE)
            k3 = jnp.concatenate([kx_ref[pl.ds(p, TILE), lanes] for p in spots[t]], axis=0)
            v3 = jnp.concatenate([vx_ref[pl.ds(p, TILE), lanes] for p in spots[t]], axis=0)
            scores = dot_nt(q_ref[rows, lanes], k3) * scale + biases[t]
            raised = jnp.exp(scores - jnp.max(scores, axis=-1, keepdims=True))
            weights = raised / jnp.sum(raised, axis=-1, keepdims=True)
            wts_ref[t * heads + h] = weights
            out_ref[rows, lanes] = dot(weights.astype(BF16), v3)

    def body(step, carry):
        for u in range(4):
            one_head(step * 4 + u)
        return carry

    lax.fori_loop(0, heads // 4, body, 0)
    out = out_ref[...]
    inv = lax.rsqrt(jnp.mean(out * out, axis=-1, keepdims=True) + EPSILON)
    unit = out * inv
    unit_ref[...] = unit
    inv_ref[...] = jnp.broadcast_to(inv, inv_ref.shape)
    normed = (unit * gain_ref[...]).astype(BF16)
    send_rows(seq_ref, ids_ref, normed, perm_ref, sent_ref, rows_ref)


def hidden_kernel(
    g0_ref, g1_ref, g2_ref, g3_ref, perm_t_ref, down0_ref, down1_ref, o0_ref, o1_ref, o2_ref,
    rows_ref, w_ref, sems,
):
    copies = [
        pltpu.make_async_copy(src, w_ref.at[i], sems.at[i])
        for i, src in enumerate((down0_ref, down1_ref))
    ]
    for copy in copies:
        copy.start()
    piece = g0_ref.shape[1]
    chunks = g0_ref.shape[0] // CHUNK
    slots = chunks * ROWS
    perm_t = perm_t_ref[...]
    for b, block in enumerate((g0_ref, g1_ref, g2_ref, g3_ref)):
        from_wire(block, rows_ref, b * slots, perm_t, chunks, piece)
    part = down0_ref.shape[0]
    for i, copy in enumerate(copies):
        copy.wait()
        cols = slice(i * part, (i + 1) * part)
        both = dot_nt(rows_ref[...], w_ref[i])
        o0_ref[:, cols] = both[:slots]
        o1_ref[:, cols] = both[slots : 3 * slots]
        o2_ref[:, cols] = both[3 * slots :]


def expert_kernel(*refs, blocks):
    ins = refs[:blocks]
    hg_ref, perm_ref, perm_t_ref = refs[blocks : blocks + 3]
    weights = refs[blocks + 3 : blocks + 7]
    outs = refs[blocks + 7 : 2 * blocks + 7]
    rows_ref, w_ref, act_ref, total_ref, sems = refs[2 * blocks + 7 :]
    copies = [pltpu.make_async_copy(src, w_ref.at[i], sems.at[i]) for i, src in enumerate(weights)]
    for copy in copies:
        copy.start()
    piece = ins[0].shape[1]
    chunks = ins[0].shape[0] // CHUNK
    perm_t = perm_t_ref[...]
    for b, block in enumerate(ins):
        from_wire(block, rows_ref, b * chunks * ROWS, perm_t, chunks, piece)
    part = w_ref.shape[2]
    for i in range(2):
        copies[2 * i].wait()
        gate_proj = dot(rows_ref[...], w_ref[2 * i])
        copies[2 * i + 1].wait()
        up_proj = dot(rows_ref[...], w_ref[2 * i + 1])
        hidden = hg_ref[:, i * part : (i + 1) * part]
        sig = jax.nn.sigmoid(gate_proj)
        act_ref[2 * i + 1] = (hidden * gate_proj * sig).astype(BF16)
        act_ref[2 * i] = (hidden * up_proj * sig * (1.0 + gate_proj * (1.0 - sig))).astype(BF16)
    width = total_ref.shape[1]
    for n in range(width // 512):
        cols = slice(n * 512, (n + 1) * 512)
        total = dot_nt(act_ref[0], w_ref[0, cols, :])
        for i in range(1, 4):
            total = total + dot_nt(act_ref[i], w_ref[i, cols, :])
        total_ref[:, cols] = total
    perm = perm_ref[...]
    for b, dst in enumerate(outs):
        for chunk in range(chunks):
            block = to_wire(total_ref, b * chunks * ROWS, perm, chunk, piece)
            dst[chunk * CHUNK : (chunk + 1) * CHUNK, :] = block


def value_kernel(
    seq_ref, offs_ref, ids_ref, gates_ref, home_ref, grad_ref, unit_ref, inv_ref, wts_hbm,
    gain_ref, perm_t_ref, own_ref, left_ref, right_ref, ag_ref, wts_ref, rows_ref, acc_ref, sems,
    total_tiles,
):
    wts_copy = pltpu.make_async_copy(wts_hbm, wts_ref, sems.at[0])
    wts_copy.start()
    count, width = grad_ref.shape
    heads = width // HEAD_DIM
    tiles = count // TILE
    acc_ref[...] = jnp.zeros_like(acc_ref)
    columns, _, _, piece = home_ref.shape
    chunks = columns // GROUP
    perm_t = perm_t_ref[...]
    for rel in range(2):
        blocks = [
            home_ref[c * GROUP : (c + 1) * GROUP, rel].reshape(CHUNK, piece) for c in range(chunks)
        ]
        from_wire(blocks, rows_ref, rel * chunks * ROWS, perm_t, chunks, piece)
    slot0, slot1 = slot_rows(ids_ref, seq_ref[0] // 4, 2 * columns)
    places = lax.broadcasted_iota(jnp.int32, (rows_ref.shape[0], count), 0)
    mix = jnp.where(places == slot0, gates_ref[0:1, :], 0.0)
    mix = jnp.where(places == slot1, gates_ref[1:2, :], mix)
    high = mix.astype(BF16)
    low = (mix - high.astype(F32)).astype(BF16)
    normed_grad = dot_tn(high, rows_ref[...]) + dot_tn(low, rows_ref[...])
    scaled = normed_grad * gain_ref[...]
    unit = unit_ref[...]
    inner = jnp.mean(scaled * unit, axis=-1, keepdims=True)
    attn_grad = grad_ref[...].astype(F32) + inv_ref[:, 0:1] * (scaled - unit * inner)
    ag_ref[...] = attn_grad.astype(BF16)
    spots = [tile_places(seq_ref, offs_ref, t, tiles, total_tiles)[0] for t in range(tiles)]
    wts_copy.wait()

    def one_head(h):
        lanes = pl.ds(pl.multiple_of(h * HEAD_DIM, HEAD_DIM), HEAD_DIM)
        for t in range(tiles):
            rows = slice(t * TILE, (t + 1) * TILE)
            part = dot_tn(wts_ref[t * heads + h].astype(BF16), ag_ref[rows, lanes])
            for m in range(NBR):
                acc_ref[pl.ds(spots[t][m], TILE), lanes] += part[m * TILE : (m + 1) * TILE]

    def body(step, carry):
        for u in range(4):
            one_head(step * 4 + u)
        return carry

    lax.fori_loop(0, heads // 4, body, 0)
    own_ref[...] = acc_ref[count : 2 * count, :]
    left_ref[...] = acc_ref[0:count, :].astype(BF16)
    right_ref[...] = acc_ref[2 * count : 3 * count, :].astype(BF16)


def key_kernel(
    seq_ref, offs_ref, ag_ref, q_ref, vl_ref, v_ref, vr_ref, wts_ref, own_ref, left_ref, right_ref,
    vx_ref, acc_ref, sems, total_tiles,
):
    copies = halo_copies(vx_ref, vl_ref, v_ref, vr_ref, 1, sems, 0)
    for copy in copies:
        copy.start()
    count, width = q_ref.shape
    heads = width // HEAD_DIM
    tiles = count // TILE
    scale = HEAD_DIM ** (-0.5)
    acc_ref[...] = jnp.zeros_like(acc_ref)
    spots = [tile_places(seq_ref, offs_ref, t, tiles, total_tiles)[0] for t in range(tiles)]
    for copy in copies:
        copy.wait()

    def one_head(h):
        lanes = pl.ds(pl.multiple_of(h * HEAD_DIM, HEAD_DIM), HEAD_DIM)
        for t in range(tiles):
            rows = slice(t * TILE, (t + 1) * TILE)
            v3 = jnp.concatenate([vx_ref[pl.ds(p, TILE), lanes] for p in spots[t]], axis=0)
            weights = wts_ref[t * heads + h]
            prob_grad = dot_nt(ag_ref[rows, lanes], v3)
            sums = jnp.sum(weights * prob_grad, axis=-1, keepdims=True)
            score_grad = (weights * (prob_grad - sums)).astype(BF16)
            part = dot_tn(score_grad, q_ref[rows, lanes]) * scale
            for m in range(NBR):
                acc_ref[pl.ds(spots[t][m], TILE), lanes] += part[m * TILE : (m + 1) * TILE]

    def body(step, carry):
        for u in range(4):
            one_head(step * 4 + u)
        return carry

    lax.fori_loop(0, heads // 4, body, 0)
    own_ref[...] = acc_ref[count : 2 * count, :]
    left_ref[...] = acc_ref[0:count, :].astype(BF16)
    right_ref[...] = acc_ref[2 * count : 3 * count, :].astype(BF16)


def call(body, outs, kinds, scratch, name, flops, out_kinds=None):
    spaces = {"s": pltpu.SMEM, "v": pltpu.VMEM, "a": pl.ANY}
    return pl.pallas_call(
        body,
        out_shape=outs,
        in_specs=[pl.BlockSpec(memory_space=spaces[kind]) for kind in kinds],
        out_specs=[pl.BlockSpec(memory_space=spaces[kind]) for kind in out_kinds or "v" * len(outs)],
        scratch_shapes=scratch,
        compiler_params=pltpu.CompilerParams(vmem_limit_bytes=56 * 1024 * 1024),
        cost_estimate=pl.CostEstimate(flops=flops, transcendentals=0, bytes_accessed=1 << 20),
        name=name,
    )


def shape(dims, kind):
    return jax.ShapeDtypeStruct(dims, kind)


def on_device(
    queries, keys, values, out_grad, norm_gain, gate_values, expert_ids, tile_offsets, gate_weight,
    up_weight, down_weight,
):
    count, width = queries.shape[1:]
    heads = width // HEAD_DIM
    tiles = count // TILE
    seq_count = lax.axis_size("seq")
    columns = lax.axis_size("exp")
    total_tiles = tiles * seq_count
    piece = width // PIECES
    slots = columns * CAP
    seq = lax.axis_index("seq").astype(jnp.int32).reshape(1)
    ids_t = expert_ids[0].T
    gates_t = gate_values[0].T
    offsets = tile_offsets[0]
    gain = norm_gain.reshape(1, width)
    perm = jnp.asarray(shuffle_matrix(), BF16)
    perm_t = jnp.asarray(shuffle_matrix().T, BF16)
    q, k, v, grad = queries[0], keys[0], values[0], out_grad[0]
    gate, up, down = gate_weight[0, 0], up_weight[0, 0], down_weight[0, 0]
    wire = (columns, 2, CELL, piece)
    flat = (columns * CELL, piece)

    up_by = [(i, i + 1) for i in range(seq_count - 1)]
    down_by = [(i + 1, i) for i in range(seq_count - 1)]

    def swap(x, bits):
        return lax.ppermute(x, "seq", [(i, i ^ bits) for i in range(seq_count)])

    def exchange(x):
        return lax.all_to_all(x, "exp", split_axis=0, concat_axis=0, tiled=True)

    barrier = lax.optimization_barrier
    pair = (2, count, width)
    sent_grad, kv = call(
        grad_kernel,
        (shape(wire, BF16), shape(pair, BF16)),
        "svvvaa",
        [pltpu.VMEM((2 * slots, width), F32), pltpu.SemaphoreType.DMA((2,))],
        "place_grad", 4 * MICRO, "va",
    )(seq, ids_t, grad, perm, k, v)
    left, right = lax.ppermute(kv, "seq", up_by), lax.ppermute(kv, "seq", down_by)
    got_grad = exchange(sent_grad)
    gate_s, up_s, down_s = swap(gate, 1), swap(up, 1), swap(down, 1)

    wts, unit, inv, sent = call(
        lambda *refs: forward_kernel(*refs, total_tiles=total_tiles),
        (
            shape((tiles * heads, TILE, NBR * TILE), F32),
            shape((count, width), F32),
            shape((count, HEAD_DIM), F32),
            shape(wire, BF16),
        ),
        "ssvvaaaavv",
        [
            pltpu.VMEM((3 * count, width), BF16),
            pltpu.VMEM((3 * count, width), BF16),
            pltpu.VMEM((count, width), F32),
            pltpu.VMEM((2 * slots, width), F32),
            pltpu.SemaphoreType.DMA((2 * NBR,)),
        ],
        "attention", ATTN * MICRO,
    )(seq, offsets, ids_t, q, left, k, v, right, gain, perm)

    sent, got_grad, gate_s, up_s, down_s = barrier((sent, got_grad, gate_s, up_s, down_s))
    got = exchange(sent)
    g0, grad_oth = got_grad[:, 0].reshape(flat), got_grad[:, 1].reshape(flat)
    g1, g2, g3 = swap(grad_oth, 6), swap(g0, 2), swap(grad_oth, 4)
    n0, oth = got[:, 0].reshape(flat), got[:, 1].reshape(flat)
    n1, n2 = swap(oth, 6), swap(n0, 2)

    n0, g0, g1, g2, g3 = barrier((n0, g0, g1, g2, g3))
    part = down.shape[0]
    hidden = call(
        hidden_kernel,
        tuple(shape((m * slots, 2 * part), F32) for m in (1, 2, 1)),
        "vvvvvaa",
        [
            pltpu.VMEM((4 * slots, width), BF16),
            pltpu.VMEM((2, part, width), BF16),
            pltpu.SemaphoreType.DMA((2,)),
        ],
        "hidden", 8 * MICRO,
    )(g0, g1, g2, g3, perm_t, down, down_s)

    def expert(ins, hg, micros):
        blocks = len(ins)
        return call(
            lambda *refs: expert_kernel(*refs, blocks=blocks),
            (shape(flat, BF16),) * blocks,
            "v" * (blocks + 3) + "aaaa",
            [
                pltpu.VMEM((blocks * slots, width), BF16),
                pltpu.VMEM((4, width, part), BF16),
                pltpu.VMEM((4, blocks * slots, part), BF16),
                pltpu.VMEM((blocks * slots, width), F32),
                pltpu.SemaphoreType.DMA((4,)),
            ],
            "expert", micros * MICRO,
        )(*ins, hg, perm, perm_t, gate, up, gate_s, up_s)

    n1, n2, oth = barrier((n1, n2, oth))
    n3 = swap(oth, 4)
    (p0,) = expert((n0,), hidden[0], 7)
    p0, n1, n2 = barrier((p0, n1, n2))
    p1, p2 = expert((n1, n2), hidden[1], 11)
    (p3,) = expert((n3,), hidden[2], 7)
    h1, h2 = swap(p1, 6), swap(p2, 2)
    h3 = swap(p3, 4)
    own = (p0.astype(F32) + h2.astype(F32)).astype(BF16).reshape(columns, 1, CELL, piece)
    oth = (h1.astype(F32) + h3.astype(F32)).astype(BF16).reshape(columns, 1, CELL, piece)
    home = exchange(jnp.concatenate([own, oth], axis=1))

    rows = shape((count, width), F32)
    half = shape((count, width), BF16)
    v_own, v_left, v_right, attn_grad = call(
        lambda *refs: value_kernel(*refs, total_tiles=total_tiles),
        (rows, half, half, half),
        "ssvvvvvvavv",
        [
            pltpu.VMEM(wts.shape, F32),
            pltpu.VMEM((2 * slots, width), BF16),
            pltpu.VMEM((3 * count, width), F32),
            pltpu.SemaphoreType.DMA((1,)),
        ],
        "value_grad", 7 * MICRO,
    )(seq, offsets, ids_t, gates_t, home, grad, unit, inv, wts, gain, perm_t)

    def gather(left_part, right_part):
        from_right = lax.ppermute(left_part, "seq", down_by)
        from_left = lax.ppermute(right_part, "seq", up_by)
        return from_right, from_left

    def finish(own_part, parts):
        return (own_part + parts[0].astype(F32) + parts[1].astype(F32)).astype(BF16)[None]

    v_parts = gather(v_left, v_right)
    k_own, k_left, k_right = call(
        lambda *refs: key_kernel(*refs, total_tiles=total_tiles),
        (rows, half, half),
        "ssvvaaav",
        [
            pltpu.VMEM((3 * count, width), BF16),
            pltpu.VMEM((3 * count, width), F32),
            pltpu.SemaphoreType.DMA((NBR,)),
        ],
        "key_grad", 9 * MICRO,
    )(seq, offsets, attn_grad, q, left, v, right, wts)
    k_parts = gather(k_left, k_right)
    return (finish(k_own, k_parts), finish(v_own, v_parts))


def solution(mesh):
    rows = P("exp", "seq", None)
    weights = P("exp", "seq", None, None)
    return jax.shard_map(
        on_device,
        mesh=mesh,
        in_specs=(rows, rows, rows, rows, P(), rows, rows, rows, weights, weights, weights),
        out_specs=(rows, rows),
        check_vma=False,
    )
```

```python
import jax
import jax.numpy as jnp
import numpy as np
from jax import lax
from jax.experimental import pallas as pl
from jax.experimental.pallas import tpu as pltpu
from jax.sharding import PartitionSpec as P

HEAD_DIM = 128
TILE = 64
NBR = 3
CAP = 5
PIECES = 8
GROUP = 8
EPSILON = 1e-06
ATTN = 16
UNROLL = 4
MICRO = 1 << 30
F32 = jnp.float32
BF16 = jnp.bfloat16

CELL = PIECES * CAP
CHUNK = GROUP * CELL
ROWS = GROUP * CAP


def shuffle_matrix():
    out = np.zeros((CHUNK, CHUNK), np.float32)
    for d in range(GROUP):
        for q in range(PIECES):
            for r in range(CAP):
                out[d * CELL + q * CAP + r, q * ROWS + d * CAP + r] = 1.0
    return out


def dot(a, b):
    return jnp.dot(a, b, preferred_element_type=F32)


def dot_nt(a, b):
    return lax.dot_general(a, b, (((1,), (1,)), ((), ())), preferred_element_type=F32)


def dot_tn(a, b):
    return lax.dot_general(a, b, (((0,), (0,)), ((), ())), preferred_element_type=F32)


def to_wire(rows_ref, base, perm, chunk, piece):
    start = base + chunk * ROWS
    stacked = jnp.concatenate(
        [rows_ref[start : start + ROWS, q * piece : (q + 1) * piece] for q in range(PIECES)], axis=0
    )
    return dot(perm, stacked.astype(BF16)).astype(BF16)


def from_wire(block_ref, rows_ref, base, perm_t, chunks, piece):
    if not isinstance(block_ref, list):
        block_ref = [block_ref[c * CHUNK : (c + 1) * CHUNK, :] for c in range(chunks)]
    for pair in range(chunks // 2):
        low = dot(perm_t, block_ref[2 * pair])
        high = dot(perm_t, block_ref[2 * pair + 1])
        start = base + 2 * pair * ROWS
        for q in range(PIECES):
            both = jnp.concatenate(
                [low[q * ROWS : (q + 1) * ROWS], high[q * ROWS : (q + 1) * ROWS]], axis=0
            )
            rows_ref[start : start + 2 * ROWS, q * piece : (q + 1) * piece] = both.astype(BF16)


def slot_rows(ids_ref, half, experts):
    tokens = ids_ref.shape[1]
    first = ids_ref[0:1, :]
    second = ids_ref[1:2, :]
    names = lax.broadcasted_iota(jnp.int32, (experts, tokens), 0)
    hot0 = (names == first).astype(F32)
    hot1 = (names == second).astype(F32)
    before = (
        lax.broadcasted_iota(jnp.int32, (tokens, tokens), 0)
        < lax.broadcasted_iota(jnp.int32, (tokens, tokens), 1)
    ).astype(F32).astype(BF16)
    seen0 = dot(hot0.astype(BF16), before)
    seen1 = dot(hot1.astype(BF16), before) + jnp.sum(hot0, axis=1, keepdims=True)
    rank0 = jnp.sum(hot0 * seen0, axis=0, keepdims=True).astype(jnp.int32)
    rank1 = jnp.sum(hot1 * seen1, axis=0, keepdims=True).astype(jnp.int32)
    slots = (experts // 2) * CAP
    slot0 = ((first & 1) ^ half) * slots + (first >> 1) * CAP + rank0
    slot1 = ((second & 1) ^ half) * slots + (second >> 1) * CAP + rank1
    return slot0, slot1


def place_rows(ids_ref, half, experts, x, rows_ref):
    slot0, slot1 = slot_rows(ids_ref, half, experts)
    places = lax.broadcasted_iota(jnp.int32, (rows_ref.shape[0], x.shape[0]), 0)
    hot = ((places == slot0) | (places == slot1)).astype(F32).astype(BF16)
    rows_ref[...] = dot(hot, x)


def send_rows(seq_ref, ids_ref, x, perm_ref, out_ref, rows_ref):
    columns = out_ref.shape[0]
    piece = out_ref.shape[3]
    place_rows(ids_ref, seq_ref[0] // 4, 2 * columns, x, rows_ref)
    perm = perm_ref[...]
    for rel in range(2):
        for chunk in range(columns // GROUP):
            block = to_wire(rows_ref, rel * columns * CAP, perm, chunk, piece)
            out_ref[chunk * GROUP : (chunk + 1) * GROUP, rel] = block.reshape(GROUP, CELL, piece)


def grad_kernel(seq_ref, ids_ref, x_ref, perm_ref, k_ref, v_ref, out_ref, pair_ref, rows_ref):
    pair_ref[0] = k_ref[...]
    pair_ref[1] = v_ref[...]
    send_rows(seq_ref, ids_ref, x_ref[...], perm_ref, out_ref, rows_ref)


def tile_places(seq_ref, offs_ref, tile, tiles, total):
    places = []
    valid = []
    for m in range(NBR):
        off = offs_ref[tile, m]
        places.append(pl.multiple_of((tile + 2 + off) * TILE, TILE))
        where = seq_ref[0] * tiles + tile + off
        valid.append((where >= 0) & (where < total))
    return places, valid


def head_spans(step, heads, tiles):
    spans = []
    for u in range(UNROLL):
        h = step * UNROLL + u
        lanes = pl.ds(pl.multiple_of(h * HEAD_DIM, HEAD_DIM), HEAD_DIM)
        spans += [(t, h, slice(t * TILE, (t + 1) * TILE), lanes) for t in range(tiles)]
    return spans


def window(ref, places, lanes):
    return jnp.concatenate([ref[pl.ds(p, TILE), lanes] for p in places], axis=0)


def halo_copies(dst_ref, left_ref, own_ref, right_ref, which, sems, first):
    count = own_ref.shape[0]
    return [
        pltpu.make_async_copy(src, dst_ref.at[i * count : (i + 1) * count], sems.at[first + i])
        for i, src in enumerate((left_ref.at[which], own_ref, right_ref.at[which]))
    ]


def forward_kernel(
    seq_ref, offs_ref, ids_ref, q_ref, left_ref, k_ref, v_ref, right_ref, gain_ref, perm_ref,
    wts_ref, unit_ref, inv_ref, sent_ref, kx_ref, vx_ref, out_ref, rows_ref, sems, total_tiles,
):
    copies = halo_copies(kx_ref, left_ref, k_ref, right_ref, 0, sems, 0)
    copies += halo_copies(vx_ref, left_ref, v_ref, right_ref, 1, sems, NBR)
    for copy in copies:
        copy.start()
    count, width = q_ref.shape
    heads = width // HEAD_DIM
    tiles = count // TILE
    scale = HEAD_DIM ** (-0.5)
    lane = lax.broadcasted_iota(jnp.int32, (TILE, NBR * TILE), 1) // TILE
    spots = []
    biases = []
    for t in range(tiles):
        places, valid = tile_places(seq_ref, offs_ref, t, tiles, total_tiles)
        bias = jnp.zeros((TILE, NBR * TILE), F32)
        for m in range(NBR):
            lost = jnp.where(valid[m], 0.0, -jnp.inf).astype(F32)
            bias = jnp.where(lane == m, lost, bias)
        spots.append(places)
        biases.append(bias)

    for copy in copies:
        copy.wait()

    def body(step, carry):
        spans = head_spans(step, heads, tiles)
        scores = [
            dot_nt(q_ref[rows, lanes], window(kx_ref, spots[t], lanes)) * scale + biases[t]
            for t, h, rows, lanes in spans
        ]
        tops = [jnp.max(x, axis=-1, keepdims=True) for x in scores]
        raised = [jnp.exp(x - top) for x, top in zip(scores, tops)]
        sums = [jnp.sum(x, axis=-1, keepdims=True) for x in raised]
        weights = [x / total for x, total in zip(raised, sums)]
        for x, (t, h, rows, lanes) in zip(weights, spans):
            wts_ref[t * heads + h] = x
            out_ref[rows, lanes] = dot(x.astype(BF16), window(vx_ref, spots[t], lanes))
        return carry

    lax.fori_loop(0, heads // UNROLL, body, 0)
    out = out_ref[...]
    inv = lax.rsqrt(jnp.mean(out * out, axis=-1, keepdims=True) + EPSILON)
    unit = out * inv
    unit_ref[...] = unit
    inv_ref[...] = jnp.broadcast_to(inv, inv_ref.shape)
    normed = (unit * gain_ref[...]).astype(BF16)
    send_rows(seq_ref, ids_ref, normed, perm_ref, sent_ref, rows_ref)


def hidden_kernel(*refs, blocks):
    ins = refs[:blocks]
    perm_t_ref, down0_ref, down1_ref, out_ref, rows_ref, w_ref, sems = refs[blocks:]
    copies = [
        pltpu.make_async_copy(src, w_ref.at[i], sems.at[i])
        for i, src in enumerate((down0_ref, down1_ref))
    ]
    for copy in copies:
        copy.start()
    piece = ins[0].shape[1]
    chunks = ins[0].shape[0] // CHUNK
    perm_t = perm_t_ref[...]
    for b, block in enumerate(ins):
        from_wire(block, rows_ref, b * chunks * ROWS, perm_t, chunks, piece)
    part = down0_ref.shape[0]
    for i, copy in enumerate(copies):
        copy.wait()
        out_ref[:, i * part : (i + 1) * part] = dot_nt(rows_ref[...], w_ref[i])


def expert_kernel(*refs, blocks):
    ins = refs[:blocks]
    hg_ref, perm_ref, perm_t_ref = refs[blocks : blocks + 3]
    weights = refs[blocks + 3 : blocks + 7]
    outs = refs[blocks + 7 : 2 * blocks + 7]
    rows_ref, w_ref, act_ref, total_ref, sems = refs[2 * blocks + 7 :]
    copies = [pltpu.make_async_copy(src, w_ref.at[i], sems.at[i]) for i, src in enumerate(weights)]
    for copy in copies:
        copy.start()
    piece = ins[0].shape[1]
    chunks = ins[0].shape[0] // CHUNK
    perm_t = perm_t_ref[...]
    for b, block in enumerate(ins):
        from_wire(block, rows_ref, b * chunks * ROWS, perm_t, chunks, piece)
    part = w_ref.shape[2]
    for i in range(2):
        copies[2 * i].wait()
        gate_proj = dot(rows_ref[...], w_ref[2 * i])
        copies[2 * i + 1].wait()
        up_proj = dot(rows_ref[...], w_ref[2 * i + 1])
        hidden = hg_ref[:, i * part : (i + 1) * part]
        sig = jax.nn.sigmoid(gate_proj)
        act_ref[2 * i + 1] = (hidden * gate_proj * sig).astype(BF16)
        act_ref[2 * i] = (hidden * up_proj * sig * (1.0 + gate_proj * (1.0 - sig))).astype(BF16)
    width = total_ref.shape[1]
    for n in range(width // 512):
        cols = slice(n * 512, (n + 1) * 512)
        total = dot_nt(act_ref[0], w_ref[0, cols, :])
        for i in range(1, 4):
            total = total + dot_nt(act_ref[i], w_ref[i, cols, :])
        total_ref[:, cols] = total
    perm = perm_ref[...]
    for b, dst in enumerate(outs):
        for chunk in range(chunks):
            block = to_wire(total_ref, b * chunks * ROWS, perm, chunk, piece)
            dst[chunk * CHUNK : (chunk + 1) * CHUNK, :] = block


def backward_kernel(
    seq_ref, offs_ref, ids_ref, gates_ref, home_ref, grad_ref, unit_ref, inv_ref, gain_ref,
    perm_t_ref, q_hbm, left_ref, v_ref, right_ref, wts_hbm, k_out_ref, v_out_ref, to_left_ref,
    to_right_ref, vx_ref, q_ref, wts_ref, rows_ref, ag_ref, ka_ref, va_ref, sems, total_tiles,
):
    copies = halo_copies(vx_ref, left_ref, v_ref, right_ref, 1, sems, 0)
    copies.append(pltpu.make_async_copy(q_hbm, q_ref, sems.at[NBR]))
    copies.append(pltpu.make_async_copy(wts_hbm, wts_ref, sems.at[NBR + 1]))
    for copy in copies:
        copy.start()
    count, width = q_ref.shape
    heads = width // HEAD_DIM
    tiles = count // TILE
    scale = HEAD_DIM ** (-0.5)
    ka_ref[...] = jnp.zeros_like(ka_ref)
    va_ref[...] = jnp.zeros_like(va_ref)
    columns, _, _, piece = home_ref.shape
    chunks = columns // GROUP
    perm_t = perm_t_ref[...]
    for rel in range(2):
        blocks = [
            home_ref[c * GROUP : (c + 1) * GROUP, rel].reshape(CHUNK, piece) for c in range(chunks)
        ]
        from_wire(blocks, rows_ref, rel * chunks * ROWS, perm_t, chunks, piece)
    slot0, slot1 = slot_rows(ids_ref, seq_ref[0] // 4, 2 * columns)
    places = lax.broadcasted_iota(jnp.int32, (rows_ref.shape[0], count), 0)
    mix = jnp.where(places == slot0, gates_ref[0:1, :], 0.0)
    mix = jnp.where(places == slot1, gates_ref[1:2, :], mix)
    high = mix.astype(BF16)
    low = (mix - high.astype(F32)).astype(BF16)
    normed_grad = dot_tn(high, rows_ref[...]) + dot_tn(low, rows_ref[...])
    scaled = normed_grad * gain_ref[...]
    unit = unit_ref[...]
    inner = jnp.mean(scaled * unit, axis=-1, keepdims=True)
    attn_grad = grad_ref[...].astype(F32) + inv_ref[:, 0:1] * (scaled - unit * inner)
    ag_ref[...] = attn_grad.astype(BF16)
    spots = [tile_places(seq_ref, offs_ref, t, tiles, total_tiles)[0] for t in range(tiles)]
    for copy in copies:
        copy.wait()

    def body(step, carry):
        spans = head_spans(step, heads, tiles)
        prob_grads = [
            dot_nt(ag_ref[rows, lanes], window(vx_ref, spots[t], lanes))
            for t, h, rows, lanes in spans
        ]
        values = [
            dot_tn(wts_ref[t * heads + h].astype(BF16), ag_ref[rows, lanes])
            for t, h, rows, lanes in spans
        ]
        sums = [
            jnp.sum(wts_ref[t * heads + h] * x, axis=-1, keepdims=True)
            for x, (t, h, rows, lanes) in zip(prob_grads, spans)
        ]
        score_grads = [
            (wts_ref[t * heads + h] * (x - total)).astype(BF16)
            for x, total, (t, h, rows, lanes) in zip(prob_grads, sums, spans)
        ]
        keys = [
            dot_tn(x, q_ref[rows, lanes]) * scale
            for x, (t, h, rows, lanes) in zip(score_grads, spans)
        ]
        for acc_ref, parts in ((va_ref, values), (ka_ref, keys)):
            for x, (t, h, rows, lanes) in zip(parts, spans):
                for m in range(NBR):
                    acc_ref[pl.ds(spots[t][m], TILE), lanes] += x[m * TILE : (m + 1) * TILE]
        return carry

    lax.fori_loop(0, heads // UNROLL, body, 0)
    k_out_ref[...] = ka_ref[count : 2 * count, :]
    v_out_ref[...] = va_ref[count : 2 * count, :]
    to_left_ref[0] = ka_ref[0:count, :].astype(BF16)
    to_left_ref[1] = va_ref[0:count, :].astype(BF16)
    to_right_ref[0] = ka_ref[2 * count : 3 * count, :].astype(BF16)
    to_right_ref[1] = va_ref[2 * count : 3 * count, :].astype(BF16)


def call(body, outs, kinds, scratch, name, flops, out_kinds=None):
    spaces = {"s": pltpu.SMEM, "v": pltpu.VMEM, "a": pl.ANY}
    return pl.pallas_call(
        body,
        out_shape=outs,
        in_specs=[pl.BlockSpec(memory_space=spaces[kind]) for kind in kinds],
        out_specs=[pl.BlockSpec(memory_space=spaces[kind]) for kind in out_kinds or "v" * len(outs)],
        scratch_shapes=scratch,
        compiler_params=pltpu.CompilerParams(vmem_limit_bytes=56 * 1024 * 1024),
        cost_estimate=pl.CostEstimate(flops=flops, transcendentals=0, bytes_accessed=1 << 20),
        name=name,
    )


def shape(dims, kind):
    return jax.ShapeDtypeStruct(dims, kind)


def on_device(
    queries, keys, values, out_grad, norm_gain, gate_values, expert_ids, tile_offsets, gate_weight,
    up_weight, down_weight,
):
    count, width = queries.shape[1:]
    heads = width // HEAD_DIM
    tiles = count // TILE
    seq_count = lax.axis_size("seq")
    columns = lax.axis_size("exp")
    total_tiles = tiles * seq_count
    piece = width // PIECES
    slots = columns * CAP
    seq = lax.axis_index("seq").astype(jnp.int32).reshape(1)
    ids_t = expert_ids[0].T
    gates_t = gate_values[0].T
    offsets = tile_offsets[0]
    gain = norm_gain.reshape(1, width)
    perm = jnp.asarray(shuffle_matrix(), BF16)
    perm_t = jnp.asarray(shuffle_matrix().T, BF16)
    q, k, v, grad = queries[0], keys[0], values[0], out_grad[0]
    gate, up, down = gate_weight[0, 0], up_weight[0, 0], down_weight[0, 0]
    wire = (columns, 2, CELL, piece)
    flat = (columns * CELL, piece)

    up_by = [(i, i + 1) for i in range(seq_count - 1)]
    down_by = [(i + 1, i) for i in range(seq_count - 1)]

    def swap(x, bits):
        return lax.ppermute(x, "seq", [(i, i ^ bits) for i in range(seq_count)])

    def exchange(x):
        return lax.all_to_all(x, "exp", split_axis=0, concat_axis=0, tiled=True)

    barrier = lax.optimization_barrier
    pair = (2, count, width)
    sent_grad, kv = call(
        grad_kernel,
        (shape(wire, BF16), shape(pair, BF16)),
        "svvvvv",
        [pltpu.VMEM((2 * slots, width), F32)],
        "place_grad", 4 * MICRO,
    )(seq, ids_t, grad, perm, k, v)
    left, right = lax.ppermute(kv, "seq", up_by), lax.ppermute(kv, "seq", down_by)
    got_grad = exchange(sent_grad)
    gate_s, up_s, down_s = swap(gate, 1), swap(up, 1), swap(down, 1)

    wts, unit, inv, sent = call(
        lambda *refs: forward_kernel(*refs, total_tiles=total_tiles),
        (
            shape((tiles * heads, TILE, NBR * TILE), F32),
            shape((count, width), F32),
            shape((count, HEAD_DIM), F32),
            shape(wire, BF16),
        ),
        "ssvvaaaavv",
        [
            pltpu.VMEM((3 * count, width), BF16),
            pltpu.VMEM((3 * count, width), BF16),
            pltpu.VMEM((count, width), F32),
            pltpu.VMEM((2 * slots, width), F32),
            pltpu.SemaphoreType.DMA((2 * NBR,)),
        ],
        "attention", ATTN * MICRO,
    )(seq, offsets, ids_t, q, left, k, v, right, gain, perm)

    sent, got_grad, gate_s, up_s, down_s = barrier((sent, got_grad, gate_s, up_s, down_s))
    got = exchange(sent)
    g0, grad_oth = got_grad[:, 0].reshape(flat), got_grad[:, 1].reshape(flat)
    g1, g2 = swap(grad_oth, 6), swap(g0, 2)
    g1, g2, grad_oth = barrier((g1, g2, grad_oth))
    g3 = swap(grad_oth, 4)
    n0, oth = got[:, 0].reshape(flat), got[:, 1].reshape(flat)
    n1, n2 = swap(oth, 6), swap(n0, 2)
    n1, n2, oth = barrier((n1, n2, oth))
    n3 = swap(oth, 4)

    part = down.shape[0]

    def hidden(ins, micros):
        blocks = len(ins)
        (out,) = call(
            lambda *refs: hidden_kernel(*refs, blocks=blocks),
            (shape((blocks * slots, 2 * part), F32),),
            "v" * (blocks + 1) + "aa",
            [
                pltpu.VMEM((blocks * slots, width), BF16),
                pltpu.VMEM((2, part, width), BF16),
                pltpu.SemaphoreType.DMA((2,)),
            ],
            "hidden", micros * MICRO,
        )(*ins, perm_t, down, down_s)
        return out

    def expert(ins, hg, micros):
        blocks = len(ins)
        return call(
            lambda *refs: expert_kernel(*refs, blocks=blocks),
            (shape(flat, BF16),) * blocks,
            "v" * (blocks + 3) + "aaaa",
            [
                pltpu.VMEM((blocks * slots, width), BF16),
                pltpu.VMEM((4, width, part), BF16),
                pltpu.VMEM((4, blocks * slots, part), BF16),
                pltpu.VMEM((blocks * slots, width), F32),
                pltpu.SemaphoreType.DMA((4,)),
            ],
            "expert", micros * MICRO,
        )(*ins, hg, perm, perm_t, gate, up, gate_s, up_s)

    hidden_own = hidden((g0,), 4)
    hidden_near = hidden((g1, g2), 5)
    (p0,) = expert((n0,), hidden_own, 9)
    p0, g3 = barrier((p0, g3))
    hidden_far = hidden((g3,), 4)
    hidden_far, n1, n2 = barrier((hidden_far, n1, n2))
    p1, p2 = expert((n1, n2), hidden_near, 11)
    (p3,) = expert((n3,), hidden_far, 9)
    h1, h2 = swap(p1, 6), swap(p2, 2)
    h3 = swap(p3, 4)
    own = (p0.astype(F32) + h2.astype(F32)).astype(BF16).reshape(columns, 1, CELL, piece)
    oth = (h1.astype(F32) + h3.astype(F32)).astype(BF16).reshape(columns, 1, CELL, piece)
    home = exchange(jnp.concatenate([own, oth], axis=1))

    k_own, v_own, to_left, to_right = call(
        lambda *refs: backward_kernel(*refs, total_tiles=total_tiles),
        (shape((count, width), F32), shape((count, width), F32), shape(pair, BF16), shape(pair, BF16)),
        "ssvvvvvvvvaaaaa",
        [
            pltpu.VMEM((3 * count, width), BF16),
            pltpu.VMEM((count, width), BF16),
            pltpu.VMEM(wts.shape, F32),
            pltpu.VMEM((2 * slots, width), BF16),
            pltpu.VMEM((count, width), BF16),
            pltpu.VMEM((3 * count, width), F32),
            pltpu.VMEM((3 * count, width), F32),
            pltpu.SemaphoreType.DMA((NBR + 2,)),
        ],
        "attention_grad", 12 * MICRO,
    )(seq, offsets, ids_t, gates_t, home, grad, unit, inv, gain, perm_t, q, left, v, right, wts)
    from_right = lax.ppermute(to_left, "seq", down_by)
    from_left = lax.ppermute(to_right, "seq", up_by)

    def finish(own_part, i):
        return (own_part + from_right[i].astype(F32) + from_left[i].astype(F32)).astype(BF16)[None]

    return (finish(k_own, 0), finish(v_own, 1))


def solution(mesh):
    rows = P("exp", "seq", None)
    weights = P("exp", "seq", None, None)
    return jax.shard_map(
        on_device,
        mesh=mesh,
        in_specs=(rows, rows, rows, rows, P(), rows, rows, rows, weights, weights, weights),
        out_specs=(rows, rows),
        check_vma=False,
    )
```

```python
import jax
import jax.numpy as jnp
import numpy as np
from jax import lax
from jax.experimental import pallas as pl
from jax.experimental.pallas import tpu as pltpu
from jax.sharding import PartitionSpec as P

HEAD_DIM = 128
TILE = 64
NBR = 3
CAP = 5
PIECES = 8
GROUP = 8
EPSILON = 1e-06
ATTN = 8
UNROLL = 4
MICRO = 1 << 30
F32 = jnp.float32
BF16 = jnp.bfloat16

CELL = PIECES * CAP
CHUNK = GROUP * CELL
ROWS = GROUP * CAP


def shuffle_matrix():
    out = np.zeros((CHUNK, CHUNK), np.float32)
    for d in range(GROUP):
        for q in range(PIECES):
            for r in range(CAP):
                out[d * CELL + q * CAP + r, q * ROWS + d * CAP + r] = 1.0
    return out


def dot(a, b):
    return jnp.dot(a, b, preferred_element_type=F32)


def dot_nt(a, b):
    return lax.dot_general(a, b, (((1,), (1,)), ((), ())), preferred_element_type=F32)


def dot_tn(a, b):
    return lax.dot_general(a, b, (((0,), (0,)), ((), ())), preferred_element_type=F32)


def to_wire(rows_ref, base, perm, chunk, piece):
    start = base + chunk * ROWS
    stacked = jnp.concatenate(
        [rows_ref[start : start + ROWS, q * piece : (q + 1) * piece] for q in range(PIECES)], axis=0
    )
    return dot(perm, stacked.astype(BF16)).astype(BF16)


def from_wire(block_ref, rows_ref, base, perm_t, chunks, piece):
    if not isinstance(block_ref, list):
        block_ref = [block_ref[c * CHUNK : (c + 1) * CHUNK, :] for c in range(chunks)]
    for pair in range(chunks // 2):
        low = dot(perm_t, block_ref[2 * pair])
        high = dot(perm_t, block_ref[2 * pair + 1])
        start = base + 2 * pair * ROWS
        for q in range(PIECES):
            both = jnp.concatenate(
                [low[q * ROWS : (q + 1) * ROWS], high[q * ROWS : (q + 1) * ROWS]], axis=0
            )
            rows_ref[start : start + 2 * ROWS, q * piece : (q + 1) * piece] = both.astype(BF16)


def slot_rows(ids_ref, half, experts):
    tokens = ids_ref.shape[1]
    first = ids_ref[0:1, :]
    second = ids_ref[1:2, :]
    names = lax.broadcasted_iota(jnp.int32, (experts, tokens), 0)
    hot0 = (names == first).astype(F32)
    hot1 = (names == second).astype(F32)
    before = (
        lax.broadcasted_iota(jnp.int32, (tokens, tokens), 0)
        < lax.broadcasted_iota(jnp.int32, (tokens, tokens), 1)
    ).astype(F32).astype(BF16)
    seen0 = dot(hot0.astype(BF16), before)
    seen1 = dot(hot1.astype(BF16), before) + jnp.sum(hot0, axis=1, keepdims=True)
    rank0 = jnp.sum(hot0 * seen0, axis=0, keepdims=True).astype(jnp.int32)
    rank1 = jnp.sum(hot1 * seen1, axis=0, keepdims=True).astype(jnp.int32)
    slots = (experts // 2) * CAP
    slot0 = ((first & 1) ^ half) * slots + (first >> 1) * CAP + rank0
    slot1 = ((second & 1) ^ half) * slots + (second >> 1) * CAP + rank1
    return slot0, slot1


def place_rows(ids_ref, half, experts, x, rows_ref):
    slot0, slot1 = slot_rows(ids_ref, half, experts)
    places = lax.broadcasted_iota(jnp.int32, (rows_ref.shape[0], x.shape[0]), 0)
    hot = ((places == slot0) | (places == slot1)).astype(F32).astype(BF16)
    rows_ref[...] = dot(hot, x)


def send_rows(seq_ref, ids_ref, x, perm_ref, out_ref, rows_ref):
    columns = out_ref.shape[0]
    piece = out_ref.shape[3]
    place_rows(ids_ref, seq_ref[0] // 4, 2 * columns, x, rows_ref)
    perm = perm_ref[...]
    for rel in range(2):
        for chunk in range(columns // GROUP):
            block = to_wire(rows_ref, rel * columns * CAP, perm, chunk, piece)
            out_ref[chunk * GROUP : (chunk + 1) * GROUP, rel] = block.reshape(GROUP, CELL, piece)


def grad_kernel(seq_ref, ids_ref, x_ref, perm_ref, out_ref, rows_ref):
    send_rows(seq_ref, ids_ref, x_ref[...], perm_ref, out_ref, rows_ref)


def tile_places(seq_ref, offs_ref, tile, tiles, total):
    places = []
    valid = []
    for m in range(NBR):
        off = offs_ref[tile, m]
        places.append(pl.multiple_of((tile + 2 + off) * TILE, TILE))
        where = seq_ref[0] * tiles + tile + off
        valid.append((where >= 0) & (where < total))
    return places, valid


def head_spans(step, heads, tiles):
    spans = []
    for u in range(UNROLL):
        h = step * UNROLL + u
        lanes = pl.ds(pl.multiple_of(h * HEAD_DIM, HEAD_DIM), HEAD_DIM)
        spans += [(t, h, slice(t * TILE, (t + 1) * TILE), lanes) for t in range(tiles)]
    return spans


def window(ref, places, lanes):
    return jnp.concatenate([ref[pl.ds(p, TILE), lanes] for p in places], axis=0)


def fill_halo(dst_ref, left_ref, own_ref, right_ref):
    count = own_ref.shape[0]
    for i, src in enumerate((left_ref, own_ref, right_ref)):
        dst_ref[i * count : (i + 1) * count, :] = src[...]


def forward_kernel(
    seq_ref, offs_ref, ids_ref, q_ref, kl_ref, k_ref, kr_ref, vl_ref, v_ref, vr_ref, gain_ref,
    perm_ref, wts_ref, unit_ref, inv_ref, sent_ref, kx_ref, vx_ref, out_ref, rows_ref, total_tiles,
):
    fill_halo(kx_ref, kl_ref, k_ref, kr_ref)
    fill_halo(vx_ref, vl_ref, v_ref, vr_ref)
    count, width = q_ref.shape
    heads = width // HEAD_DIM
    tiles = count // TILE
    scale = HEAD_DIM ** (-0.5)
    lane = lax.broadcasted_iota(jnp.int32, (TILE, NBR * TILE), 1) // TILE
    spots = []
    biases = []
    for t in range(tiles):
        places, valid = tile_places(seq_ref, offs_ref, t, tiles, total_tiles)
        bias = jnp.zeros((TILE, NBR * TILE), F32)
        for m in range(NBR):
            lost = jnp.where(valid[m], 0.0, -jnp.inf).astype(F32)
            bias = jnp.where(lane == m, lost, bias)
        spots.append(places)
        biases.append(bias)

    def body(step, carry):
        spans = head_spans(step, heads, tiles)
        scores = [
            dot_nt(q_ref[rows, lanes], window(kx_ref, spots[t], lanes)) * scale + biases[t]
            for t, h, rows, lanes in spans
        ]
        tops = [jnp.max(x, axis=-1, keepdims=True) for x in scores]
        raised = [jnp.exp(x - top) for x, top in zip(scores, tops)]
        sums = [jnp.sum(x, axis=-1, keepdims=True) for x in raised]
        weights = [x / total for x, total in zip(raised, sums)]
        for x, (t, h, rows, lanes) in zip(weights, spans):
            wts_ref[t * heads + h] = x
            out_ref[rows, lanes] = dot(x.astype(BF16), window(vx_ref, spots[t], lanes))
        return carry

    lax.fori_loop(0, heads // UNROLL, body, 0)
    out = out_ref[...]
    inv = lax.rsqrt(jnp.mean(out * out, axis=-1, keepdims=True) + EPSILON)
    unit = out * inv
    unit_ref[...] = unit
    inv_ref[...] = jnp.broadcast_to(inv, inv_ref.shape)
    normed = (unit * gain_ref[...]).astype(BF16)
    send_rows(seq_ref, ids_ref, normed, perm_ref, sent_ref, rows_ref)


def hidden_kernel(*refs, blocks):
    ins = refs[:blocks]
    perm_t_ref, down0_ref, down1_ref, out_ref, rows_ref = refs[blocks:]
    piece = ins[0].shape[1]
    chunks = ins[0].shape[0] // CHUNK
    perm_t = perm_t_ref[...]
    for b, block in enumerate(ins):
        from_wire(block, rows_ref, b * chunks * ROWS, perm_t, chunks, piece)
    part = down0_ref.shape[0]
    for i, w_ref in enumerate((down0_ref, down1_ref)):
        out_ref[:, i * part : (i + 1) * part] = dot_nt(rows_ref[...], w_ref[...])


def expert_kernel(*refs, blocks):
    ins = refs[:blocks]
    hg_ref, perm_ref, perm_t_ref = refs[blocks : blocks + 3]
    weights = refs[blocks + 3 : blocks + 7]
    outs = refs[blocks + 7 : 2 * blocks + 7]
    rows_ref, act_ref, total_ref = refs[2 * blocks + 7 :]
    piece = ins[0].shape[1]
    chunks = ins[0].shape[0] // CHUNK
    perm_t = perm_t_ref[...]
    for b, block in enumerate(ins):
        from_wire(block, rows_ref, b * chunks * ROWS, perm_t, chunks, piece)
    width, part = weights[0].shape
    for i in range(2):
        gate_proj = dot(rows_ref[...], weights[2 * i][...])
        up_proj = dot(rows_ref[...], weights[2 * i + 1][...])
        hidden = hg_ref[:, i * part : (i + 1) * part]
        sig = jax.nn.sigmoid(gate_proj)
        act_ref[2 * i + 1] = (hidden * gate_proj * sig).astype(BF16)
        act_ref[2 * i] = (hidden * up_proj * sig * (1.0 + gate_proj * (1.0 - sig))).astype(BF16)
    for n in range(width // 512):
        cols = slice(n * 512, (n + 1) * 512)
        total = dot_nt(act_ref[0], weights[0][cols, :])
        for i in range(1, 4):
            total = total + dot_nt(act_ref[i], weights[i][cols, :])
        total_ref[:, cols] = total
    perm = perm_ref[...]
    for b, dst in enumerate(outs):
        for chunk in range(chunks):
            block = to_wire(total_ref, b * chunks * ROWS, perm, chunk, piece)
            dst[chunk * CHUNK : (chunk + 1) * CHUNK, :] = block


def backward_kernel(
    seq_ref, offs_ref, ids_ref, gates_ref, home_ref, grad_ref, unit_ref, inv_ref, gain_ref,
    perm_t_ref, q_ref, vl_ref, v_ref, vr_ref, wts_ref, k_out_ref, v_out_ref, to_left_ref,
    to_right_ref, vx_ref, rows_ref, ag_ref, ka_ref, va_ref, total_tiles,
):
    fill_halo(vx_ref, vl_ref, v_ref, vr_ref)
    count, width = q_ref.shape
    heads = width // HEAD_DIM
    tiles = count // TILE
    scale = HEAD_DIM ** (-0.5)
    ka_ref[...] = jnp.zeros_like(ka_ref)
    va_ref[...] = jnp.zeros_like(va_ref)
    columns, _, _, piece = home_ref.shape
    chunks = columns // GROUP
    perm_t = perm_t_ref[...]
    for rel in range(2):
        blocks = [
            home_ref[c * GROUP : (c + 1) * GROUP, rel].reshape(CHUNK, piece) for c in range(chunks)
        ]
        from_wire(blocks, rows_ref, rel * chunks * ROWS, perm_t, chunks, piece)
    slot0, slot1 = slot_rows(ids_ref, seq_ref[0] // 4, 2 * columns)
    places = lax.broadcasted_iota(jnp.int32, (rows_ref.shape[0], count), 0)
    mix = jnp.where(places == slot0, gates_ref[0:1, :], 0.0)
    mix = jnp.where(places == slot1, gates_ref[1:2, :], mix)
    high = mix.astype(BF16)
    low = (mix - high.astype(F32)).astype(BF16)
    normed_grad = dot_tn(high, rows_ref[...]) + dot_tn(low, rows_ref[...])
    scaled = normed_grad * gain_ref[...]
    unit = unit_ref[...]
    inner = jnp.mean(scaled * unit, axis=-1, keepdims=True)
    attn_grad = grad_ref[...].astype(F32) + inv_ref[:, 0:1] * (scaled - unit * inner)
    ag_ref[...] = attn_grad.astype(BF16)
    spots = [tile_places(seq_ref, offs_ref, t, tiles, total_tiles)[0] for t in range(tiles)]
    def body(step, carry):
        spans = head_spans(step, heads, tiles)
        prob_grads = [
            dot_nt(ag_ref[rows, lanes], window(vx_ref, spots[t], lanes))
            for t, h, rows, lanes in spans
        ]
        values = [
            dot_tn(wts_ref[t * heads + h].astype(BF16), ag_ref[rows, lanes])
            for t, h, rows, lanes in spans
        ]
        sums = [
            jnp.sum(wts_ref[t * heads + h] * x, axis=-1, keepdims=True)
            for x, (t, h, rows, lanes) in zip(prob_grads, spans)
        ]
        score_grads = [
            (wts_ref[t * heads + h] * (x - total)).astype(BF16)
            for x, total, (t, h, rows, lanes) in zip(prob_grads, sums, spans)
        ]
        keys = [
            dot_tn(x, q_ref[rows, lanes]) * scale
            for x, (t, h, rows, lanes) in zip(score_grads, spans)
        ]
        for acc_ref, parts in ((va_ref, values), (ka_ref, keys)):
            for x, (t, h, rows, lanes) in zip(parts, spans):
                for m in range(NBR):
                    acc_ref[pl.ds(spots[t][m], TILE), lanes] += x[m * TILE : (m + 1) * TILE]
        return carry

    lax.fori_loop(0, heads // UNROLL, body, 0)
    k_out_ref[...] = ka_ref[count : 2 * count, :]
    v_out_ref[...] = va_ref[count : 2 * count, :]
    to_left_ref[0] = ka_ref[0:count, :].astype(BF16)
    to_left_ref[1] = va_ref[0:count, :].astype(BF16)
    to_right_ref[0] = ka_ref[2 * count : 3 * count, :].astype(BF16)
    to_right_ref[1] = va_ref[2 * count : 3 * count, :].astype(BF16)


def call(body, outs, kinds, scratch, name, flops, megabytes):
    spaces = {"s": pltpu.SMEM, "v": pltpu.VMEM}
    return pl.pallas_call(
        body,
        out_shape=outs,
        in_specs=[pl.BlockSpec(memory_space=spaces[kind]) for kind in kinds],
        out_specs=[pl.BlockSpec(memory_space=pltpu.VMEM) for _ in outs],
        scratch_shapes=scratch,
        compiler_params=pltpu.CompilerParams(vmem_limit_bytes=megabytes << 20),
        cost_estimate=pl.CostEstimate(flops=flops, transcendentals=0, bytes_accessed=1 << 20),
        name=name,
    )


def shape(dims, kind):
    return jax.ShapeDtypeStruct(dims, kind)


def on_device(
    queries, keys, values, out_grad, norm_gain, gate_values, expert_ids, tile_offsets, gate_weight,
    up_weight, down_weight,
):
    count, width = queries.shape[1:]
    heads = width // HEAD_DIM
    tiles = count // TILE
    seq_count = lax.axis_size("seq")
    columns = lax.axis_size("exp")
    total_tiles = tiles * seq_count
    piece = width // PIECES
    slots = columns * CAP
    seq = lax.axis_index("seq").astype(jnp.int32).reshape(1)
    ids_t = expert_ids[0].T
    gates_t = gate_values[0].T
    offsets = tile_offsets[0]
    gain = norm_gain.reshape(1, width)
    perm = jnp.asarray(shuffle_matrix(), BF16)
    perm_t = jnp.asarray(shuffle_matrix().T, BF16)
    q, k, v, grad = queries[0], keys[0], values[0], out_grad[0]
    gate, up, down = gate_weight[0, 0], up_weight[0, 0], down_weight[0, 0]
    wire = (columns, 2, CELL, piece)
    flat = (columns * CELL, piece)

    up_by = [(i, i + 1) for i in range(seq_count - 1)]
    down_by = [(i + 1, i) for i in range(seq_count - 1)]

    def swap(x, bits):
        return lax.ppermute(x, "seq", [(i, i ^ bits) for i in range(seq_count)])

    def exchange(x):
        return lax.all_to_all(x, "exp", split_axis=0, concat_axis=0, tiled=True)

    barrier = lax.optimization_barrier
    pair = (2, count, width)
    kl, kr = lax.ppermute(k, "seq", up_by), lax.ppermute(k, "seq", down_by)
    vl, vr = lax.ppermute(v, "seq", up_by), lax.ppermute(v, "seq", down_by)
    (sent_grad,) = call(
        grad_kernel, (shape(wire, BF16),), "svvv", [pltpu.VMEM((2 * slots, width), F32)],
        "place_grad", 4 * MICRO, 12,
    )(seq, ids_t, grad, perm)
    got_grad = exchange(sent_grad)
    gate_s, up_s, down_s = swap(gate, 1), swap(up, 1), swap(down, 1)

    wts, unit, inv, sent = call(
        lambda *refs: forward_kernel(*refs, total_tiles=total_tiles),
        (
            shape((tiles * heads, TILE, NBR * TILE), F32),
            shape((count, width), F32),
            shape((count, HEAD_DIM), F32),
            shape(wire, BF16),
        ),
        "ssv" + "v" * 9,
        [
            pltpu.VMEM((3 * count, width), BF16),
            pltpu.VMEM((3 * count, width), BF16),
            pltpu.VMEM((count, width), F32),
            pltpu.VMEM((2 * slots, width), F32),
        ],
        "attention", ATTN * MICRO, 20,
    )(seq, offsets, ids_t, q, kl, k, kr, vl, v, vr, gain, perm)

    sent, got_grad, gate_s, up_s, down_s = barrier((sent, got_grad, gate_s, up_s, down_s))
    got = exchange(sent)
    g0, grad_oth = got_grad[:, 0].reshape(flat), got_grad[:, 1].reshape(flat)
    g1, g2 = swap(grad_oth, 6), swap(g0, 2)
    g1, g2, grad_oth = barrier((g1, g2, grad_oth))
    g3 = swap(grad_oth, 4)
    n0, oth = got[:, 0].reshape(flat), got[:, 1].reshape(flat)
    n1, n2 = swap(oth, 6), swap(n0, 2)
    n1, n2, oth = barrier((n1, n2, oth))
    n3 = swap(oth, 4)

    part = down.shape[0]

    def hidden(ins, micros):
        blocks = len(ins)
        (out,) = call(
            lambda *refs: hidden_kernel(*refs, blocks=blocks),
            (shape((blocks * slots, 2 * part), F32),),
            "v" * (blocks + 3),
            [pltpu.VMEM((blocks * slots, width), BF16)],
            "hidden", micros * MICRO, 14,
        )(*ins, perm_t, down, down_s)
        return out

    def expert(ins, hg, micros):
        blocks = len(ins)
        return call(
            lambda *refs: expert_kernel(*refs, blocks=blocks),
            (shape(flat, BF16),) * blocks,
            "v" * (blocks + 7),
            [
                pltpu.VMEM((blocks * slots, width), BF16),
                pltpu.VMEM((4, blocks * slots, part), BF16),
                pltpu.VMEM((blocks * slots, width), F32),
            ],
            "expert", micros * MICRO, 24,
        )(*ins, hg, perm, perm_t, gate, up, gate_s, up_s)

    hidden_own = hidden((g0,), 4)
    hidden_near = hidden((g1, g2), 5)
    (p0,) = expert((n0,), hidden_own, 9)
    p0, g3 = barrier((p0, g3))
    hidden_far = hidden((g3,), 4)
    hidden_far, n1, n2 = barrier((hidden_far, n1, n2))
    p1, p2 = expert((n1, n2), hidden_near, 11)
    (p3,) = expert((n3,), hidden_far, 9)
    h1, h2 = swap(p1, 6), swap(p2, 2)
    h3 = swap(p3, 4)
    own = (p0.astype(F32) + h2.astype(F32)).astype(BF16).reshape(columns, 1, CELL, piece)
    oth = (h1.astype(F32) + h3.astype(F32)).astype(BF16).reshape(columns, 1, CELL, piece)
    home = exchange(jnp.concatenate([own, oth], axis=1))

    k_own, v_own, to_left, to_right = call(
        lambda *refs: backward_kernel(*refs, total_tiles=total_tiles),
        (shape((count, width), F32), shape((count, width), F32), shape(pair, BF16), shape(pair, BF16)),
        "ss" + "v" * 13,
        [
            pltpu.VMEM((3 * count, width), BF16),
            pltpu.VMEM((2 * slots, width), BF16),
            pltpu.VMEM((count, width), BF16),
            pltpu.VMEM((3 * count, width), F32),
            pltpu.VMEM((3 * count, width), F32),
        ],
        "attention_grad", 10 * MICRO, 24,
    )(seq, offsets, ids_t, gates_t, home, grad, unit, inv, gain, perm_t, q, vl, v, vr, wts)
    from_right = lax.ppermute(to_left, "seq", down_by).astype(F32)
    from_left = lax.ppermute(to_right, "seq", up_by).astype(F32)

    def finish(own_part, i):
        return (own_part + from_right[i] + from_left[i]).astype(BF16)[None]

    return (finish(k_own, 0), finish(v_own, 1))


def solution(mesh):
    rows = P("exp", "seq", None)
    weights = P("exp", "seq", None, None)
    return jax.shard_map(
        on_device,
        mesh=mesh,
        in_specs=(rows, rows, rows, rows, P(), rows, rows, rows, weights, weights, weights),
        out_specs=(rows, rows),
        check_vma=False,
    )
```

```python
import jax
import jax.numpy as jnp
import numpy as np
from jax import lax
from jax.experimental import pallas as pl
from jax.experimental.pallas import tpu as pltpu
from jax.sharding import PartitionSpec as P

HEAD_DIM = 128
TILE = 64
NBR = 3
CAP = 5
PIECES = 8
GROUP = 8
EPSILON = 1e-06
ATTN = 8
UNROLL = 4
MICRO = 1 << 30
F32 = jnp.float32
BF16 = jnp.bfloat16

CELL = PIECES * CAP
CHUNK = GROUP * CELL
ROWS = GROUP * CAP


def shuffle_matrix():
    out = np.zeros((CHUNK, CHUNK), np.float32)
    for d in range(GROUP):
        for q in range(PIECES):
            for r in range(CAP):
                out[d * CELL + q * CAP + r, q * ROWS + d * CAP + r] = 1.0
    return out


def dot(a, b):
    return jnp.dot(a, b, preferred_element_type=F32)


def dot_nt(a, b):
    return lax.dot_general(a, b, (((1,), (1,)), ((), ())), preferred_element_type=F32)


def dot_tn(a, b):
    return lax.dot_general(a, b, (((0,), (0,)), ((), ())), preferred_element_type=F32)


def to_wire(rows_ref, base, perm, chunk, piece):
    start = base + chunk * ROWS
    stacked = jnp.concatenate(
        [rows_ref[start : start + ROWS, q * piece : (q + 1) * piece] for q in range(PIECES)], axis=0
    )
    return dot(perm, stacked.astype(BF16)).astype(BF16)


def from_wire(block_ref, rows_ref, base, perm_t, chunks, piece):
    if not isinstance(block_ref, list):
        block_ref = [block_ref[c * CHUNK : (c + 1) * CHUNK, :] for c in range(chunks)]
    for pair in range(chunks // 2):
        low = dot(perm_t, block_ref[2 * pair])
        high = dot(perm_t, block_ref[2 * pair + 1])
        start = base + 2 * pair * ROWS
        for q in range(PIECES):
            both = jnp.concatenate(
                [low[q * ROWS : (q + 1) * ROWS], high[q * ROWS : (q + 1) * ROWS]], axis=0
            )
            rows_ref[start : start + 2 * ROWS, q * piece : (q + 1) * piece] = both.astype(BF16)


def slot_rows(ids_ref, half, experts):
    tokens = ids_ref.shape[1]
    first = ids_ref[0:1, :]
    second = ids_ref[1:2, :]
    names = lax.broadcasted_iota(jnp.int32, (experts, tokens), 0)
    hot0 = (names == first).astype(F32)
    hot1 = (names == second).astype(F32)
    before = (
        lax.broadcasted_iota(jnp.int32, (tokens, tokens), 0)
        < lax.broadcasted_iota(jnp.int32, (tokens, tokens), 1)
    ).astype(F32).astype(BF16)
    seen0 = dot(hot0.astype(BF16), before)
    seen1 = dot(hot1.astype(BF16), before) + jnp.sum(hot0, axis=1, keepdims=True)
    rank0 = jnp.sum(hot0 * seen0, axis=0, keepdims=True).astype(jnp.int32)
    rank1 = jnp.sum(hot1 * seen1, axis=0, keepdims=True).astype(jnp.int32)
    slots = (experts // 2) * CAP
    slot0 = ((first & 1) ^ half) * slots + (first >> 1) * CAP + rank0
    slot1 = ((second & 1) ^ half) * slots + (second >> 1) * CAP + rank1
    return slot0, slot1


def place_rows(ids_ref, half, experts, x, rows_ref):
    slot0, slot1 = slot_rows(ids_ref, half, experts)
    places = lax.broadcasted_iota(jnp.int32, (rows_ref.shape[0], x.shape[0]), 0)
    hot = ((places == slot0) | (places == slot1)).astype(F32).astype(BF16)
    rows_ref[...] = dot(hot, x)


def send_rows(seq_ref, ids_ref, x, perm_ref, out_ref, rows_ref):
    columns = out_ref.shape[0]
    piece = out_ref.shape[3]
    place_rows(ids_ref, seq_ref[0] // 4, 2 * columns, x, rows_ref)
    perm = perm_ref[...]
    for rel in range(2):
        for chunk in range(columns // GROUP):
            block = to_wire(rows_ref, rel * columns * CAP, perm, chunk, piece)
            out_ref[chunk * GROUP : (chunk + 1) * GROUP, rel] = block.reshape(GROUP, CELL, piece)


def grad_kernel(seq_ref, ids_ref, x_ref, perm_ref, out_ref, rows_ref):
    send_rows(seq_ref, ids_ref, x_ref[...], perm_ref, out_ref, rows_ref)


def tile_places(seq_ref, offs_ref, tile, tiles, total):
    places = []
    valid = []
    for m in range(NBR):
        off = offs_ref[tile, m]
        places.append(pl.multiple_of((tile + 2 + off) * TILE, TILE))
        where = seq_ref[0] * tiles + tile + off
        valid.append((where >= 0) & (where < total))
    return places, valid


def head_spans(step, heads, tiles):
    spans = []
    for u in range(UNROLL):
        h = step * UNROLL + u
        lanes = pl.ds(pl.multiple_of(h * HEAD_DIM, HEAD_DIM), HEAD_DIM)
        spans += [(t, h, slice(t * TILE, (t + 1) * TILE), lanes) for t in range(tiles)]
    return spans


def window(ref, places, lanes):
    return jnp.concatenate([ref[pl.ds(p, TILE), lanes] for p in places], axis=0)


def fill_halo(dst_ref, left_ref, own_ref, right_ref):
    count = own_ref.shape[0]
    for i, src in enumerate((left_ref, own_ref, right_ref)):
        dst_ref[i * count : (i + 1) * count, :] = src[...]


def forward_kernel(
    seq_ref, offs_ref, ids_ref, q_ref, kl_ref, k_ref, kr_ref, vl_ref, v_ref, vr_ref, gain_ref,
    perm_ref, wts_ref, unit_ref, inv_ref, sent_ref, kx_ref, vx_ref, out_ref, rows_ref, total_tiles,
):
    fill_halo(kx_ref, kl_ref, k_ref, kr_ref)
    fill_halo(vx_ref, vl_ref, v_ref, vr_ref)
    count, width = q_ref.shape
    heads = width // HEAD_DIM
    tiles = count // TILE
    scale = HEAD_DIM ** (-0.5)
    lane = lax.broadcasted_iota(jnp.int32, (TILE, NBR * TILE), 1) // TILE
    spots = []
    biases = []
    for t in range(tiles):
        places, valid = tile_places(seq_ref, offs_ref, t, tiles, total_tiles)
        bias = jnp.zeros((TILE, NBR * TILE), F32)
        for m in range(NBR):
            lost = jnp.where(valid[m], 0.0, -jnp.inf).astype(F32)
            bias = jnp.where(lane == m, lost, bias)
        spots.append(places)
        biases.append(bias)

    def body(step, carry):
        spans = head_spans(step, heads, tiles)
        scores = [
            dot_nt(q_ref[rows, lanes], window(kx_ref, spots[t], lanes)) * scale + biases[t]
            for t, h, rows, lanes in spans
        ]
        tops = [jnp.max(x, axis=-1, keepdims=True) for x in scores]
        raised = [jnp.exp(x - top) for x, top in zip(scores, tops)]
        sums = [jnp.sum(x, axis=-1, keepdims=True) for x in raised]
        weights = [x / total for x, total in zip(raised, sums)]
        for x, (t, h, rows, lanes) in zip(weights, spans):
            wts_ref[t * heads + h] = x
            out_ref[rows, lanes] = dot(x.astype(BF16), window(vx_ref, spots[t], lanes))
        return carry

    lax.fori_loop(0, heads // UNROLL, body, 0)
    out = out_ref[...]
    inv = lax.rsqrt(jnp.mean(out * out, axis=-1, keepdims=True) + EPSILON)
    unit = out * inv
    unit_ref[...] = unit
    inv_ref[...] = jnp.broadcast_to(inv, inv_ref.shape)
    normed = (unit * gain_ref[...]).astype(BF16)
    send_rows(seq_ref, ids_ref, normed, perm_ref, sent_ref, rows_ref)


def hidden_kernel(*refs, blocks):
    ins = refs[:blocks]
    perm_t_ref, down0_ref, down1_ref, out_ref, rows_ref = refs[blocks:]
    piece = ins[0].shape[1]
    chunks = ins[0].shape[0] // CHUNK
    perm_t = perm_t_ref[...]
    for b, block in enumerate(ins):
        from_wire(block, rows_ref, b * chunks * ROWS, perm_t, chunks, piece)
    part = down0_ref.shape[0]
    for i, w_ref in enumerate((down0_ref, down1_ref)):
        out_ref[:, i * part : (i + 1) * part] = dot_nt(rows_ref[...], w_ref[...])


def expert_kernel(*refs, blocks):
    ins = refs[:blocks]
    hg_ref, perm_ref, perm_t_ref = refs[blocks : blocks + 3]
    weights = refs[blocks + 3 : blocks + 7]
    outs = refs[blocks + 7 : 2 * blocks + 7]
    rows_ref, act_ref, total_ref = refs[2 * blocks + 7 :]
    piece = ins[0].shape[1]
    chunks = ins[0].shape[0] // CHUNK
    perm_t = perm_t_ref[...]
    for b, block in enumerate(ins):
        from_wire(block, rows_ref, b * chunks * ROWS, perm_t, chunks, piece)
    width, part = weights[0].shape
    for i in range(2):
        gate_proj = dot(rows_ref[...], weights[2 * i][...])
        up_proj = dot(rows_ref[...], weights[2 * i + 1][...])
        hidden = hg_ref[:, i * part : (i + 1) * part]
        sig = jax.nn.sigmoid(gate_proj)
        act_ref[2 * i + 1] = (hidden * gate_proj * sig).astype(BF16)
        act_ref[2 * i] = (hidden * up_proj * sig * (1.0 + gate_proj * (1.0 - sig))).astype(BF16)
    for n in range(width // 512):
        cols = slice(n * 512, (n + 1) * 512)
        total = dot_nt(act_ref[0], weights[0][cols, :])
        for i in range(1, 4):
            total = total + dot_nt(act_ref[i], weights[i][cols, :])
        total_ref[:, cols] = total
    perm = perm_ref[...]
    for b, dst in enumerate(outs):
        for chunk in range(chunks):
            block = to_wire(total_ref, b * chunks * ROWS, perm, chunk, piece)
            dst[chunk * CHUNK : (chunk + 1) * CHUNK, :] = block


def backward_kernel(
    seq_ref, offs_ref, ids_ref, gates_ref, home_ref, grad_ref, unit_ref, inv_ref, gain_ref,
    perm_t_ref, q_ref, vl_ref, v_ref, vr_ref, wts_ref, k_out_ref, v_out_ref, to_left_ref,
    to_right_ref, vx_ref, rows_ref, ag_ref, ka_ref, va_ref, total_tiles,
):
    fill_halo(vx_ref, vl_ref, v_ref, vr_ref)
    count, width = q_ref.shape
    heads = width // HEAD_DIM
    tiles = count // TILE
    scale = HEAD_DIM ** (-0.5)
    ka_ref[...] = jnp.zeros_like(ka_ref)
    va_ref[...] = jnp.zeros_like(va_ref)
    columns, _, _, piece = home_ref.shape
    chunks = columns // GROUP
    perm_t = perm_t_ref[...]
    for rel in range(2):
        blocks = [
            home_ref[c * GROUP : (c + 1) * GROUP, rel].reshape(CHUNK, piece) for c in range(chunks)
        ]
        from_wire(blocks, rows_ref, rel * chunks * ROWS, perm_t, chunks, piece)
    slot0, slot1 = slot_rows(ids_ref, seq_ref[0] // 4, 2 * columns)
    places = lax.broadcasted_iota(jnp.int32, (rows_ref.shape[0], count), 0)
    mix = jnp.where(places == slot0, gates_ref[0:1, :], 0.0)
    mix = jnp.where(places == slot1, gates_ref[1:2, :], mix)
    high = mix.astype(BF16)
    low = (mix - high.astype(F32)).astype(BF16)
    normed_grad = dot_tn(high, rows_ref[...]) + dot_tn(low, rows_ref[...])
    scaled = normed_grad * gain_ref[...]
    unit = unit_ref[...]
    inner = jnp.mean(scaled * unit, axis=-1, keepdims=True)
    attn_grad = grad_ref[...].astype(F32) + inv_ref[:, 0:1] * (scaled - unit * inner)
    ag_ref[...] = attn_grad.astype(BF16)
    spots = [tile_places(seq_ref, offs_ref, t, tiles, total_tiles)[0] for t in range(tiles)]
    def body(step, carry):
        spans = head_spans(step, heads, tiles)
        prob_grads = [
            dot_nt(ag_ref[rows, lanes], window(vx_ref, spots[t], lanes))
            for t, h, rows, lanes in spans
        ]
        values = [
            dot_tn(wts_ref[t * heads + h].astype(BF16), ag_ref[rows, lanes])
            for t, h, rows, lanes in spans
        ]
        sums = [
            jnp.sum(wts_ref[t * heads + h] * x, axis=-1, keepdims=True)
            for x, (t, h, rows, lanes) in zip(prob_grads, spans)
        ]
        score_grads = [
            (wts_ref[t * heads + h] * (x - total)).astype(BF16)
            for x, total, (t, h, rows, lanes) in zip(prob_grads, sums, spans)
        ]
        keys = [
            dot_tn(x, q_ref[rows, lanes]) * scale
            for x, (t, h, rows, lanes) in zip(score_grads, spans)
        ]
        for acc_ref, parts in ((va_ref, values), (ka_ref, keys)):
            for x, (t, h, rows, lanes) in zip(parts, spans):
                for m in range(NBR):
                    acc_ref[pl.ds(spots[t][m], TILE), lanes] += x[m * TILE : (m + 1) * TILE]
        return carry

    lax.fori_loop(0, heads // UNROLL, body, 0)
    k_out_ref[...] = ka_ref[count : 2 * count, :]
    v_out_ref[...] = va_ref[count : 2 * count, :]
    to_left_ref[0] = ka_ref[0:count, :].astype(BF16)
    to_left_ref[1] = va_ref[0:count, :].astype(BF16)
    to_right_ref[0] = ka_ref[2 * count : 3 * count, :].astype(BF16)
    to_right_ref[1] = va_ref[2 * count : 3 * count, :].astype(BF16)


def call(body, outs, kinds, scratch, name, flops, megabytes):
    spaces = {"s": pltpu.SMEM, "v": pltpu.VMEM}
    return pl.pallas_call(
        body,
        out_shape=outs,
        in_specs=[pl.BlockSpec(memory_space=spaces[kind]) for kind in kinds],
        out_specs=[pl.BlockSpec(memory_space=pltpu.VMEM) for _ in outs],
        scratch_shapes=scratch,
        compiler_params=pltpu.CompilerParams(vmem_limit_bytes=megabytes << 20),
        cost_estimate=pl.CostEstimate(flops=flops, transcendentals=0, bytes_accessed=1 << 20),
        name=name,
    )


def shape(dims, kind):
    return jax.ShapeDtypeStruct(dims, kind)


def on_device(
    queries, keys, values, out_grad, norm_gain, gate_values, expert_ids, tile_offsets, gate_weight,
    up_weight, down_weight,
):
    count, width = queries.shape[1:]
    heads = width // HEAD_DIM
    tiles = count // TILE
    seq_count = lax.axis_size("seq")
    columns = lax.axis_size("exp")
    total_tiles = tiles * seq_count
    piece = width // PIECES
    slots = columns * CAP
    seq = lax.axis_index("seq").astype(jnp.int32).reshape(1)
    ids_t = expert_ids[0].T
    gates_t = gate_values[0].T
    offsets = tile_offsets[0]
    gain = norm_gain.reshape(1, width)
    perm = jnp.asarray(shuffle_matrix(), BF16)
    perm_t = jnp.asarray(shuffle_matrix().T, BF16)
    q, k, v, grad = queries[0], keys[0], values[0], out_grad[0]
    gate, up, down = gate_weight[0, 0], up_weight[0, 0], down_weight[0, 0]
    wire = (columns, 2, CELL, piece)
    flat = (columns * CELL, piece)

    up_by = [(i, i + 1) for i in range(seq_count - 1)]
    down_by = [(i + 1, i) for i in range(seq_count - 1)]

    def swap(x, bits):
        return lax.ppermute(x, "seq", [(i, i ^ bits) for i in range(seq_count)])

    def exchange(x):
        return lax.all_to_all(x, "exp", split_axis=0, concat_axis=0, tiled=True)

    barrier = lax.optimization_barrier
    pair = (2, count, width)
    (sent_grad,) = call(
        grad_kernel, (shape(wire, BF16),), "svvv", [pltpu.VMEM((2 * slots, width), F32)],
        "place_grad", 4 * MICRO, 12,
    )(seq, ids_t, grad, perm)
    k, v, sent_grad = barrier((k, v, sent_grad))
    kl, kr = lax.ppermute(k, "seq", up_by), lax.ppermute(k, "seq", down_by)
    vl, vr = lax.ppermute(v, "seq", up_by), lax.ppermute(v, "seq", down_by)
    got_grad = exchange(sent_grad)


    wts, unit, inv, sent = call(
        lambda *refs: forward_kernel(*refs, total_tiles=total_tiles),
        (
            shape((tiles * heads, TILE, NBR * TILE), F32),
            shape((count, width), F32),
            shape((count, HEAD_DIM), F32),
            shape(wire, BF16),
        ),
        "ssv" + "v" * 9,
        [
            pltpu.VMEM((3 * count, width), BF16),
            pltpu.VMEM((3 * count, width), BF16),
            pltpu.VMEM((count, width), F32),
            pltpu.VMEM((2 * slots, width), F32),
        ],
        "attention", ATTN * MICRO, 20,
    )(seq, offsets, ids_t, q, kl, k, kr, vl, v, vr, gain, perm)

    sent, *weights = barrier((sent, gate, up, down))
    sent, got_grad = barrier((sent, got_grad))
    gate_s, up_s, down_s = [swap(x, 1) for x in weights]
    got = exchange(sent)
    g0, grad_oth = got_grad[:, 0].reshape(flat), got_grad[:, 1].reshape(flat)
    g1, g2 = swap(grad_oth, 6), swap(g0, 2)
    g3 = swap(grad_oth, 4)
    n0, oth = got[:, 0].reshape(flat), got[:, 1].reshape(flat)
    n1, n2 = swap(oth, 6), swap(n0, 2)
    n3 = swap(n1, 2)

    part = down.shape[0]

    def hidden(ins, micros):
        blocks = len(ins)
        (out,) = call(
            lambda *refs: hidden_kernel(*refs, blocks=blocks),
            (shape((blocks * slots, 2 * part), F32),),
            "v" * (blocks + 3),
            [pltpu.VMEM((blocks * slots, width), BF16)],
            "hidden", micros * MICRO, 14,
        )(*ins, perm_t, down, down_s)
        return out

    def expert(ins, hg, micros):
        blocks = len(ins)
        return call(
            lambda *refs: expert_kernel(*refs, blocks=blocks),
            (shape(flat, BF16),) * blocks,
            "v" * (blocks + 7),
            [
                pltpu.VMEM((blocks * slots, width), BF16),
                pltpu.VMEM((4, blocks * slots, part), BF16),
                pltpu.VMEM((blocks * slots, width), F32),
            ],
            "expert", micros * MICRO, 24,
        )(*ins, hg, perm, perm_t, gate, up, gate_s, up_s)

    hidden_own = hidden((g0,), 4)
    hidden_near = hidden((g1, g2), 5)
    (p0,) = expert((n0,), hidden_own, 9)
    p0, g3 = barrier((p0, g3))
    hidden_far = hidden((g3,), 4)
    hidden_far, n1, n2 = barrier((hidden_far, n1, n2))
    p1, p2 = expert((n1, n2), hidden_near, 11)
    (p3,) = expert((n3,), hidden_far, 9)
    h1, h2 = swap(p1, 6), swap(p2, 2)
    h3 = swap(p3, 4)
    own = (p0.astype(F32) + h2.astype(F32)).astype(BF16).reshape(columns, 1, CELL, piece)
    oth = (h1.astype(F32) + h3.astype(F32)).astype(BF16).reshape(columns, 1, CELL, piece)
    home = exchange(jnp.concatenate([own, oth], axis=1))

    k_own, v_own, to_left, to_right = call(
        lambda *refs: backward_kernel(*refs, total_tiles=total_tiles),
        (shape((count, width), F32), shape((count, width), F32), shape(pair, BF16), shape(pair, BF16)),
        "ss" + "v" * 13,
        [
            pltpu.VMEM((3 * count, width), BF16),
            pltpu.VMEM((2 * slots, width), BF16),
            pltpu.VMEM((count, width), BF16),
            pltpu.VMEM((3 * count, width), F32),
            pltpu.VMEM((3 * count, width), F32),
        ],
        "attention_grad", 10 * MICRO, 24,
    )(seq, offsets, ids_t, gates_t, home, grad, unit, inv, gain, perm_t, q, vl, v, vr, wts)
    from_right = lax.ppermute(to_left, "seq", down_by).astype(F32)
    from_left = lax.ppermute(to_right, "seq", up_by).astype(F32)

    def finish(own_part, i):
        return (own_part + from_right[i] + from_left[i]).astype(BF16)[None]

    return (finish(k_own, 0), finish(v_own, 1))


def solution(mesh):
    rows = P("exp", "seq", None)
    weights = P("exp", "seq", None, None)
    return jax.shard_map(
        on_device,
        mesh=mesh,
        in_specs=(rows, rows, rows, rows, P(), rows, rows, rows, weights, weights, weights),
        out_specs=(rows, rows),
        check_vma=False,
    )
```

```python
import jax
import jax.numpy as jnp
import numpy as np
from jax import lax
from jax.experimental import pallas as pl
from jax.experimental.pallas import tpu as pltpu
from jax.sharding import PartitionSpec as P

HEAD_DIM = 128
TILE = 64
NBR = 3
CAP = 5
PIECES = 8
GROUP = 8
EPSILON = 1e-06
ATTN = 8
UNROLL = 4
MICRO = 1 << 30
F32 = jnp.float32
BF16 = jnp.bfloat16

CELL = PIECES * CAP
CHUNK = GROUP * CELL
ROWS = GROUP * CAP


def shuffle_matrix():
    out = np.zeros((CHUNK, CHUNK), np.float32)
    for d in range(GROUP):
        for q in range(PIECES):
            for r in range(CAP):
                out[d * CELL + q * CAP + r, q * ROWS + d * CAP + r] = 1.0
    return out


def dot(a, b):
    return jnp.dot(a, b, preferred_element_type=F32)


def dot_nt(a, b):
    return lax.dot_general(a, b, (((1,), (1,)), ((), ())), preferred_element_type=F32)


def dot_tn(a, b):
    return lax.dot_general(a, b, (((0,), (0,)), ((), ())), preferred_element_type=F32)


def to_wire(rows_ref, base, perm, chunk, piece):
    start = base + chunk * ROWS
    stacked = jnp.concatenate(
        [rows_ref[start : start + ROWS, q * piece : (q + 1) * piece] for q in range(PIECES)], axis=0
    )
    return dot(perm, stacked.astype(BF16)).astype(BF16)


def from_wire(block_ref, rows_ref, base, perm_t, chunks, piece):
    for pair in range(chunks // 2):
        low = dot(perm_t, block_ref[2 * pair * CHUNK : (2 * pair + 1) * CHUNK, :])
        high = dot(perm_t, block_ref[(2 * pair + 1) * CHUNK : (2 * pair + 2) * CHUNK, :])
        start = base + 2 * pair * ROWS
        for q in range(PIECES):
            both = jnp.concatenate(
                [low[q * ROWS : (q + 1) * ROWS], high[q * ROWS : (q + 1) * ROWS]], axis=0
            )
            rows_ref[start : start + 2 * ROWS, q * piece : (q + 1) * piece] = both.astype(BF16)


def slot_rows(ids_ref, half, experts):
    tokens = ids_ref.shape[1]
    first = ids_ref[0:1, :]
    second = ids_ref[1:2, :]
    names = lax.broadcasted_iota(jnp.int32, (experts, tokens), 0)
    hot0 = (names == first).astype(F32)
    hot1 = (names == second).astype(F32)
    before = (
        lax.broadcasted_iota(jnp.int32, (tokens, tokens), 0)
        < lax.broadcasted_iota(jnp.int32, (tokens, tokens), 1)
    ).astype(F32).astype(BF16)
    seen0 = dot(hot0.astype(BF16), before)
    seen1 = dot(hot1.astype(BF16), before) + jnp.sum(hot0, axis=1, keepdims=True)
    rank0 = jnp.sum(hot0 * seen0, axis=0, keepdims=True).astype(jnp.int32)
    rank1 = jnp.sum(hot1 * seen1, axis=0, keepdims=True).astype(jnp.int32)
    slots = (experts // 2) * CAP
    slot0 = ((first & 1) ^ half) * slots + (first >> 1) * CAP + rank0
    slot1 = ((second & 1) ^ half) * slots + (second >> 1) * CAP + rank1
    return slot0, slot1


def place_rows(ids_ref, half, experts, x, rows_ref):
    slot0, slot1 = slot_rows(ids_ref, half, experts)
    places = lax.broadcasted_iota(jnp.int32, (rows_ref.shape[0], x.shape[0]), 0)
    hot = ((places == slot0) | (places == slot1)).astype(F32).astype(BF16)
    rows_ref[...] = dot(hot, x)


def send_rows(seq_ref, ids_ref, x, perm_ref, out_ref, rows_ref):
    columns = out_ref.shape[0]
    piece = out_ref.shape[3]
    place_rows(ids_ref, seq_ref[0] // 4, 2 * columns, x, rows_ref)
    perm = perm_ref[...]
    for rel in range(2):
        for chunk in range(columns // GROUP):
            block = to_wire(rows_ref, rel * columns * CAP, perm, chunk, piece)
            out_ref[chunk * GROUP : (chunk + 1) * GROUP, rel] = block.reshape(GROUP, CELL, piece)


def grad_kernel(seq_ref, ids_ref, x_ref, perm_ref, out_ref, rows_ref):
    send_rows(seq_ref, ids_ref, x_ref[...], perm_ref, out_ref, rows_ref)


def tile_places(seq_ref, offs_ref, tile, tiles, total):
    places = []
    valid = []
    for m in range(NBR):
        off = offs_ref[tile, m]
        places.append(pl.multiple_of((tile + 2 + off) * TILE, TILE))
        where = seq_ref[0] * tiles + tile + off
        valid.append((where >= 0) & (where < total))
    return places, valid


def head_spans(step, heads, tiles):
    spans = []
    for u in range(UNROLL):
        h = step * UNROLL + u
        lanes = pl.ds(pl.multiple_of(h * HEAD_DIM, HEAD_DIM), HEAD_DIM)
        spans += [(t, h, slice(t * TILE, (t + 1) * TILE), lanes) for t in range(tiles)]
    return spans


def window(ref, places, lanes):
    return jnp.concatenate([ref[pl.ds(p, TILE), lanes] for p in places], axis=0)


def fill_halo(dst_ref, left_ref, own_ref, right_ref):
    count = own_ref.shape[0]
    for i, src in enumerate((left_ref, own_ref, right_ref)):
        dst_ref[i * count : (i + 1) * count, :] = src[...]


def forward_kernel(
    seq_ref, offs_ref, ids_ref, q_ref, kl_ref, k_ref, kr_ref, vl_ref, v_ref, vr_ref, gain_ref,
    perm_ref, wts_ref, unit_ref, inv_ref, sent_ref, kx_ref, vx_ref, out_ref, rows_ref, total_tiles,
):
    fill_halo(kx_ref, kl_ref, k_ref, kr_ref)
    fill_halo(vx_ref, vl_ref, v_ref, vr_ref)
    count, width = q_ref.shape
    heads = width // HEAD_DIM
    tiles = count // TILE
    scale = HEAD_DIM ** (-0.5)
    lane = lax.broadcasted_iota(jnp.int32, (TILE, NBR * TILE), 1) // TILE
    spots = []
    biases = []
    for t in range(tiles):
        places, valid = tile_places(seq_ref, offs_ref, t, tiles, total_tiles)
        bias = jnp.zeros((TILE, NBR * TILE), F32)
        for m in range(NBR):
            lost = jnp.where(valid[m], 0.0, -jnp.inf).astype(F32)
            bias = jnp.where(lane == m, lost, bias)
        spots.append(places)
        biases.append(bias)

    def body(step, carry):
        spans = head_spans(step, heads, tiles)
        scores = [
            dot_nt(q_ref[rows, lanes], window(kx_ref, spots[t], lanes)) * scale + biases[t]
            for t, h, rows, lanes in spans
        ]
        tops = [jnp.max(x, axis=-1, keepdims=True) for x in scores]
        raised = [jnp.exp(x - top) for x, top in zip(scores, tops)]
        sums = [jnp.sum(x, axis=-1, keepdims=True) for x in raised]
        weights = [x / total for x, total in zip(raised, sums)]
        for x, (t, h, rows, lanes) in zip(weights, spans):
            wts_ref[t * heads + h] = x
            out_ref[rows, lanes] = dot(x.astype(BF16), window(vx_ref, spots[t], lanes))
        return carry

    lax.fori_loop(0, heads // UNROLL, body, 0)
    out = out_ref[...]
    inv = lax.rsqrt(jnp.mean(out * out, axis=-1, keepdims=True) + EPSILON)
    unit = out * inv
    unit_ref[...] = unit
    inv_ref[...] = jnp.broadcast_to(inv, inv_ref.shape)
    normed = (unit * gain_ref[...]).astype(BF16)
    send_rows(seq_ref, ids_ref, normed, perm_ref, sent_ref, rows_ref)


def hidden_kernel(*refs, blocks):
    ins = refs[:blocks]
    perm_t_ref, down0_ref, down1_ref, out_ref, rows_ref = refs[blocks:]
    piece = ins[0].shape[1]
    chunks = ins[0].shape[0] // CHUNK
    perm_t = perm_t_ref[...]
    for b, block in enumerate(ins):
        from_wire(block, rows_ref, b * chunks * ROWS, perm_t, chunks, piece)
    part = down0_ref.shape[0]
    for i, w_ref in enumerate((down0_ref, down1_ref)):
        out_ref[:, i * part : (i + 1) * part] = dot_nt(rows_ref[...], w_ref[...])


def expert_kernel(*refs, blocks):
    ins = refs[:blocks]
    hg_ref, perm_ref, perm_t_ref = refs[blocks : blocks + 3]
    gate_ref, up_ref, gate_hbm, up_hbm = refs[blocks + 3 : blocks + 7]
    outs = refs[blocks + 7 : 2 * blocks + 7]
    rows_ref, act_ref, total_ref, w_ref, sems = refs[2 * blocks + 7 :]
    copies = [
        pltpu.make_async_copy(src, w_ref.at[i], sems.at[i])
        for i, src in enumerate((gate_hbm, up_hbm))
    ]
    for copy in copies:
        copy.start()
    weights = (gate_ref, up_ref, w_ref.at[0], w_ref.at[1])
    piece = ins[0].shape[1]
    chunks = ins[0].shape[0] // CHUNK
    perm_t = perm_t_ref[...]
    for b, block in enumerate(ins):
        from_wire(block, rows_ref, b * chunks * ROWS, perm_t, chunks, piece)
    width, part = weights[0].shape
    for i in range(2):
        if i == 1:
            for copy in copies:
                copy.wait()
        gate_proj = dot(rows_ref[...], weights[2 * i][...])
        up_proj = dot(rows_ref[...], weights[2 * i + 1][...])
        hidden = hg_ref[:, i * part : (i + 1) * part]
        sig = jax.nn.sigmoid(gate_proj)
        act_ref[2 * i + 1] = (hidden * gate_proj * sig).astype(BF16)
        act_ref[2 * i] = (hidden * up_proj * sig * (1.0 + gate_proj * (1.0 - sig))).astype(BF16)
    for n in range(width // 512):
        cols = slice(n * 512, (n + 1) * 512)
        total = dot_nt(act_ref[0], weights[0][cols, :])
        for i in range(1, 4):
            total = total + dot_nt(act_ref[i], weights[i][cols, :])
        total_ref[:, cols] = total
    perm = perm_ref[...]
    for b, dst in enumerate(outs):
        for chunk in range(chunks):
            block = to_wire(total_ref, b * chunks * ROWS, perm, chunk, piece)
            dst[chunk * CHUNK : (chunk + 1) * CHUNK, :] = block


def backward_kernel(
    seq_ref, offs_ref, ids_ref, gates_ref, own_ref, oth_ref, grad_ref, unit_ref, inv_ref, gain_ref,
    perm_t_ref, q_ref, vl_ref, v_ref, vr_ref, wts_ref, k_out_ref, v_out_ref, to_left_ref,
    to_right_ref, vx_ref, rows_ref, ag_ref, ka_ref, va_ref, total_tiles,
):
    fill_halo(vx_ref, vl_ref, v_ref, vr_ref)
    count, width = q_ref.shape
    heads = width // HEAD_DIM
    tiles = count // TILE
    scale = HEAD_DIM ** (-0.5)
    ka_ref[...] = jnp.zeros_like(ka_ref)
    va_ref[...] = jnp.zeros_like(va_ref)
    piece = own_ref.shape[1]
    chunks = own_ref.shape[0] // CHUNK
    columns = chunks * GROUP
    perm_t = perm_t_ref[...]
    from_wire(own_ref, rows_ref, 0, perm_t, chunks, piece)
    from_wire(oth_ref, rows_ref, chunks * ROWS, perm_t, chunks, piece)
    slot0, slot1 = slot_rows(ids_ref, seq_ref[0] // 4, 2 * columns)
    places = lax.broadcasted_iota(jnp.int32, (rows_ref.shape[0], count), 0)
    mix = jnp.where(places == slot0, gates_ref[0:1, :], 0.0)
    mix = jnp.where(places == slot1, gates_ref[1:2, :], mix)
    high = mix.astype(BF16)
    low = (mix - high.astype(F32)).astype(BF16)
    normed_grad = dot_tn(high, rows_ref[...]) + dot_tn(low, rows_ref[...])
    scaled = normed_grad * gain_ref[...]
    unit = unit_ref[...]
    inner = jnp.mean(scaled * unit, axis=-1, keepdims=True)
    attn_grad = grad_ref[...].astype(F32) + inv_ref[:, 0:1] * (scaled - unit * inner)
    ag_ref[...] = attn_grad.astype(BF16)
    spots = [tile_places(seq_ref, offs_ref, t, tiles, total_tiles)[0] for t in range(tiles)]
    def body(step, carry):
        spans = head_spans(step, heads, tiles)
        prob_grads = [
            dot_nt(ag_ref[rows, lanes], window(vx_ref, spots[t], lanes))
            for t, h, rows, lanes in spans
        ]
        values = [
            dot_tn(wts_ref[t * heads + h].astype(BF16), ag_ref[rows, lanes])
            for t, h, rows, lanes in spans
        ]
        sums = [
            jnp.sum(wts_ref[t * heads + h] * x, axis=-1, keepdims=True)
            for x, (t, h, rows, lanes) in zip(prob_grads, spans)
        ]
        score_grads = [
            (wts_ref[t * heads + h] * (x - total)).astype(BF16)
            for x, total, (t, h, rows, lanes) in zip(prob_grads, sums, spans)
        ]
        keys = [
            dot_tn(x, q_ref[rows, lanes]) * scale
            for x, (t, h, rows, lanes) in zip(score_grads, spans)
        ]
        for acc_ref, parts in ((va_ref, values), (ka_ref, keys)):
            for x, (t, h, rows, lanes) in zip(parts, spans):
                for m in range(NBR):
                    acc_ref[pl.ds(spots[t][m], TILE), lanes] += x[m * TILE : (m + 1) * TILE]
        return carry

    lax.fori_loop(0, heads // UNROLL, body, 0)
    k_out_ref[...] = ka_ref[count : 2 * count, :]
    v_out_ref[...] = va_ref[count : 2 * count, :]
    to_left_ref[0] = ka_ref[0:count, :].astype(BF16)
    to_left_ref[1] = va_ref[0:count, :].astype(BF16)
    to_right_ref[0] = ka_ref[2 * count : 3 * count, :].astype(BF16)
    to_right_ref[1] = va_ref[2 * count : 3 * count, :].astype(BF16)


def call(body, outs, kinds, scratch, name, flops, megabytes):
    spaces = {"s": pltpu.SMEM, "v": pltpu.VMEM, "a": pl.ANY}
    return pl.pallas_call(
        body,
        out_shape=outs,
        in_specs=[pl.BlockSpec(memory_space=spaces[kind]) for kind in kinds],
        out_specs=[pl.BlockSpec(memory_space=pltpu.VMEM) for _ in outs],
        scratch_shapes=scratch,
        compiler_params=pltpu.CompilerParams(vmem_limit_bytes=megabytes << 20),
        cost_estimate=pl.CostEstimate(flops=flops, transcendentals=0, bytes_accessed=1 << 20),
        name=name,
    )


def shape(dims, kind):
    return jax.ShapeDtypeStruct(dims, kind)


def on_device(
    queries, keys, values, out_grad, norm_gain, gate_values, expert_ids, tile_offsets, gate_weight,
    up_weight, down_weight,
):
    count, width = queries.shape[1:]
    heads = width // HEAD_DIM
    tiles = count // TILE
    seq_count = lax.axis_size("seq")
    columns = lax.axis_size("exp")
    total_tiles = tiles * seq_count
    piece = width // PIECES
    slots = columns * CAP
    seq = lax.axis_index("seq").astype(jnp.int32).reshape(1)
    ids_t = expert_ids[0].T
    gates_t = gate_values[0].T
    offsets = tile_offsets[0]
    gain = norm_gain.reshape(1, width)
    perm = jnp.asarray(shuffle_matrix(), BF16)
    perm_t = jnp.asarray(shuffle_matrix().T, BF16)
    q, k, v, grad = queries[0], keys[0], values[0], out_grad[0]
    gate, up, down = gate_weight[0, 0], up_weight[0, 0], down_weight[0, 0]
    wire = (columns, 2, CELL, piece)
    flat = (columns * CELL, piece)

    up_by = [(i, i + 1) for i in range(seq_count - 1)]
    down_by = [(i + 1, i) for i in range(seq_count - 1)]

    def swap(x, bits):
        return lax.ppermute(x, "seq", [(i, i ^ bits) for i in range(seq_count)])

    def exchange(x):
        return lax.all_to_all(x, "exp", split_axis=0, concat_axis=0, tiled=True)

    barrier = lax.optimization_barrier
    pair = (2, count, width)
    (sent_grad,) = call(
        grad_kernel, (shape(wire, BF16),), "svvv", [pltpu.VMEM((2 * slots, width), F32)],
        "place_grad", 4 * MICRO, 56,
    )(seq, ids_t, grad, perm)
    k, v, sent_grad = barrier((k, v, sent_grad))
    kl, kr = lax.ppermute(k, "seq", up_by), lax.ppermute(k, "seq", down_by)
    vl, vr = lax.ppermute(v, "seq", up_by), lax.ppermute(v, "seq", down_by)
    got_grad = exchange(sent_grad)


    wts, unit, inv, sent = call(
        lambda *refs: forward_kernel(*refs, total_tiles=total_tiles),
        (
            shape((tiles * heads, TILE, NBR * TILE), F32),
            shape((count, width), F32),
            shape((count, HEAD_DIM), F32),
            shape(wire, BF16),
        ),
        "ssv" + "v" * 9,
        [
            pltpu.VMEM((3 * count, width), BF16),
            pltpu.VMEM((3 * count, width), BF16),
            pltpu.VMEM((count, width), F32),
            pltpu.VMEM((2 * slots, width), F32),
        ],
        "attention", ATTN * MICRO, 16,
    )(seq, offsets, ids_t, q, kl, k, kr, vl, v, vr, gain, perm)

    sent, *weights = barrier((sent, gate, up, down))
    sent, got_grad = barrier((sent, got_grad))
    gate_s, up_s, down_s = [swap(x, 1) for x in weights]
    got = exchange(sent)
    g0, grad_oth = got_grad[:, 0].reshape(flat), got_grad[:, 1].reshape(flat)
    g1, g2 = swap(grad_oth, 6), swap(g0, 2)
    g3 = swap(grad_oth, 4)
    n0, oth = got[:, 0].reshape(flat), got[:, 1].reshape(flat)
    n1, n2 = swap(oth, 6), swap(n0, 2)
    n3 = swap(n1, 2)

    part = down.shape[0]

    def hidden(ins, micros):
        blocks = len(ins)
        (out,) = call(
            lambda *refs: hidden_kernel(*refs, blocks=blocks),
            (shape((blocks * slots, 2 * part), F32),),
            "v" * (blocks + 3),
            [pltpu.VMEM((blocks * slots, width), BF16)],
            "hidden", micros * MICRO, 8,
        )(*ins, perm_t, down, down_s)
        return out

    def expert(ins, hg, micros):
        blocks = len(ins)
        return call(
            lambda *refs: expert_kernel(*refs, blocks=blocks),
            (shape(flat, BF16),) * blocks,
            "v" * (blocks + 5) + "aa",
            [
                pltpu.VMEM((blocks * slots, width), BF16),
                pltpu.VMEM((4, blocks * slots, part), BF16),
                pltpu.VMEM((blocks * slots, width), F32),
                pltpu.VMEM((2, width, part), BF16),
                pltpu.SemaphoreType.DMA((2,)),
            ],
            "expert", micros * MICRO, 20,
        )(*ins, hg, perm, perm_t, gate, up, gate_s, up_s)

    hidden_own = hidden((g0,), 4)
    hidden_near = hidden((g1, g2), 5)
    (p0,) = expert((n0,), hidden_own, 9)
    p0, g3 = barrier((p0, g3))
    hidden_far = hidden((g3,), 4)
    hidden_far, n1, n2 = barrier((hidden_far, n1, n2))
    p1, p2 = expert((n1, n2), hidden_near, 11)
    (p3,) = expert((n3,), hidden_far, 9)
    h1, h2 = swap(p1, 6), swap(p2, 2)
    half_wire = (columns, CELL, piece)
    h1, h2, p3 = barrier((h1, h2, p3))
    h3 = swap(p3, 4)
    own = (p0.astype(F32) + h2.astype(F32)).astype(BF16)
    oth = (h1.astype(F32) + h3.astype(F32)).astype(BF16)
    home_own = exchange(own.reshape(half_wire)).reshape(flat)
    home_own, oth = barrier((home_own, oth))
    home_oth = exchange(oth.reshape(half_wire)).reshape(flat)

    k_own, v_own, to_left, to_right = call(
        lambda *refs: backward_kernel(*refs, total_tiles=total_tiles),
        (shape((count, width), F32), shape((count, width), F32), shape(pair, BF16), shape(pair, BF16)),
        "ss" + "v" * 14,
        [
            pltpu.VMEM((3 * count, width), BF16),
            pltpu.VMEM((2 * slots, width), BF16),
            pltpu.VMEM((count, width), BF16),
            pltpu.VMEM((3 * count, width), F32),
            pltpu.VMEM((3 * count, width), F32),
        ],
        "attention_grad", 10 * MICRO, 18,
    )(seq, offsets, ids_t, gates_t, home_own, home_oth, grad, unit, inv, gain, perm_t, q, vl, v, vr, wts)
    from_right = lax.ppermute(to_left, "seq", down_by).astype(F32)
    from_left = lax.ppermute(to_right, "seq", up_by).astype(F32)

    def finish(own_part, i):
        return (own_part + from_right[i] + from_left[i]).astype(BF16)[None]

    return (finish(k_own, 0), finish(v_own, 1))


def solution(mesh):
    rows = P("exp", "seq", None)
    weights = P("exp", "seq", None, None)
    return jax.shard_map(
        on_device,
        mesh=mesh,
        in_specs=(rows, rows, rows, rows, P(), rows, rows, rows, weights, weights, weights),
        out_specs=(rows, rows),
        check_vma=False,
    )
```

```python
import jax
import jax.numpy as jnp
import numpy as np
from jax import lax
from jax.experimental import pallas as pl
from jax.experimental.pallas import tpu as pltpu
from jax.sharding import PartitionSpec as P

HEAD_DIM = 128
TILE = 64
NBR = 3
CAP = 5
PIECES = 8
GROUP = 8
EPSILON = 1e-06
ATTN = 8
UNROLL = 4
MICRO = 1 << 30
F32 = jnp.float32
BF16 = jnp.bfloat16

CELL = PIECES * CAP
CHUNK = GROUP * CELL
ROWS = GROUP * CAP


def shuffle_matrix():
    out = np.zeros((CHUNK, CHUNK), np.float32)
    for d in range(GROUP):
        for q in range(PIECES):
            for r in range(CAP):
                out[d * CELL + q * CAP + r, q * ROWS + d * CAP + r] = 1.0
    return out


def dot(a, b):
    return jnp.dot(a, b, preferred_element_type=F32)


def dot_nt(a, b):
    return lax.dot_general(a, b, (((1,), (1,)), ((), ())), preferred_element_type=F32)


def dot_tn(a, b):
    return lax.dot_general(a, b, (((0,), (0,)), ((), ())), preferred_element_type=F32)


def to_wire(rows_ref, base, perm, chunk, piece):
    start = base + chunk * ROWS
    stacked = jnp.concatenate(
        [rows_ref[start : start + ROWS, q * piece : (q + 1) * piece] for q in range(PIECES)], axis=0
    )
    return dot(perm, stacked.astype(BF16)).astype(BF16)


def from_wire(block_ref, rows_ref, base, perm_t, chunks, piece):
    if not isinstance(block_ref, list):
        block_ref = [block_ref[c * CHUNK : (c + 1) * CHUNK, :] for c in range(chunks)]
    for pair in range(chunks // 2):
        low = dot(perm_t, block_ref[2 * pair])
        high = dot(perm_t, block_ref[2 * pair + 1])
        start = base + 2 * pair * ROWS
        for q in range(PIECES):
            both = jnp.concatenate(
                [low[q * ROWS : (q + 1) * ROWS], high[q * ROWS : (q + 1) * ROWS]], axis=0
            )
            rows_ref[start : start + 2 * ROWS, q * piece : (q + 1) * piece] = both.astype(BF16)


def slot_rows(ids_ref, half, experts):
    tokens = ids_ref.shape[1]
    first = ids_ref[0:1, :]
    second = ids_ref[1:2, :]
    names = lax.broadcasted_iota(jnp.int32, (experts, tokens), 0)
    hot0 = (names == first).astype(F32)
    hot1 = (names == second).astype(F32)
    before = (
        lax.broadcasted_iota(jnp.int32, (tokens, tokens), 0)
        < lax.broadcasted_iota(jnp.int32, (tokens, tokens), 1)
    ).astype(F32).astype(BF16)
    seen0 = dot(hot0.astype(BF16), before)
    seen1 = dot(hot1.astype(BF16), before) + jnp.sum(hot0, axis=1, keepdims=True)
    rank0 = jnp.sum(hot0 * seen0, axis=0, keepdims=True).astype(jnp.int32)
    rank1 = jnp.sum(hot1 * seen1, axis=0, keepdims=True).astype(jnp.int32)
    slots = (experts // 2) * CAP
    slot0 = ((first & 1) ^ half) * slots + (first >> 1) * CAP + rank0
    slot1 = ((second & 1) ^ half) * slots + (second >> 1) * CAP + rank1
    return slot0, slot1


def place_rows(ids_ref, half, experts, x, rows_ref):
    slot0, slot1 = slot_rows(ids_ref, half, experts)
    places = lax.broadcasted_iota(jnp.int32, (rows_ref.shape[0], x.shape[0]), 0)
    hot = ((places == slot0) | (places == slot1)).astype(F32).astype(BF16)
    rows_ref[...] = dot(hot, x)


def send_rows(seq_ref, ids_ref, x, perm_ref, out_ref, rows_ref):
    columns = out_ref.shape[0]
    piece = out_ref.shape[3]
    place_rows(ids_ref, seq_ref[0] // 4, 2 * columns, x, rows_ref)
    perm = perm_ref[...]
    for rel in range(2):
        for chunk in range(columns // GROUP):
            block = to_wire(rows_ref, rel * columns * CAP, perm, chunk, piece)
            out_ref[chunk * GROUP : (chunk + 1) * GROUP, rel] = block.reshape(GROUP, CELL, piece)


def grad_kernel(seq_ref, ids_ref, x_ref, perm_ref, out_ref, rows_ref):
    send_rows(seq_ref, ids_ref, x_ref[...], perm_ref, out_ref, rows_ref)


def tile_places(seq_ref, offs_ref, tile, tiles, total):
    places = []
    valid = []
    for m in range(NBR):
        off = offs_ref[tile, m]
        places.append(pl.multiple_of((tile + 2 + off) * TILE, TILE))
        where = seq_ref[0] * tiles + tile + off
        valid.append((where >= 0) & (where < total))
    return places, valid


def head_spans(step, heads, tiles):
    spans = []
    for u in range(UNROLL):
        h = step * UNROLL + u
        lanes = pl.ds(pl.multiple_of(h * HEAD_DIM, HEAD_DIM), HEAD_DIM)
        spans += [(t, h, slice(t * TILE, (t + 1) * TILE), lanes) for t in range(tiles)]
    return spans


def window(ref, places, lanes):
    return jnp.concatenate([ref[pl.ds(p, TILE), lanes] for p in places], axis=0)


def fill_halo(dst_ref, left_ref, own_ref, right_ref):
    count = own_ref.shape[0]
    for i, src in enumerate((left_ref, own_ref, right_ref)):
        dst_ref[i * count : (i + 1) * count, :] = src[...]


def forward_kernel(
    seq_ref, offs_ref, ids_ref, q_ref, kl_ref, k_ref, kr_ref, vl_ref, v_ref, vr_ref, gain_ref,
    perm_ref, wts_ref, unit_ref, inv_ref, sent_ref, kx_ref, vx_ref, out_ref, rows_ref, total_tiles,
):
    fill_halo(kx_ref, kl_ref, k_ref, kr_ref)
    fill_halo(vx_ref, vl_ref, v_ref, vr_ref)
    count, width = q_ref.shape
    heads = width // HEAD_DIM
    tiles = count // TILE
    scale = HEAD_DIM ** (-0.5)
    lane = lax.broadcasted_iota(jnp.int32, (TILE, NBR * TILE), 1) // TILE
    spots = []
    biases = []
    for t in range(tiles):
        places, valid = tile_places(seq_ref, offs_ref, t, tiles, total_tiles)
        bias = jnp.zeros((TILE, NBR * TILE), F32)
        for m in range(NBR):
            lost = jnp.where(valid[m], 0.0, -jnp.inf).astype(F32)
            bias = jnp.where(lane == m, lost, bias)
        spots.append(places)
        biases.append(bias)

    def body(step, carry):
        spans = head_spans(step, heads, tiles)
        scores = [
            dot_nt(q_ref[rows, lanes], window(kx_ref, spots[t], lanes)) * scale + biases[t]
            for t, h, rows, lanes in spans
        ]
        tops = [jnp.max(x, axis=-1, keepdims=True) for x in scores]
        raised = [jnp.exp(x - top) for x, top in zip(scores, tops)]
        sums = [jnp.sum(x, axis=-1, keepdims=True) for x in raised]
        weights = [x / total for x, total in zip(raised, sums)]
        for x, (t, h, rows, lanes) in zip(weights, spans):
            wts_ref[t * heads + h] = x
            out_ref[rows, lanes] = dot(x.astype(BF16), window(vx_ref, spots[t], lanes))
        return carry

    lax.fori_loop(0, heads // UNROLL, body, 0)
    out = out_ref[...]
    inv = lax.rsqrt(jnp.mean(out * out, axis=-1, keepdims=True) + EPSILON)
    unit = out * inv
    unit_ref[...] = unit
    inv_ref[...] = jnp.broadcast_to(inv, inv_ref.shape)
    normed = (unit * gain_ref[...]).astype(BF16)
    send_rows(seq_ref, ids_ref, normed, perm_ref, sent_ref, rows_ref)


def hidden_kernel(*refs, blocks):
    ins = refs[:blocks]
    perm_t_ref, down0_ref, down1_ref, out_ref, rows_ref = refs[blocks:]
    piece = ins[0].shape[1]
    chunks = ins[0].shape[0] // CHUNK
    perm_t = perm_t_ref[...]
    for b, block in enumerate(ins):
        from_wire(block, rows_ref, b * chunks * ROWS, perm_t, chunks, piece)
    part = down0_ref.shape[0]
    for i, w_ref in enumerate((down0_ref, down1_ref)):
        out_ref[:, i * part : (i + 1) * part] = dot_nt(rows_ref[...], w_ref[...])


def expert_kernel(*refs, blocks):
    ins = refs[:blocks]
    hg_ref, perm_ref, perm_t_ref = refs[blocks : blocks + 3]
    gate_ref, up_ref, gate_hbm, up_hbm = refs[blocks + 3 : blocks + 7]
    outs = refs[blocks + 7 : 2 * blocks + 7]
    rows_ref, act_ref, total_ref, w_ref, sems = refs[2 * blocks + 7 :]
    copies = [
        pltpu.make_async_copy(src, w_ref.at[i], sems.at[i])
        for i, src in enumerate((gate_hbm, up_hbm))
    ]
    for copy in copies:
        copy.start()
    weights = (gate_ref, up_ref, w_ref.at[0], w_ref.at[1])
    piece = ins[0].shape[1]
    chunks = ins[0].shape[0] // CHUNK
    perm_t = perm_t_ref[...]
    for b, block in enumerate(ins):
        from_wire(block, rows_ref, b * chunks * ROWS, perm_t, chunks, piece)
    width, part = weights[0].shape
    for i in range(2):
        if i == 1:
            for copy in copies:
                copy.wait()
        gate_proj = dot(rows_ref[...], weights[2 * i][...])
        up_proj = dot(rows_ref[...], weights[2 * i + 1][...])
        hidden = hg_ref[:, i * part : (i + 1) * part]
        sig = jax.nn.sigmoid(gate_proj)
        act_ref[2 * i + 1] = (hidden * gate_proj * sig).astype(BF16)
        act_ref[2 * i] = (hidden * up_proj * sig * (1.0 + gate_proj * (1.0 - sig))).astype(BF16)
    for n in range(width // 512):
        cols = slice(n * 512, (n + 1) * 512)
        total = dot_nt(act_ref[0], weights[0][cols, :])
        for i in range(1, 4):
            total = total + dot_nt(act_ref[i], weights[i][cols, :])
        total_ref[:, cols] = total
    perm = perm_ref[...]
    for b, dst in enumerate(outs):
        for chunk in range(chunks):
            block = to_wire(total_ref, b * chunks * ROWS, perm, chunk, piece)
            dst[chunk * CHUNK : (chunk + 1) * CHUNK, :] = block


def backward_kernel(
    seq_ref, offs_ref, ids_ref, gates_ref, home_ref, grad_ref, unit_ref, inv_ref, gain_ref,
    perm_t_ref, q_ref, vl_ref, v_ref, vr_ref, wts_ref, k_out_ref, v_out_ref, to_left_ref,
    to_right_ref, vx_ref, rows_ref, ag_ref, ka_ref, va_ref, total_tiles,
):
    fill_halo(vx_ref, vl_ref, v_ref, vr_ref)
    count, width = q_ref.shape
    heads = width // HEAD_DIM
    tiles = count // TILE
    scale = HEAD_DIM ** (-0.5)
    ka_ref[...] = jnp.zeros_like(ka_ref)
    va_ref[...] = jnp.zeros_like(va_ref)
    columns, _, _, piece = home_ref.shape
    chunks = columns // GROUP
    perm_t = perm_t_ref[...]
    for rel in range(2):
        blocks = [
            home_ref[c * GROUP : (c + 1) * GROUP, rel].reshape(CHUNK, piece) for c in range(chunks)
        ]
        from_wire(blocks, rows_ref, rel * chunks * ROWS, perm_t, chunks, piece)
    slot0, slot1 = slot_rows(ids_ref, seq_ref[0] // 4, 2 * columns)
    places = lax.broadcasted_iota(jnp.int32, (rows_ref.shape[0], count), 0)
    mix = jnp.where(places == slot0, gates_ref[0:1, :], 0.0)
    mix = jnp.where(places == slot1, gates_ref[1:2, :], mix)
    high = mix.astype(BF16)
    low = (mix - high.astype(F32)).astype(BF16)
    normed_grad = dot_tn(high, rows_ref[...]) + dot_tn(low, rows_ref[...])
    scaled = normed_grad * gain_ref[...]
    unit = unit_ref[...]
    inner = jnp.mean(scaled * unit, axis=-1, keepdims=True)
    attn_grad = grad_ref[...].astype(F32) + inv_ref[:, 0:1] * (scaled - unit * inner)
    ag_ref[...] = attn_grad.astype(BF16)
    spots = [tile_places(seq_ref, offs_ref, t, tiles, total_tiles)[0] for t in range(tiles)]
    def body(step, carry):
        spans = head_spans(step, heads, tiles)
        prob_grads = [
            dot_nt(ag_ref[rows, lanes], window(vx_ref, spots[t], lanes))
            for t, h, rows, lanes in spans
        ]
        values = [
            dot_tn(wts_ref[t * heads + h].astype(BF16), ag_ref[rows, lanes])
            for t, h, rows, lanes in spans
        ]
        sums = [
            jnp.sum(wts_ref[t * heads + h] * x, axis=-1, keepdims=True)
            for x, (t, h, rows, lanes) in zip(prob_grads, spans)
        ]
        score_grads = [
            (wts_ref[t * heads + h] * (x - total)).astype(BF16)
            for x, total, (t, h, rows, lanes) in zip(prob_grads, sums, spans)
        ]
        keys = [
            dot_tn(x, q_ref[rows, lanes]) * scale
            for x, (t, h, rows, lanes) in zip(score_grads, spans)
        ]
        for acc_ref, parts in ((va_ref, values), (ka_ref, keys)):
            for x, (t, h, rows, lanes) in zip(parts, spans):
                for m in range(NBR):
                    acc_ref[pl.ds(spots[t][m], TILE), lanes] += x[m * TILE : (m + 1) * TILE]
        return carry

    lax.fori_loop(0, heads // UNROLL, body, 0)
    k_out_ref[...] = ka_ref[count : 2 * count, :]
    v_out_ref[...] = va_ref[count : 2 * count, :]
    to_left_ref[0] = ka_ref[0:count, :].astype(BF16)
    to_left_ref[1] = va_ref[0:count, :].astype(BF16)
    to_right_ref[0] = ka_ref[2 * count : 3 * count, :].astype(BF16)
    to_right_ref[1] = va_ref[2 * count : 3 * count, :].astype(BF16)


def call(body, outs, kinds, scratch, name, flops, megabytes):
    spaces = {"s": pltpu.SMEM, "v": pltpu.VMEM, "a": pl.ANY}
    return pl.pallas_call(
        body,
        out_shape=outs,
        in_specs=[pl.BlockSpec(memory_space=spaces[kind]) for kind in kinds],
        out_specs=[pl.BlockSpec(memory_space=pltpu.VMEM) for _ in outs],
        scratch_shapes=scratch,
        compiler_params=pltpu.CompilerParams(vmem_limit_bytes=megabytes << 20),
        cost_estimate=pl.CostEstimate(flops=flops, transcendentals=0, bytes_accessed=1 << 20),
        name=name,
    )


def shape(dims, kind):
    return jax.ShapeDtypeStruct(dims, kind)


def on_device(
    queries, keys, values, out_grad, norm_gain, gate_values, expert_ids, tile_offsets, gate_weight,
    up_weight, down_weight,
):
    count, width = queries.shape[1:]
    heads = width // HEAD_DIM
    tiles = count // TILE
    seq_count = lax.axis_size("seq")
    columns = lax.axis_size("exp")
    total_tiles = tiles * seq_count
    piece = width // PIECES
    slots = columns * CAP
    seq = lax.axis_index("seq").astype(jnp.int32).reshape(1)
    ids_t = expert_ids[0].T
    gates_t = gate_values[0].T
    offsets = tile_offsets[0]
    gain = norm_gain.reshape(1, width)
    perm = jnp.asarray(shuffle_matrix(), BF16)
    perm_t = jnp.asarray(shuffle_matrix().T, BF16)
    q, k, v, grad = queries[0], keys[0], values[0], out_grad[0]
    gate, up, down = gate_weight[0, 0], up_weight[0, 0], down_weight[0, 0]
    wire = (columns, 2, CELL, piece)
    flat = (columns * CELL, piece)

    up_by = [(i, i + 1) for i in range(seq_count - 1)]
    down_by = [(i + 1, i) for i in range(seq_count - 1)]

    def swap(x, bits):
        return lax.ppermute(x, "seq", [(i, i ^ bits) for i in range(seq_count)])

    def exchange(x):
        return lax.all_to_all(x, "exp", split_axis=0, concat_axis=0, tiled=True)

    barrier = lax.optimization_barrier
    pair = (2, count, width)
    (sent_grad,) = call(
        grad_kernel, (shape(wire, BF16),), "svvv", [pltpu.VMEM((2 * slots, width), F32)],
        "place_grad", 4 * MICRO, 56,
    )(seq, ids_t, grad, perm)
    k, v, sent_grad = barrier((k, v, sent_grad))
    kl, kr = lax.ppermute(k, "seq", up_by), lax.ppermute(k, "seq", down_by)
    vl, vr = lax.ppermute(v, "seq", up_by), lax.ppermute(v, "seq", down_by)
    got_grad = exchange(sent_grad)


    wts, unit, inv, sent = call(
        lambda *refs: forward_kernel(*refs, total_tiles=total_tiles),
        (
            shape((tiles * heads, TILE, NBR * TILE), F32),
            shape((count, width), F32),
            shape((count, HEAD_DIM), F32),
            shape(wire, BF16),
        ),
        "ssv" + "v" * 9,
        [
            pltpu.VMEM((3 * count, width), BF16),
            pltpu.VMEM((3 * count, width), BF16),
            pltpu.VMEM((count, width), F32),
            pltpu.VMEM((2 * slots, width), F32),
        ],
        "attention", ATTN * MICRO, 20,
    )(seq, offsets, ids_t, q, kl, k, kr, vl, v, vr, gain, perm)

    sent, *weights = barrier((sent, gate, up, down))
    sent, got_grad = barrier((sent, got_grad))
    gate_s, up_s, down_s = [swap(x, 1) for x in weights]
    got = exchange(sent)
    g0, grad_oth = got_grad[:, 0].reshape(flat), got_grad[:, 1].reshape(flat)
    g1, g2 = swap(grad_oth, 6), swap(g0, 2)
    g3 = swap(grad_oth, 4)
    n0, oth = got[:, 0].reshape(flat), got[:, 1].reshape(flat)
    n1, n2 = swap(oth, 6), swap(n0, 2)
    n3 = swap(n1, 2)

    part = down.shape[0]

    def hidden(ins, micros):
        blocks = len(ins)
        (out,) = call(
            lambda *refs: hidden_kernel(*refs, blocks=blocks),
            (shape((blocks * slots, 2 * part), F32),),
            "v" * (blocks + 3),
            [pltpu.VMEM((blocks * slots, width), BF16)],
            "hidden", micros * MICRO, 14,
        )(*ins, perm_t, down, down_s)
        return out

    def expert(ins, hg, micros):
        blocks = len(ins)
        return call(
            lambda *refs: expert_kernel(*refs, blocks=blocks),
            (shape(flat, BF16),) * blocks,
            "v" * (blocks + 5) + "aa",
            [
                pltpu.VMEM((blocks * slots, width), BF16),
                pltpu.VMEM((4, blocks * slots, part), BF16),
                pltpu.VMEM((blocks * slots, width), F32),
                pltpu.VMEM((2, width, part), BF16),
                pltpu.SemaphoreType.DMA((2,)),
            ],
            "expert", micros * MICRO, 20,
        )(*ins, hg, perm, perm_t, gate, up, gate_s, up_s)

    hidden_own = hidden((g0,), 4)
    hidden_near = hidden((g1, g2), 5)
    (p0,) = expert((n0,), hidden_own, 9)
    p0, g3 = barrier((p0, g3))
    hidden_far = hidden((g3,), 4)
    hidden_far, n1, n2 = barrier((hidden_far, n1, n2))
    p1, p2 = expert((n1, n2), hidden_near, 11)
    (p3,) = expert((n3,), hidden_far, 9)
    h1, h2 = swap(p1, 6), swap(p2, 2)
    h3 = swap(p3, 4)
    own = (p0.astype(F32) + h2.astype(F32)).astype(BF16).reshape(columns, 1, CELL, piece)
    oth = (h1.astype(F32) + h3.astype(F32)).astype(BF16).reshape(columns, 1, CELL, piece)
    home = exchange(jnp.concatenate([own, oth], axis=1))

    k_own, v_own, to_left, to_right = call(
        lambda *refs: backward_kernel(*refs, total_tiles=total_tiles),
        (shape((count, width), F32), shape((count, width), F32), shape(pair, BF16), shape(pair, BF16)),
        "ss" + "v" * 13,
        [
            pltpu.VMEM((3 * count, width), BF16),
            pltpu.VMEM((2 * slots, width), BF16),
            pltpu.VMEM((count, width), BF16),
            pltpu.VMEM((3 * count, width), F32),
            pltpu.VMEM((3 * count, width), F32),
        ],
        "attention_grad", 10 * MICRO, 24,
    )(seq, offsets, ids_t, gates_t, home, grad, unit, inv, gain, perm_t, q, vl, v, vr, wts)
    from_right = lax.ppermute(to_left, "seq", down_by).astype(F32)
    from_left = lax.ppermute(to_right, "seq", up_by).astype(F32)

    def finish(own_part, i):
        return (own_part + from_right[i] + from_left[i]).astype(BF16)[None]

    return (finish(k_own, 0), finish(v_own, 1))


def solution(mesh):
    rows = P("exp", "seq", None)
    weights = P("exp", "seq", None, None)
    return jax.shard_map(
        on_device,
        mesh=mesh,
        in_specs=(rows, rows, rows, rows, P(), rows, rows, rows, weights, weights, weights),
        out_specs=(rows, rows),
        check_vma=False,
    )
```

```python
import jax
import jax.numpy as jnp
import numpy as np
from jax import lax
from jax.experimental import pallas as pl
from jax.experimental.pallas import tpu as pltpu
from jax.sharding import PartitionSpec as P

HEAD_DIM = 128
TILE = 64
NBR = 3
CAP = 5
PIECES = 8
GROUP = 8
EPSILON = 1e-06
ATTN = 8
UNROLL = 4
MICRO = 1 << 30
F32 = jnp.float32
BF16 = jnp.bfloat16

CELL = PIECES * CAP
CHUNK = GROUP * CELL
ROWS = GROUP * CAP


def shuffle_matrix():
    out = np.zeros((CHUNK, CHUNK), np.float32)
    for d in range(GROUP):
        for q in range(PIECES):
            for r in range(CAP):
                out[d * CELL + q * CAP + r, q * ROWS + d * CAP + r] = 1.0
    return out


def dot(a, b):
    return jnp.dot(a, b, preferred_element_type=F32)


def dot_nt(a, b):
    return lax.dot_general(a, b, (((1,), (1,)), ((), ())), preferred_element_type=F32)


def dot_tn(a, b):
    return lax.dot_general(a, b, (((0,), (0,)), ((), ())), preferred_element_type=F32)


def to_wire(rows_ref, base, perm, chunk, piece):
    start = base + chunk * ROWS
    stacked = jnp.concatenate(
        [rows_ref[start : start + ROWS, q * piece : (q + 1) * piece] for q in range(PIECES)], axis=0
    )
    return dot(perm, stacked.astype(BF16)).astype(BF16)


def from_wire(block_ref, rows_ref, base, perm_t, chunks, piece):
    if not isinstance(block_ref, list):
        block_ref = [block_ref[c * CHUNK : (c + 1) * CHUNK, :] for c in range(chunks)]
    for pair in range(chunks // 2):
        low = dot(perm_t, block_ref[2 * pair])
        high = dot(perm_t, block_ref[2 * pair + 1])
        start = base + 2 * pair * ROWS
        for q in range(PIECES):
            both = jnp.concatenate(
                [low[q * ROWS : (q + 1) * ROWS], high[q * ROWS : (q + 1) * ROWS]], axis=0
            )
            rows_ref[start : start + 2 * ROWS, q * piece : (q + 1) * piece] = both.astype(BF16)


def slot_rows(ids_ref, half, experts):
    tokens = ids_ref.shape[1]
    first = ids_ref[0:1, :]
    second = ids_ref[1:2, :]
    names = lax.broadcasted_iota(jnp.int32, (experts, tokens), 0)
    hot0 = (names == first).astype(F32)
    hot1 = (names == second).astype(F32)
    before = (
        lax.broadcasted_iota(jnp.int32, (tokens, tokens), 0)
        < lax.broadcasted_iota(jnp.int32, (tokens, tokens), 1)
    ).astype(F32).astype(BF16)
    seen0 = dot(hot0.astype(BF16), before)
    seen1 = dot(hot1.astype(BF16), before) + jnp.sum(hot0, axis=1, keepdims=True)
    rank0 = jnp.sum(hot0 * seen0, axis=0, keepdims=True).astype(jnp.int32)
    rank1 = jnp.sum(hot1 * seen1, axis=0, keepdims=True).astype(jnp.int32)
    slots = (experts // 2) * CAP
    slot0 = ((first & 1) ^ half) * slots + (first >> 1) * CAP + rank0
    slot1 = ((second & 1) ^ half) * slots + (second >> 1) * CAP + rank1
    return slot0, slot1


def place_rows(ids_ref, half, experts, x, rows_ref):
    slot0, slot1 = slot_rows(ids_ref, half, experts)
    places = lax.broadcasted_iota(jnp.int32, (rows_ref.shape[0], x.shape[0]), 0)
    hot = ((places == slot0) | (places == slot1)).astype(F32).astype(BF16)
    rows_ref[...] = dot(hot, x)


def send_rows(seq_ref, ids_ref, x, perm_ref, out_ref, rows_ref):
    columns = out_ref.shape[0]
    piece = out_ref.shape[3]
    place_rows(ids_ref, seq_ref[0] // 4, 2 * columns, x, rows_ref)
    perm = perm_ref[...]
    for rel in range(2):
        for chunk in range(columns // GROUP):
            block = to_wire(rows_ref, rel * columns * CAP, perm, chunk, piece)
            out_ref[chunk * GROUP : (chunk + 1) * GROUP, rel] = block.reshape(GROUP, CELL, piece)


def grad_kernel(seq_ref, ids_ref, x_ref, perm_ref, out_ref, rows_ref):
    send_rows(seq_ref, ids_ref, x_ref[...], perm_ref, out_ref, rows_ref)


def tile_places(seq_ref, offs_ref, tile, tiles, total):
    places = []
    valid = []
    for m in range(NBR):
        off = offs_ref[tile, m]
        places.append(pl.multiple_of((tile + 2 + off) * TILE, TILE))
        where = seq_ref[0] * tiles + tile + off
        valid.append((where >= 0) & (where < total))
    return places, valid


def head_spans(step, heads, tiles):
    spans = []
    for u in range(UNROLL):
        h = step * UNROLL + u
        lanes = pl.ds(pl.multiple_of(h * HEAD_DIM, HEAD_DIM), HEAD_DIM)
        spans += [(t, h, slice(t * TILE, (t + 1) * TILE), lanes) for t in range(tiles)]
    return spans


def window(ref, places, lanes):
    return jnp.concatenate([ref[pl.ds(p, TILE), lanes] for p in places], axis=0)


def fill_halo(dst_ref, left_ref, own_ref, right_ref):
    count = own_ref.shape[0]
    for i, src in enumerate((left_ref, own_ref, right_ref)):
        dst_ref[i * count : (i + 1) * count, :] = src[...]


def forward_kernel(
    seq_ref, offs_ref, ids_ref, q_ref, kl_ref, k_ref, kr_ref, vl_ref, v_ref, vr_ref, gain_ref,
    perm_ref, wts_ref, unit_ref, inv_ref, sent_ref, kx_ref, vx_ref, out_ref, rows_ref, total_tiles,
):
    fill_halo(kx_ref, kl_ref, k_ref, kr_ref)
    fill_halo(vx_ref, vl_ref, v_ref, vr_ref)
    count, width = q_ref.shape
    heads = width // HEAD_DIM
    tiles = count // TILE
    scale = HEAD_DIM ** (-0.5)
    lane = lax.broadcasted_iota(jnp.int32, (TILE, NBR * TILE), 1) // TILE
    spots = []
    biases = []
    for t in range(tiles):
        places, valid = tile_places(seq_ref, offs_ref, t, tiles, total_tiles)
        bias = jnp.zeros((TILE, NBR * TILE), F32)
        for m in range(NBR):
            lost = jnp.where(valid[m], 0.0, -jnp.inf).astype(F32)
            bias = jnp.where(lane == m, lost, bias)
        spots.append(places)
        biases.append(bias)

    def body(step, carry):
        spans = head_spans(step, heads, tiles)
        scores = [
            dot_nt(q_ref[rows, lanes], window(kx_ref, spots[t], lanes)) * scale + biases[t]
            for t, h, rows, lanes in spans
        ]
        tops = [jnp.max(x, axis=-1, keepdims=True) for x in scores]
        raised = [jnp.exp(x - top) for x, top in zip(scores, tops)]
        sums = [jnp.sum(x, axis=-1, keepdims=True) for x in raised]
        weights = [x / total for x, total in zip(raised, sums)]
        for x, (t, h, rows, lanes) in zip(weights, spans):
            wts_ref[t * heads + h] = x
            out_ref[rows, lanes] = dot(x.astype(BF16), window(vx_ref, spots[t], lanes))
        return carry

    lax.fori_loop(0, heads // UNROLL, body, 0)
    out = out_ref[...]
    inv = lax.rsqrt(jnp.mean(out * out, axis=-1, keepdims=True) + EPSILON)
    unit = out * inv
    unit_ref[...] = unit
    inv_ref[...] = jnp.broadcast_to(inv, inv_ref.shape)
    normed = (unit * gain_ref[...]).astype(BF16)
    send_rows(seq_ref, ids_ref, normed, perm_ref, sent_ref, rows_ref)


def hidden_kernel(*refs, blocks):
    ins = refs[:blocks]
    perm_t_ref, down0_ref, down1_ref, out_ref, rows_ref = refs[blocks:]
    piece = ins[0].shape[1]
    chunks = ins[0].shape[0] // CHUNK
    perm_t = perm_t_ref[...]
    for b, block in enumerate(ins):
        from_wire(block, rows_ref, b * chunks * ROWS, perm_t, chunks, piece)
    part = down0_ref.shape[0]
    for i, w_ref in enumerate((down0_ref, down1_ref)):
        out_ref[:, i * part : (i + 1) * part] = dot_nt(rows_ref[...], w_ref[...])


def expert_kernel(*refs, blocks):
    ins = refs[:blocks]
    hg_ref, perm_ref, perm_t_ref = refs[blocks : blocks + 3]
    gate_ref, up_ref, gate_hbm, up_hbm = refs[blocks + 3 : blocks + 7]
    outs = refs[blocks + 7 : 2 * blocks + 7]
    rows_ref, act_ref, total_ref, w_ref, sems = refs[2 * blocks + 7 :]
    copies = [
        pltpu.make_async_copy(src, w_ref.at[i], sems.at[i])
        for i, src in enumerate((gate_hbm, up_hbm))
    ]
    for copy in copies:
        copy.start()
    weights = (gate_ref, up_ref, w_ref.at[0], w_ref.at[1])
    piece = ins[0].shape[1]
    chunks = ins[0].shape[0] // CHUNK
    perm_t = perm_t_ref[...]
    for b, block in enumerate(ins):
        from_wire(block, rows_ref, b * chunks * ROWS, perm_t, chunks, piece)
    width, part = weights[0].shape
    for i in range(2):
        if i == 1:
            for copy in copies:
                copy.wait()
        gate_proj = dot(rows_ref[...], weights[2 * i][...])
        up_proj = dot(rows_ref[...], weights[2 * i + 1][...])
        hidden = hg_ref[:, i * part : (i + 1) * part]
        sig = jax.nn.sigmoid(gate_proj)
        act_ref[2 * i + 1] = (hidden * gate_proj * sig).astype(BF16)
        act_ref[2 * i] = (hidden * up_proj * sig * (1.0 + gate_proj * (1.0 - sig))).astype(BF16)
    for n in range(width // 512):
        cols = slice(n * 512, (n + 1) * 512)
        total = dot_nt(act_ref[0], weights[0][cols, :])
        for i in range(1, 4):
            total = total + dot_nt(act_ref[i], weights[i][cols, :])
        total_ref[:, cols] = total
    perm = perm_ref[...]
    for b, dst in enumerate(outs):
        for chunk in range(chunks):
            block = to_wire(total_ref, b * chunks * ROWS, perm, chunk, piece)
            dst[chunk * CHUNK : (chunk + 1) * CHUNK, :] = block


def backward_kernel(
    seq_ref, offs_ref, ids_ref, gates_ref, home_ref, grad_ref, unit_ref, inv_ref, gain_ref,
    perm_t_ref, q_hbm, vl_ref, v_ref, vr_ref, wts_hbm, k_out_ref, v_out_ref, to_left_ref,
    to_right_ref, vx_ref, rows_ref, ag_ref, ka_ref, va_ref, q_ref, wts_ref, sems, total_tiles,
):
    span = v_ref.shape[0]
    pairs = [(src, vx_ref.at[i * span : (i + 1) * span]) for i, src in enumerate((vl_ref, v_ref, vr_ref))]
    pairs += [(q_hbm, q_ref), (wts_hbm, wts_ref)]
    copies = [pltpu.make_async_copy(src, dst, sems.at[i]) for i, (src, dst) in enumerate(pairs)]
    for copy in copies:
        copy.start()
    count, width = q_ref.shape
    heads = width // HEAD_DIM
    tiles = count // TILE
    scale = HEAD_DIM ** (-0.5)
    ka_ref[...] = jnp.zeros_like(ka_ref)
    va_ref[...] = jnp.zeros_like(va_ref)
    columns, _, _, piece = home_ref.shape
    chunks = columns // GROUP
    perm_t = perm_t_ref[...]
    for rel in range(2):
        blocks = [
            home_ref[c * GROUP : (c + 1) * GROUP, rel].reshape(CHUNK, piece) for c in range(chunks)
        ]
        from_wire(blocks, rows_ref, rel * chunks * ROWS, perm_t, chunks, piece)
    slot0, slot1 = slot_rows(ids_ref, seq_ref[0] // 4, 2 * columns)
    places = lax.broadcasted_iota(jnp.int32, (rows_ref.shape[0], count), 0)
    mix = jnp.where(places == slot0, gates_ref[0:1, :], 0.0)
    mix = jnp.where(places == slot1, gates_ref[1:2, :], mix)
    high = mix.astype(BF16)
    low = (mix - high.astype(F32)).astype(BF16)
    normed_grad = dot_tn(high, rows_ref[...]) + dot_tn(low, rows_ref[...])
    scaled = normed_grad * gain_ref[...]
    unit = unit_ref[...]
    inner = jnp.mean(scaled * unit, axis=-1, keepdims=True)
    attn_grad = grad_ref[...].astype(F32) + inv_ref[:, 0:1] * (scaled - unit * inner)
    ag_ref[...] = attn_grad.astype(BF16)
    spots = [tile_places(seq_ref, offs_ref, t, tiles, total_tiles)[0] for t in range(tiles)]
    for copy in copies:
        copy.wait()

    def body(step, carry):
        spans = head_spans(step, heads, tiles)
        prob_grads = [
            dot_nt(ag_ref[rows, lanes], window(vx_ref, spots[t], lanes))
            for t, h, rows, lanes in spans
        ]
        values = [
            dot_tn(wts_ref[t * heads + h].astype(BF16), ag_ref[rows, lanes])
            for t, h, rows, lanes in spans
        ]
        sums = [
            jnp.sum(wts_ref[t * heads + h] * x, axis=-1, keepdims=True)
            for x, (t, h, rows, lanes) in zip(prob_grads, spans)
        ]
        score_grads = [
            (wts_ref[t * heads + h] * (x - total)).astype(BF16)
            for x, total, (t, h, rows, lanes) in zip(prob_grads, sums, spans)
        ]
        keys = [
            dot_tn(x, q_ref[rows, lanes]) * scale
            for x, (t, h, rows, lanes) in zip(score_grads, spans)
        ]
        for acc_ref, parts in ((va_ref, values), (ka_ref, keys)):
            for x, (t, h, rows, lanes) in zip(parts, spans):
                for m in range(NBR):
                    acc_ref[pl.ds(spots[t][m], TILE), lanes] += x[m * TILE : (m + 1) * TILE]
        return carry

    lax.fori_loop(0, heads // UNROLL, body, 0)
    k_out_ref[...] = ka_ref[count : 2 * count, :]
    v_out_ref[...] = va_ref[count : 2 * count, :]
    to_left_ref[0] = ka_ref[0:count, :].astype(BF16)
    to_left_ref[1] = va_ref[0:count, :].astype(BF16)
    to_right_ref[0] = ka_ref[2 * count : 3 * count, :].astype(BF16)
    to_right_ref[1] = va_ref[2 * count : 3 * count, :].astype(BF16)


def call(body, outs, kinds, scratch, name, flops, megabytes):
    spaces = {"s": pltpu.SMEM, "v": pltpu.VMEM, "a": pl.ANY}
    return pl.pallas_call(
        body,
        out_shape=outs,
        in_specs=[pl.BlockSpec(memory_space=spaces[kind]) for kind in kinds],
        out_specs=[pl.BlockSpec(memory_space=pltpu.VMEM) for _ in outs],
        scratch_shapes=scratch,
        compiler_params=pltpu.CompilerParams(vmem_limit_bytes=megabytes << 20),
        cost_estimate=pl.CostEstimate(flops=flops, transcendentals=0, bytes_accessed=1 << 20),
        name=name,
    )


def shape(dims, kind):
    return jax.ShapeDtypeStruct(dims, kind)


def on_device(
    queries, keys, values, out_grad, norm_gain, gate_values, expert_ids, tile_offsets, gate_weight,
    up_weight, down_weight,
):
    count, width = queries.shape[1:]
    heads = width // HEAD_DIM
    tiles = count // TILE
    seq_count = lax.axis_size("seq")
    columns = lax.axis_size("exp")
    total_tiles = tiles * seq_count
    piece = width // PIECES
    slots = columns * CAP
    seq = lax.axis_index("seq").astype(jnp.int32).reshape(1)
    ids_t = expert_ids[0].T
    gates_t = gate_values[0].T
    offsets = tile_offsets[0]
    gain = norm_gain.reshape(1, width)
    perm = jnp.asarray(shuffle_matrix(), BF16)
    perm_t = jnp.asarray(shuffle_matrix().T, BF16)
    q, k, v, grad = queries[0], keys[0], values[0], out_grad[0]
    gate, up, down = gate_weight[0, 0], up_weight[0, 0], down_weight[0, 0]
    wire = (columns, 2, CELL, piece)
    flat = (columns * CELL, piece)

    up_by = [(i, i + 1) for i in range(seq_count - 1)]
    down_by = [(i + 1, i) for i in range(seq_count - 1)]

    def swap(x, bits):
        return lax.ppermute(x, "seq", [(i, i ^ bits) for i in range(seq_count)])

    def exchange(x):
        return lax.all_to_all(x, "exp", split_axis=0, concat_axis=0, tiled=True)

    barrier = lax.optimization_barrier
    pair = (2, count, width)
    (sent_grad,) = call(
        grad_kernel, (shape(wire, BF16),), "svvv", [pltpu.VMEM((2 * slots, width), F32)],
        "place_grad", 4 * MICRO, 56,
    )(seq, ids_t, grad, perm)
    k, v, sent_grad = barrier((k, v, sent_grad))
    kl, kr = lax.ppermute(k, "seq", up_by), lax.ppermute(k, "seq", down_by)
    vl, vr = lax.ppermute(v, "seq", up_by), lax.ppermute(v, "seq", down_by)
    got_grad = exchange(sent_grad)


    wts, unit, inv, sent = call(
        lambda *refs: forward_kernel(*refs, total_tiles=total_tiles),
        (
            shape((tiles * heads, TILE, NBR * TILE), F32),
            shape((count, width), F32),
            shape((count, HEAD_DIM), F32),
            shape(wire, BF16),
        ),
        "ssv" + "v" * 9,
        [
            pltpu.VMEM((3 * count, width), BF16),
            pltpu.VMEM((3 * count, width), BF16),
            pltpu.VMEM((count, width), F32),
            pltpu.VMEM((2 * slots, width), F32),
        ],
        "attention", ATTN * MICRO, 20,
    )(seq, offsets, ids_t, q, kl, k, kr, vl, v, vr, gain, perm)

    sent, *weights = barrier((sent, gate, up, down))
    sent, got_grad = barrier((sent, got_grad))
    gate_s, up_s, down_s = [swap(x, 1) for x in weights]
    got = exchange(sent)
    g0, grad_oth = got_grad[:, 0].reshape(flat), got_grad[:, 1].reshape(flat)
    g1, g2 = swap(grad_oth, 6), swap(g0, 2)
    g3 = swap(grad_oth, 4)
    n0, oth = got[:, 0].reshape(flat), got[:, 1].reshape(flat)
    n1, n2 = swap(oth, 6), swap(n0, 2)
    n3 = swap(n1, 2)

    part = down.shape[0]

    def hidden(ins, micros):
        blocks = len(ins)
        (out,) = call(
            lambda *refs: hidden_kernel(*refs, blocks=blocks),
            (shape((blocks * slots, 2 * part), F32),),
            "v" * (blocks + 3),
            [pltpu.VMEM((blocks * slots, width), BF16)],
            "hidden", micros * MICRO, 14,
        )(*ins, perm_t, down, down_s)
        return out

    def expert(ins, hg, micros):
        blocks = len(ins)
        return call(
            lambda *refs: expert_kernel(*refs, blocks=blocks),
            (shape(flat, BF16),) * blocks,
            "v" * (blocks + 5) + "aa",
            [
                pltpu.VMEM((blocks * slots, width), BF16),
                pltpu.VMEM((4, blocks * slots, part), BF16),
                pltpu.VMEM((blocks * slots, width), F32),
                pltpu.VMEM((2, width, part), BF16),
                pltpu.SemaphoreType.DMA((2,)),
            ],
            "expert", micros * MICRO, 20,
        )(*ins, hg, perm, perm_t, gate, up, gate_s, up_s)

    hidden_own = hidden((g0,), 4)
    hidden_near = hidden((g1, g2), 5)
    (p0,) = expert((n0,), hidden_own, 9)
    p0, g3 = barrier((p0, g3))
    hidden_far = hidden((g3,), 4)
    hidden_far, n1, n2 = barrier((hidden_far, n1, n2))
    p1, p2 = expert((n1, n2), hidden_near, 11)
    (p3,) = expert((n3,), hidden_far, 9)
    h1, h2 = swap(p1, 6), swap(p2, 2)
    h3 = swap(p3, 4)
    own = (p0.astype(F32) + h2.astype(F32)).astype(BF16).reshape(columns, 1, CELL, piece)
    oth = (h1.astype(F32) + h3.astype(F32)).astype(BF16).reshape(columns, 1, CELL, piece)
    home = exchange(jnp.concatenate([own, oth], axis=1))

    k_own, v_own, to_left, to_right = call(
        lambda *refs: backward_kernel(*refs, total_tiles=total_tiles),
        (shape((count, width), F32), shape((count, width), F32), shape(pair, BF16), shape(pair, BF16)),
        "ss" + "v" * 8 + "aaaaa",
        [
            pltpu.VMEM((3 * count, width), BF16),
            pltpu.VMEM((2 * slots, width), BF16),
            pltpu.VMEM((count, width), BF16),
            pltpu.VMEM((3 * count, width), F32),
            pltpu.VMEM((3 * count, width), F32),
            pltpu.VMEM((count, width), BF16),
            pltpu.VMEM(wts.shape, F32),
            pltpu.SemaphoreType.DMA((5,)),
        ],
        "attention_grad", 10 * MICRO, 56,
    )(seq, offsets, ids_t, gates_t, home, grad, unit, inv, gain, perm_t, q, vl, v, vr, wts)
    from_right = lax.ppermute(to_left, "seq", down_by).astype(F32)
    from_left = lax.ppermute(to_right, "seq", up_by).astype(F32)

    def finish(own_part, i):
        return (own_part + from_right[i] + from_left[i]).astype(BF16)[None]

    return (finish(k_own, 0), finish(v_own, 1))


def solution(mesh):
    rows = P("exp", "seq", None)
    weights = P("exp", "seq", None, None)
    return jax.shard_map(
        on_device,
        mesh=mesh,
        in_specs=(rows, rows, rows, rows, P(), rows, rows, rows, weights, weights, weights),
        out_specs=(rows, rows),
        check_vma=False,
    )
```

```python
import jax
import jax.numpy as jnp
import numpy as np
from jax import lax
from jax.experimental import pallas as pl
from jax.experimental.pallas import tpu as pltpu
from jax.sharding import PartitionSpec as P

HEAD_DIM = 128
TILE = 64
NBR = 3
CAP = 5
PIECES = 8
GROUP = 8
EPSILON = 1e-06
ATTN = 8
UNROLL = 4
MICRO = 1 << 30
F32 = jnp.float32
BF16 = jnp.bfloat16

CELL = PIECES * CAP
CHUNK = GROUP * CELL
ROWS = GROUP * CAP


def shuffle_matrix():
    out = np.zeros((CHUNK, CHUNK), np.float32)
    for d in range(GROUP):
        for q in range(PIECES):
            for r in range(CAP):
                out[d * CELL + q * CAP + r, q * ROWS + d * CAP + r] = 1.0
    return out


def dot(a, b):
    return jnp.dot(a, b, preferred_element_type=F32)


def dot_nt(a, b):
    return lax.dot_general(a, b, (((1,), (1,)), ((), ())), preferred_element_type=F32)


def dot_tn(a, b):
    return lax.dot_general(a, b, (((0,), (0,)), ((), ())), preferred_element_type=F32)


def to_wire(rows_ref, base, perm, chunk, piece):
    start = base + chunk * ROWS
    stacked = jnp.concatenate(
        [rows_ref[start : start + ROWS, q * piece : (q + 1) * piece] for q in range(PIECES)], axis=0
    )
    return dot(perm, stacked.astype(BF16)).astype(BF16)


def from_wire(block_ref, rows_ref, base, perm_t, chunks, piece):
    if not isinstance(block_ref, list):
        block_ref = [block_ref[c * CHUNK : (c + 1) * CHUNK, :] for c in range(chunks)]
    for pair in range(chunks // 2):
        low = dot(perm_t, block_ref[2 * pair])
        high = dot(perm_t, block_ref[2 * pair + 1])
        start = base + 2 * pair * ROWS
        for q in range(PIECES):
            both = jnp.concatenate(
                [low[q * ROWS : (q + 1) * ROWS], high[q * ROWS : (q + 1) * ROWS]], axis=0
            )
            rows_ref[start : start + 2 * ROWS, q * piece : (q + 1) * piece] = both.astype(BF16)


def slot_rows(ids_ref, half, experts):
    tokens = ids_ref.shape[1]
    first = ids_ref[0:1, :]
    second = ids_ref[1:2, :]
    names = lax.broadcasted_iota(jnp.int32, (experts, tokens), 0)
    hot0 = (names == first).astype(F32)
    hot1 = (names == second).astype(F32)
    before = (
        lax.broadcasted_iota(jnp.int32, (tokens, tokens), 0)
        < lax.broadcasted_iota(jnp.int32, (tokens, tokens), 1)
    ).astype(F32).astype(BF16)
    seen0 = dot(hot0.astype(BF16), before)
    seen1 = dot(hot1.astype(BF16), before) + jnp.sum(hot0, axis=1, keepdims=True)
    rank0 = jnp.sum(hot0 * seen0, axis=0, keepdims=True).astype(jnp.int32)
    rank1 = jnp.sum(hot1 * seen1, axis=0, keepdims=True).astype(jnp.int32)
    slots = (experts // 2) * CAP
    slot0 = ((first & 1) ^ half) * slots + (first >> 1) * CAP + rank0
    slot1 = ((second & 1) ^ half) * slots + (second >> 1) * CAP + rank1
    return slot0, slot1


def place_rows(ids_ref, half, experts, x, rows_ref):
    slot0, slot1 = slot_rows(ids_ref, half, experts)
    places = lax.broadcasted_iota(jnp.int32, (rows_ref.shape[0], x.shape[0]), 0)
    hot = ((places == slot0) | (places == slot1)).astype(F32).astype(BF16)
    rows_ref[...] = dot(hot, x)


def send_rows(seq_ref, ids_ref, x, perm_ref, out_ref, rows_ref):
    columns = out_ref.shape[0]
    piece = out_ref.shape[3]
    place_rows(ids_ref, seq_ref[0] // 4, 2 * columns, x, rows_ref)
    perm = perm_ref[...]
    for rel in range(2):
        for chunk in range(columns // GROUP):
            block = to_wire(rows_ref, rel * columns * CAP, perm, chunk, piece)
            out_ref[chunk * GROUP : (chunk + 1) * GROUP, rel] = block.reshape(GROUP, CELL, piece)


def grad_kernel(seq_ref, ids_ref, x_ref, perm_ref, out_ref, rows_ref):
    send_rows(seq_ref, ids_ref, x_ref[...], perm_ref, out_ref, rows_ref)


def tile_places(seq_ref, offs_ref, tile, tiles, total):
    places = []
    valid = []
    for m in range(NBR):
        off = offs_ref[tile, m]
        places.append(pl.multiple_of((tile + 2 + off) * TILE, TILE))
        where = seq_ref[0] * tiles + tile + off
        valid.append((where >= 0) & (where < total))
    return places, valid


def head_spans(step, heads, tiles):
    spans = []
    for u in range(UNROLL):
        h = step * UNROLL + u
        lanes = pl.ds(pl.multiple_of(h * HEAD_DIM, HEAD_DIM), HEAD_DIM)
        spans += [(t, h, slice(t * TILE, (t + 1) * TILE), lanes) for t in range(tiles)]
    return spans


def window(ref, places, lanes):
    return jnp.concatenate([ref[pl.ds(p, TILE), lanes] for p in places], axis=0)


def fill_halo(dst_ref, left_ref, own_ref, right_ref):
    count = own_ref.shape[0]
    for i, src in enumerate((left_ref, own_ref, right_ref)):
        dst_ref[i * count : (i + 1) * count, :] = src[...]


def forward_kernel(
    seq_ref, offs_ref, ids_ref, q_ref, kl_ref, k_ref, kr_ref, vl_ref, v_ref, vr_ref, gain_ref,
    perm_ref, wts_ref, unit_ref, inv_ref, sent_ref, kx_ref, vx_ref, out_ref, rows_ref, total_tiles,
):
    fill_halo(kx_ref, kl_ref, k_ref, kr_ref)
    fill_halo(vx_ref, vl_ref, v_ref, vr_ref)
    count, width = q_ref.shape
    heads = width // HEAD_DIM
    tiles = count // TILE
    scale = HEAD_DIM ** (-0.5)
    lane = lax.broadcasted_iota(jnp.int32, (TILE, NBR * TILE), 1) // TILE
    spots = []
    biases = []
    for t in range(tiles):
        places, valid = tile_places(seq_ref, offs_ref, t, tiles, total_tiles)
        bias = jnp.zeros((TILE, NBR * TILE), F32)
        for m in range(NBR):
            lost = jnp.where(valid[m], 0.0, -jnp.inf).astype(F32)
            bias = jnp.where(lane == m, lost, bias)
        spots.append(places)
        biases.append(bias)

    def body(step, carry):
        spans = head_spans(step, heads, tiles)
        scores = [
            dot_nt(q_ref[rows, lanes], window(kx_ref, spots[t], lanes)) * scale + biases[t]
            for t, h, rows, lanes in spans
        ]
        tops = [jnp.max(x, axis=-1, keepdims=True) for x in scores]
        raised = [jnp.exp(x - top) for x, top in zip(scores, tops)]
        sums = [jnp.sum(x, axis=-1, keepdims=True) for x in raised]
        weights = [x / total for x, total in zip(raised, sums)]
        for x, (t, h, rows, lanes) in zip(weights, spans):
            wts_ref[t * heads + h] = x
            out_ref[rows, lanes] = dot(x.astype(BF16), window(vx_ref, spots[t], lanes))
        return carry

    lax.fori_loop(0, heads // UNROLL, body, 0)
    out = out_ref[...]
    inv = lax.rsqrt(jnp.mean(out * out, axis=-1, keepdims=True) + EPSILON)
    unit = out * inv
    unit_ref[...] = unit
    inv_ref[...] = jnp.broadcast_to(inv, inv_ref.shape)
    normed = (unit * gain_ref[...]).astype(BF16)
    send_rows(seq_ref, ids_ref, normed, perm_ref, sent_ref, rows_ref)


def hidden_kernel(*refs, blocks):
    ins = refs[:blocks]
    perm_t_ref, down0_ref, down1_ref, out_ref, rows_ref = refs[blocks:]
    piece = ins[0].shape[1]
    chunks = ins[0].shape[0] // CHUNK
    perm_t = perm_t_ref[...]
    for b, block in enumerate(ins):
        from_wire(block, rows_ref, b * chunks * ROWS, perm_t, chunks, piece)
    part = down0_ref.shape[0]
    for i, w_ref in enumerate((down0_ref, down1_ref)):
        out_ref[:, i * part : (i + 1) * part] = dot_nt(rows_ref[...], w_ref[...])


def expert_kernel(*refs, blocks):
    ins = refs[:blocks]
    hg_ref, perm_ref, perm_t_ref = refs[blocks : blocks + 3]
    gate_ref, up_ref, gate_hbm, up_hbm = refs[blocks + 3 : blocks + 7]
    outs = refs[blocks + 7 : 2 * blocks + 7]
    rows_ref, act_ref, total_ref, w_ref, sems = refs[2 * blocks + 7 :]
    copies = [
        pltpu.make_async_copy(src, w_ref.at[i], sems.at[i])
        for i, src in enumerate((gate_hbm, up_hbm))
    ]
    for copy in copies:
        copy.start()
    weights = (gate_ref, up_ref, w_ref.at[0], w_ref.at[1])
    piece = ins[0].shape[1]
    chunks = ins[0].shape[0] // CHUNK
    perm_t = perm_t_ref[...]
    for b, block in enumerate(ins):
        from_wire(block, rows_ref, b * chunks * ROWS, perm_t, chunks, piece)
    width, part = weights[0].shape
    for i in range(2):
        if i == 1:
            for copy in copies:
                copy.wait()
        gate_proj = dot(rows_ref[...], weights[2 * i][...])
        up_proj = dot(rows_ref[...], weights[2 * i + 1][...])
        hidden = hg_ref[:, i * part : (i + 1) * part]
        sig = jax.nn.sigmoid(gate_proj)
        act_ref[2 * i + 1] = (hidden * gate_proj * sig).astype(BF16)
        act_ref[2 * i] = (hidden * up_proj * sig * (1.0 + gate_proj * (1.0 - sig))).astype(BF16)
    for n in range(width // 512):
        cols = slice(n * 512, (n + 1) * 512)
        total = dot_nt(act_ref[0], weights[0][cols, :])
        for i in range(1, 4):
            total = total + dot_nt(act_ref[i], weights[i][cols, :])
        total_ref[:, cols] = total
    perm = perm_ref[...]
    for b, dst in enumerate(outs):
        for chunk in range(chunks):
            block = to_wire(total_ref, b * chunks * ROWS, perm, chunk, piece)
            dst[chunk * CHUNK : (chunk + 1) * CHUNK, :] = block


def value_kernel(
    seq_ref, offs_ref, ids_ref, gates_ref, home_ref, grad_ref, unit_ref, inv_ref, gain_ref,
    perm_t_ref, wts_ref, v_out_ref, to_left_ref, to_right_ref, ag_ref, rows_ref, va_ref,
    total_tiles,
):
    count, width = grad_ref.shape
    heads = width // HEAD_DIM
    tiles = count // TILE
    va_ref[...] = jnp.zeros_like(va_ref)
    columns, _, _, piece = home_ref.shape
    chunks = columns // GROUP
    perm_t = perm_t_ref[...]
    for rel in range(2):
        blocks = [
            home_ref[c * GROUP : (c + 1) * GROUP, rel].reshape(CHUNK, piece) for c in range(chunks)
        ]
        from_wire(blocks, rows_ref, rel * chunks * ROWS, perm_t, chunks, piece)
    slot0, slot1 = slot_rows(ids_ref, seq_ref[0] // 4, 2 * columns)
    places = lax.broadcasted_iota(jnp.int32, (rows_ref.shape[0], count), 0)
    mix = jnp.where(places == slot0, gates_ref[0:1, :], 0.0)
    mix = jnp.where(places == slot1, gates_ref[1:2, :], mix)
    high = mix.astype(BF16)
    low = (mix - high.astype(F32)).astype(BF16)
    normed_grad = dot_tn(high, rows_ref[...]) + dot_tn(low, rows_ref[...])
    scaled = normed_grad * gain_ref[...]
    unit = unit_ref[...]
    inner = jnp.mean(scaled * unit, axis=-1, keepdims=True)
    attn_grad = grad_ref[...].astype(F32) + inv_ref[:, 0:1] * (scaled - unit * inner)
    ag_ref[...] = attn_grad.astype(BF16)
    spots = [tile_places(seq_ref, offs_ref, t, tiles, total_tiles)[0] for t in range(tiles)]
    def body(step, carry):
        spans = head_spans(step, heads, tiles)
        values = [
            dot_tn(wts_ref[t * heads + h].astype(BF16), ag_ref[rows, lanes])
            for t, h, rows, lanes in spans
        ]
        for acc_ref, parts in ((va_ref, values),):
            for x, (t, h, rows, lanes) in zip(parts, spans):
                for m in range(NBR):
                    acc_ref[pl.ds(spots[t][m], TILE), lanes] += x[m * TILE : (m + 1) * TILE]
        return carry

    lax.fori_loop(0, heads // UNROLL, body, 0)
    v_out_ref[...] = va_ref[count : 2 * count, :]
    to_left_ref[...] = va_ref[0:count, :].astype(BF16)
    to_right_ref[...] = va_ref[2 * count : 3 * count, :].astype(BF16)


def key_kernel(
    seq_ref, offs_ref, ag_ref, q_ref, vl_ref, v_ref, vr_ref, wts_ref, k_out_ref, to_left_ref,
    to_right_ref, vx_ref, ka_ref, total_tiles,
):
    fill_halo(vx_ref, vl_ref, v_ref, vr_ref)
    count, width = q_ref.shape
    heads = width // HEAD_DIM
    tiles = count // TILE
    scale = HEAD_DIM ** (-0.5)
    ka_ref[...] = jnp.zeros_like(ka_ref)
    spots = [tile_places(seq_ref, offs_ref, t, tiles, total_tiles)[0] for t in range(tiles)]

    def body(step, carry):
        spans = head_spans(step, heads, tiles)
        prob_grads = [
            dot_nt(ag_ref[rows, lanes], window(vx_ref, spots[t], lanes))
            for t, h, rows, lanes in spans
        ]
        sums = [
            jnp.sum(wts_ref[t * heads + h] * x, axis=-1, keepdims=True)
            for x, (t, h, rows, lanes) in zip(prob_grads, spans)
        ]
        score_grads = [
            (wts_ref[t * heads + h] * (x - total)).astype(BF16)
            for x, total, (t, h, rows, lanes) in zip(prob_grads, sums, spans)
        ]
        keys = [
            dot_tn(x, q_ref[rows, lanes]) * scale
            for x, (t, h, rows, lanes) in zip(score_grads, spans)
        ]
        for acc_ref, parts in ((ka_ref, keys),):
            for x, (t, h, rows, lanes) in zip(parts, spans):
                for m in range(NBR):
                    acc_ref[pl.ds(spots[t][m], TILE), lanes] += x[m * TILE : (m + 1) * TILE]
        return carry

    lax.fori_loop(0, heads // UNROLL, body, 0)
    k_out_ref[...] = ka_ref[count : 2 * count, :]
    to_left_ref[...] = ka_ref[0:count, :].astype(BF16)
    to_right_ref[...] = ka_ref[2 * count : 3 * count, :].astype(BF16)


def call(body, outs, kinds, scratch, name, flops, megabytes):
    spaces = {"s": pltpu.SMEM, "v": pltpu.VMEM, "a": pl.ANY}
    return pl.pallas_call(
        body,
        out_shape=outs,
        in_specs=[pl.BlockSpec(memory_space=spaces[kind]) for kind in kinds],
        out_specs=[pl.BlockSpec(memory_space=pltpu.VMEM) for _ in outs],
        scratch_shapes=scratch,
        compiler_params=pltpu.CompilerParams(vmem_limit_bytes=megabytes << 20),
        cost_estimate=pl.CostEstimate(flops=flops, transcendentals=0, bytes_accessed=1 << 20),
        name=name,
    )


def shape(dims, kind):
    return jax.ShapeDtypeStruct(dims, kind)


def on_device(
    queries, keys, values, out_grad, norm_gain, gate_values, expert_ids, tile_offsets, gate_weight,
    up_weight, down_weight,
):
    count, width = queries.shape[1:]
    heads = width // HEAD_DIM
    tiles = count // TILE
    seq_count = lax.axis_size("seq")
    columns = lax.axis_size("exp")
    total_tiles = tiles * seq_count
    piece = width // PIECES
    slots = columns * CAP
    seq = lax.axis_index("seq").astype(jnp.int32).reshape(1)
    ids_t = expert_ids[0].T
    gates_t = gate_values[0].T
    offsets = tile_offsets[0]
    gain = norm_gain.reshape(1, width)
    perm = jnp.asarray(shuffle_matrix(), BF16)
    perm_t = jnp.asarray(shuffle_matrix().T, BF16)
    q, k, v, grad = queries[0], keys[0], values[0], out_grad[0]
    gate, up, down = gate_weight[0, 0], up_weight[0, 0], down_weight[0, 0]
    wire = (columns, 2, CELL, piece)
    flat = (columns * CELL, piece)

    up_by = [(i, i + 1) for i in range(seq_count - 1)]
    down_by = [(i + 1, i) for i in range(seq_count - 1)]

    def swap(x, bits):
        return lax.ppermute(x, "seq", [(i, i ^ bits) for i in range(seq_count)])

    def exchange(x):
        return lax.all_to_all(x, "exp", split_axis=0, concat_axis=0, tiled=True)

    barrier = lax.optimization_barrier
    pair = (2, count, width)
    (sent_grad,) = call(
        grad_kernel, (shape(wire, BF16),), "svvv", [pltpu.VMEM((2 * slots, width), F32)],
        "place_grad", 4 * MICRO, 56,
    )(seq, ids_t, grad, perm)
    k, v, sent_grad = barrier((k, v, sent_grad))
    kl, kr = lax.ppermute(k, "seq", up_by), lax.ppermute(k, "seq", down_by)
    vl, vr = lax.ppermute(v, "seq", up_by), lax.ppermute(v, "seq", down_by)
    got_grad = exchange(sent_grad)


    wts, unit, inv, sent = call(
        lambda *refs: forward_kernel(*refs, total_tiles=total_tiles),
        (
            shape((tiles * heads, TILE, NBR * TILE), F32),
            shape((count, width), F32),
            shape((count, HEAD_DIM), F32),
            shape(wire, BF16),
        ),
        "ssv" + "v" * 9,
        [
            pltpu.VMEM((3 * count, width), BF16),
            pltpu.VMEM((3 * count, width), BF16),
            pltpu.VMEM((count, width), F32),
            pltpu.VMEM((2 * slots, width), F32),
        ],
        "attention", ATTN * MICRO, 20,
    )(seq, offsets, ids_t, q, kl, k, kr, vl, v, vr, gain, perm)

    sent, *weights = barrier((sent, gate, up, down))
    sent, got_grad = barrier((sent, got_grad))
    gate_s, up_s, down_s = [swap(x, 1) for x in weights]
    got = exchange(sent)
    g0, grad_oth = got_grad[:, 0].reshape(flat), got_grad[:, 1].reshape(flat)
    g1, g2 = swap(grad_oth, 6), swap(g0, 2)
    g3 = swap(grad_oth, 4)
    n0, oth = got[:, 0].reshape(flat), got[:, 1].reshape(flat)
    n1, n2 = swap(oth, 6), swap(n0, 2)
    n3 = swap(n1, 2)

    part = down.shape[0]

    def hidden(ins, micros):
        blocks = len(ins)
        (out,) = call(
            lambda *refs: hidden_kernel(*refs, blocks=blocks),
            (shape((blocks * slots, 2 * part), F32),),
            "v" * (blocks + 3),
            [pltpu.VMEM((blocks * slots, width), BF16)],
            "hidden", micros * MICRO, 14,
        )(*ins, perm_t, down, down_s)
        return out

    def expert(ins, hg, micros):
        blocks = len(ins)
        return call(
            lambda *refs: expert_kernel(*refs, blocks=blocks),
            (shape(flat, BF16),) * blocks,
            "v" * (blocks + 5) + "aa",
            [
                pltpu.VMEM((blocks * slots, width), BF16),
                pltpu.VMEM((4, blocks * slots, part), BF16),
                pltpu.VMEM((blocks * slots, width), F32),
                pltpu.VMEM((2, width, part), BF16),
                pltpu.SemaphoreType.DMA((2,)),
            ],
            "expert", micros * MICRO, 20,
        )(*ins, hg, perm, perm_t, gate, up, gate_s, up_s)

    hidden_own = hidden((g0,), 4)
    hidden_near = hidden((g1, g2), 5)
    (p0,) = expert((n0,), hidden_own, 9)
    p0, g3 = barrier((p0, g3))
    hidden_far = hidden((g3,), 4)
    hidden_far, n1, n2 = barrier((hidden_far, n1, n2))
    p1, p2 = expert((n1, n2), hidden_near, 11)
    (p3,) = expert((n3,), hidden_far, 9)
    h1, h2 = swap(p1, 6), swap(p2, 2)
    h3 = swap(p3, 4)
    own = (p0.astype(F32) + h2.astype(F32)).astype(BF16).reshape(columns, 1, CELL, piece)
    oth = (h1.astype(F32) + h3.astype(F32)).astype(BF16).reshape(columns, 1, CELL, piece)
    home = exchange(jnp.concatenate([own, oth], axis=1))

    full = shape((count, width), F32)
    side = shape((count, width), BF16)
    v_own, v_left, v_right, attn_grad = call(
        lambda *refs: value_kernel(*refs, total_tiles=total_tiles),
        (full, side, side, side),
        "ss" + "v" * 9,
        [pltpu.VMEM((2 * slots, width), BF16), pltpu.VMEM((3 * count, width), F32)],
        "value_grad", 5 * MICRO, 20,
    )(seq, offsets, ids_t, gates_t, home, grad, unit, inv, gain, perm_t, wts)

    def finish(own_part, left_part, right_part):
        from_right = lax.ppermute(left_part, "seq", down_by).astype(F32)
        from_left = lax.ppermute(right_part, "seq", up_by).astype(F32)
        return (own_part + from_right + from_left).astype(BF16)[None]

    value_out = finish(v_own, v_left, v_right)
    k_own, k_left, k_right = call(
        lambda *refs: key_kernel(*refs, total_tiles=total_tiles),
        (full, side, side),
        "ss" + "v" * 6,
        [pltpu.VMEM((3 * count, width), BF16), pltpu.VMEM((3 * count, width), F32)],
        "key_grad", 4 * MICRO, 20,
    )(seq, offsets, attn_grad, q, vl, v, vr, wts)
    return (finish(k_own, k_left, k_right), value_out)


def solution(mesh):
    rows = P("exp", "seq", None)
    weights = P("exp", "seq", None, None)
    return jax.shard_map(
        on_device,
        mesh=mesh,
        in_specs=(rows, rows, rows, rows, P(), rows, rows, rows, weights, weights, weights),
        out_specs=(rows, rows),
        check_vma=False,
    )
```

```python
import jax
import jax.numpy as jnp
import numpy as np
from jax import lax
from jax.experimental import pallas as pl
from jax.experimental.pallas import tpu as pltpu
from jax.sharding import PartitionSpec as P

HEAD_DIM = 128
TILE = 64
NBR = 3
CAP = 5
PIECES = 8
GROUP = 8
EPSILON = 1e-06
ATTN = 8
UNROLL = 4
MICRO = 1 << 30
F32 = jnp.float32
BF16 = jnp.bfloat16

CELL = PIECES * CAP
CHUNK = GROUP * CELL
ROWS = GROUP * CAP


def shuffle_matrix():
    out = np.zeros((CHUNK, CHUNK), np.float32)
    for d in range(GROUP):
        for q in range(PIECES):
            for r in range(CAP):
                out[d * CELL + q * CAP + r, q * ROWS + d * CAP + r] = 1.0
    return out


def dot(a, b):
    return jnp.dot(a, b, preferred_element_type=F32)


def dot_nt(a, b):
    return lax.dot_general(a, b, (((1,), (1,)), ((), ())), preferred_element_type=F32)


def dot_tn(a, b):
    return lax.dot_general(a, b, (((0,), (0,)), ((), ())), preferred_element_type=F32)


def to_wire(rows_ref, base, perm, chunk, piece):
    start = base + chunk * ROWS
    stacked = jnp.concatenate(
        [rows_ref[start : start + ROWS, q * piece : (q + 1) * piece] for q in range(PIECES)], axis=0
    )
    return dot(perm, stacked.astype(BF16)).astype(BF16)


def from_wire(block_ref, rows_ref, base, perm_t, chunks, piece):
    if not isinstance(block_ref, list):
        block_ref = [block_ref[c * CHUNK : (c + 1) * CHUNK, :] for c in range(chunks)]
    for pair in range(chunks // 2):
        low = dot(perm_t, block_ref[2 * pair])
        high = dot(perm_t, block_ref[2 * pair + 1])
        start = base + 2 * pair * ROWS
        for q in range(PIECES):
            both = jnp.concatenate(
                [low[q * ROWS : (q + 1) * ROWS], high[q * ROWS : (q + 1) * ROWS]], axis=0
            )
            rows_ref[start : start + 2 * ROWS, q * piece : (q + 1) * piece] = both.astype(BF16)


def slot_rows(ids_ref, half, experts):
    tokens = ids_ref.shape[1]
    first = ids_ref[0:1, :]
    second = ids_ref[1:2, :]
    names = lax.broadcasted_iota(jnp.int32, (experts, tokens), 0)
    hot0 = (names == first).astype(F32)
    hot1 = (names == second).astype(F32)
    before = (
        lax.broadcasted_iota(jnp.int32, (tokens, tokens), 0)
        < lax.broadcasted_iota(jnp.int32, (tokens, tokens), 1)
    ).astype(F32).astype(BF16)
    seen0 = dot(hot0.astype(BF16), before)
    seen1 = dot(hot1.astype(BF16), before) + jnp.sum(hot0, axis=1, keepdims=True)
    rank0 = jnp.sum(hot0 * seen0, axis=0, keepdims=True).astype(jnp.int32)
    rank1 = jnp.sum(hot1 * seen1, axis=0, keepdims=True).astype(jnp.int32)
    slots = (experts // 2) * CAP
    slot0 = ((first & 1) ^ half) * slots + (first >> 1) * CAP + rank0
    slot1 = ((second & 1) ^ half) * slots + (second >> 1) * CAP + rank1
    return slot0, slot1


def place_rows(ids_ref, half, experts, x, rows_ref):
    slot0, slot1 = slot_rows(ids_ref, half, experts)
    places = lax.broadcasted_iota(jnp.int32, (rows_ref.shape[0], x.shape[0]), 0)
    hot = ((places == slot0) | (places == slot1)).astype(F32).astype(BF16)
    rows_ref[...] = dot(hot, x)


def send_rows(seq_ref, ids_ref, x, perm_ref, out_ref, rows_ref):
    columns = out_ref.shape[0]
    piece = out_ref.shape[3]
    place_rows(ids_ref, seq_ref[0] // 4, 2 * columns, x, rows_ref)
    perm = perm_ref[...]
    for rel in range(2):
        for chunk in range(columns // GROUP):
            block = to_wire(rows_ref, rel * columns * CAP, perm, chunk, piece)
            out_ref[chunk * GROUP : (chunk + 1) * GROUP, rel] = block.reshape(GROUP, CELL, piece)


def grad_kernel(seq_ref, ids_ref, x_ref, perm_ref, out_ref, rows_ref):
    send_rows(seq_ref, ids_ref, x_ref[...], perm_ref, out_ref, rows_ref)


def tile_places(seq_ref, offs_ref, tile, tiles, total):
    places = []
    valid = []
    for m in range(NBR):
        off = offs_ref[tile, m]
        places.append(pl.multiple_of((tile + 2 + off) * TILE, TILE))
        where = seq_ref[0] * tiles + tile + off
        valid.append((where >= 0) & (where < total))
    return places, valid


def head_spans(step, heads, tiles):
    spans = []
    for u in range(UNROLL):
        h = step * UNROLL + u
        lanes = pl.ds(pl.multiple_of(h * HEAD_DIM, HEAD_DIM), HEAD_DIM)
        spans += [(t, h, slice(t * TILE, (t + 1) * TILE), lanes) for t in range(tiles)]
    return spans


def window(ref, places, lanes):
    return jnp.concatenate([ref[pl.ds(p, TILE), lanes] for p in places], axis=0)


def fill_halo(dst_ref, left_ref, own_ref, right_ref):
    count = own_ref.shape[0]
    for i, src in enumerate((left_ref, own_ref, right_ref)):
        dst_ref[i * count : (i + 1) * count, :] = src[...]


def forward_kernel(
    seq_ref, offs_ref, ids_ref, q_ref, kl_ref, k_ref, kr_ref, vl_ref, v_ref, vr_ref, gain_ref,
    perm_ref, wts_ref, unit_ref, inv_ref, sent_ref, kx_ref, vx_ref, out_ref, rows_ref, total_tiles,
):
    fill_halo(kx_ref, kl_ref, k_ref, kr_ref)
    fill_halo(vx_ref, vl_ref, v_ref, vr_ref)
    count, width = q_ref.shape
    heads = width // HEAD_DIM
    tiles = count // TILE
    scale = HEAD_DIM ** (-0.5)
    lane = lax.broadcasted_iota(jnp.int32, (TILE, NBR * TILE), 1) // TILE
    spots = []
    biases = []
    for t in range(tiles):
        places, valid = tile_places(seq_ref, offs_ref, t, tiles, total_tiles)
        bias = jnp.zeros((TILE, NBR * TILE), F32)
        for m in range(NBR):
            lost = jnp.where(valid[m], 0.0, -jnp.inf).astype(F32)
            bias = jnp.where(lane == m, lost, bias)
        spots.append(places)
        biases.append(bias)

    def body(step, carry):
        spans = head_spans(step, heads, tiles)
        scores = [
            dot_nt(q_ref[rows, lanes], window(kx_ref, spots[t], lanes)) * scale + biases[t]
            for t, h, rows, lanes in spans
        ]
        tops = [jnp.max(x, axis=-1, keepdims=True) for x in scores]
        raised = [jnp.exp(x - top) for x, top in zip(scores, tops)]
        sums = [jnp.sum(x, axis=-1, keepdims=True) for x in raised]
        weights = [x / total for x, total in zip(raised, sums)]
        for x, (t, h, rows, lanes) in zip(weights, spans):
            wts_ref[t * heads + h] = x
            out_ref[rows, lanes] = dot(x.astype(BF16), window(vx_ref, spots[t], lanes))
        return carry

    lax.fori_loop(0, heads // UNROLL, body, 0)
    out = out_ref[...]
    inv = lax.rsqrt(jnp.mean(out * out, axis=-1, keepdims=True) + EPSILON)
    unit = out * inv
    unit_ref[...] = unit
    inv_ref[...] = jnp.broadcast_to(inv, inv_ref.shape)
    normed = (unit * gain_ref[...]).astype(BF16)
    send_rows(seq_ref, ids_ref, normed, perm_ref, sent_ref, rows_ref)


def hidden_kernel(*refs, blocks):
    ins = refs[:blocks]
    perm_t_ref, down0_ref, down1_ref, out_ref, rows_ref = refs[blocks:]
    piece = ins[0].shape[1]
    chunks = ins[0].shape[0] // CHUNK
    perm_t = perm_t_ref[...]
    for b, block in enumerate(ins):
        from_wire(block, rows_ref, b * chunks * ROWS, perm_t, chunks, piece)
    part = down0_ref.shape[0]
    for i, w_ref in enumerate((down0_ref, down1_ref)):
        out_ref[:, i * part : (i + 1) * part] = dot_nt(rows_ref[...], w_ref[...])


def expert_kernel(*refs, blocks):
    ins = refs[:blocks]
    hg_ref, perm_ref, perm_t_ref = refs[blocks : blocks + 3]
    gate_ref, up_ref, gate_hbm, up_hbm = refs[blocks + 3 : blocks + 7]
    outs = refs[blocks + 7 : 2 * blocks + 7]
    rows_ref, act_ref, total_ref, w_ref, sems = refs[2 * blocks + 7 :]
    copies = [
        pltpu.make_async_copy(src, w_ref.at[i], sems.at[i])
        for i, src in enumerate((gate_hbm, up_hbm))
    ]
    for copy in copies:
        copy.start()
    weights = (gate_ref, up_ref, w_ref.at[0], w_ref.at[1])
    piece = ins[0].shape[1]
    chunks = ins[0].shape[0] // CHUNK
    perm_t = perm_t_ref[...]
    for b, block in enumerate(ins):
        from_wire(block, rows_ref, b * chunks * ROWS, perm_t, chunks, piece)
    width, part = weights[0].shape
    for i in range(2):
        if i == 1:
            for copy in copies:
                copy.wait()
        gate_proj = dot(rows_ref[...], weights[2 * i][...])
        up_proj = dot(rows_ref[...], weights[2 * i + 1][...])
        hidden = hg_ref[:, i * part : (i + 1) * part]
        sig = jax.nn.sigmoid(gate_proj)
        act_ref[2 * i + 1] = (hidden * gate_proj * sig).astype(BF16)
        act_ref[2 * i] = (hidden * up_proj * sig * (1.0 + gate_proj * (1.0 - sig))).astype(BF16)
    for n in range(width // 512):
        cols = slice(n * 512, (n + 1) * 512)
        total = dot_nt(act_ref[0], weights[0][cols, :])
        for i in range(1, 4):
            total = total + dot_nt(act_ref[i], weights[i][cols, :])
        total_ref[:, cols] = total
    perm = perm_ref[...]
    for b, dst in enumerate(outs):
        for chunk in range(chunks):
            block = to_wire(total_ref, b * chunks * ROWS, perm, chunk, piece)
            dst[chunk * CHUNK : (chunk + 1) * CHUNK, :] = block


def backward_kernel(
    seq_ref, offs_ref, ids_ref, gates_ref, home_ref, grad_ref, unit_ref, inv_ref, gain_ref,
    perm_t_ref, q_ref, vl_ref, v_ref, vr_ref, wts_ref, k_out_ref, v_out_ref, to_left_ref,
    to_right_ref, vx_ref, rows_ref, ag_ref, ka_ref, va_ref, total_tiles,
):
    fill_halo(vx_ref, vl_ref, v_ref, vr_ref)
    count, width = q_ref.shape
    heads = width // HEAD_DIM
    tiles = count // TILE
    scale = HEAD_DIM ** (-0.5)
    ka_ref[...] = jnp.zeros_like(ka_ref)
    va_ref[...] = jnp.zeros_like(va_ref)
    columns, _, _, piece = home_ref.shape
    chunks = columns // GROUP
    perm_t = perm_t_ref[...]
    for rel in range(2):
        blocks = [
            home_ref[c * GROUP : (c + 1) * GROUP, rel].reshape(CHUNK, piece) for c in range(chunks)
        ]
        from_wire(blocks, rows_ref, rel * chunks * ROWS, perm_t, chunks, piece)
    slot0, slot1 = slot_rows(ids_ref, seq_ref[0] // 4, 2 * columns)
    places = lax.broadcasted_iota(jnp.int32, (rows_ref.shape[0], count), 0)
    mix = jnp.where(places == slot0, gates_ref[0:1, :], 0.0)
    mix = jnp.where(places == slot1, gates_ref[1:2, :], mix)
    high = mix.astype(BF16)
    low = (mix - high.astype(F32)).astype(BF16)
    normed_grad = dot_tn(high, rows_ref[...]) + dot_tn(low, rows_ref[...])
    scaled = normed_grad * gain_ref[...]
    unit = unit_ref[...]
    inner = jnp.mean(scaled * unit, axis=-1, keepdims=True)
    attn_grad = grad_ref[...].astype(F32) + inv_ref[:, 0:1] * (scaled - unit * inner)
    ag_ref[...] = attn_grad.astype(BF16)
    spots = [tile_places(seq_ref, offs_ref, t, tiles, total_tiles)[0] for t in range(tiles)]
    def body(step, carry):
        spans = head_spans(step, heads, tiles)
        prob_grads = [
            dot_nt(ag_ref[rows, lanes], window(vx_ref, spots[t], lanes))
            for t, h, rows, lanes in spans
        ]
        values = [
            dot_tn(wts_ref[t * heads + h].astype(BF16), ag_ref[rows, lanes])
            for t, h, rows, lanes in spans
        ]
        sums = [
            jnp.sum(wts_ref[t * heads + h] * x, axis=-1, keepdims=True)
            for x, (t, h, rows, lanes) in zip(prob_grads, spans)
        ]
        score_grads = [
            (wts_ref[t * heads + h] * (x - total)).astype(BF16)
            for x, total, (t, h, rows, lanes) in zip(prob_grads, sums, spans)
        ]
        keys = [
            dot_tn(x, q_ref[rows, lanes]) * scale
            for x, (t, h, rows, lanes) in zip(score_grads, spans)
        ]
        for acc_ref, parts in ((va_ref, values), (ka_ref, keys)):
            for x, (t, h, rows, lanes) in zip(parts, spans):
                for m in range(NBR):
                    acc_ref[pl.ds(spots[t][m], TILE), lanes] += x[m * TILE : (m + 1) * TILE]
        return carry

    lax.fori_loop(0, heads // UNROLL, body, 0)
    k_out_ref[...] = ka_ref[count : 2 * count, :]
    v_out_ref[...] = va_ref[count : 2 * count, :]
    to_left_ref[0] = ka_ref[0:count, :].astype(BF16)
    to_left_ref[1] = va_ref[0:count, :].astype(BF16)
    to_right_ref[0] = ka_ref[2 * count : 3 * count, :].astype(BF16)
    to_right_ref[1] = va_ref[2 * count : 3 * count, :].astype(BF16)


def call(body, outs, kinds, scratch, name, flops, megabytes):
    spaces = {"s": pltpu.SMEM, "v": pltpu.VMEM, "a": pl.ANY}
    return pl.pallas_call(
        body,
        out_shape=outs,
        in_specs=[pl.BlockSpec(memory_space=spaces[kind]) for kind in kinds],
        out_specs=[pl.BlockSpec(memory_space=pltpu.VMEM) for _ in outs],
        scratch_shapes=scratch,
        compiler_params=pltpu.CompilerParams(vmem_limit_bytes=megabytes << 20),
        cost_estimate=pl.CostEstimate(flops=flops, transcendentals=0, bytes_accessed=1 << 20),
        name=name,
    )


def shape(dims, kind):
    return jax.ShapeDtypeStruct(dims, kind)


def on_device(
    queries, keys, values, out_grad, norm_gain, gate_values, expert_ids, tile_offsets, gate_weight,
    up_weight, down_weight,
):
    count, width = queries.shape[1:]
    heads = width // HEAD_DIM
    tiles = count // TILE
    seq_count = lax.axis_size("seq")
    columns = lax.axis_size("exp")
    total_tiles = tiles * seq_count
    piece = width // PIECES
    slots = columns * CAP
    seq = lax.axis_index("seq").astype(jnp.int32).reshape(1)
    ids_t = expert_ids[0].T
    gates_t = gate_values[0].T
    offsets = tile_offsets[0]
    gain = norm_gain.reshape(1, width)
    perm = jnp.asarray(shuffle_matrix(), BF16)
    perm_t = jnp.asarray(shuffle_matrix().T, BF16)
    q, k, v, grad = queries[0], keys[0], values[0], out_grad[0]
    gate, up, down = gate_weight[0, 0], up_weight[0, 0], down_weight[0, 0]
    wire = (columns, 2, CELL, piece)
    flat = (columns * CELL, piece)

    up_by = [(i, i + 1) for i in range(seq_count - 1)]
    down_by = [(i + 1, i) for i in range(seq_count - 1)]

    def swap(x, bits):
        return lax.ppermute(x, "seq", [(i, i ^ bits) for i in range(seq_count)])

    def exchange(x):
        return lax.all_to_all(x, "exp", split_axis=0, concat_axis=0, tiled=True)

    barrier = lax.optimization_barrier
    pair = (2, count, width)
    (sent_grad,) = call(
        grad_kernel, (shape(wire, BF16),), "svvv", [pltpu.VMEM((2 * slots, width), F32)],
        "place_grad", 4 * MICRO, 56,
    )(seq, ids_t, grad, perm)
    k, v, sent_grad = barrier((k, v, sent_grad))
    kl, kr = lax.ppermute(k, "seq", up_by), lax.ppermute(k, "seq", down_by)
    vl, vr = lax.ppermute(v, "seq", up_by), lax.ppermute(v, "seq", down_by)
    got_grad = exchange(sent_grad)


    wts, unit, inv, sent = call(
        lambda *refs: forward_kernel(*refs, total_tiles=total_tiles),
        (
            shape((tiles * heads, TILE, NBR * TILE), F32),
            shape((count, width), F32),
            shape((count, HEAD_DIM), F32),
            shape(wire, BF16),
        ),
        "ssv" + "v" * 9,
        [
            pltpu.VMEM((3 * count, width), BF16),
            pltpu.VMEM((3 * count, width), BF16),
            pltpu.VMEM((count, width), F32),
            pltpu.VMEM((2 * slots, width), F32),
        ],
        "attention", ATTN * MICRO, 20,
    )(seq, offsets, ids_t, q, kl, k, kr, vl, v, vr, gain, perm)

    sent, *weights = barrier((sent, gate, up, down))
    sent, got_grad = barrier((sent, got_grad))
    gate_s, up_s, down_s = [swap(x, 1) for x in weights]
    got = exchange(sent)
    g0, grad_oth = got_grad[:, 0].reshape(flat), got_grad[:, 1].reshape(flat)
    g1, g2 = swap(grad_oth, 6), swap(g0, 2)
    g3 = swap(grad_oth, 4)
    n0, oth = got[:, 0].reshape(flat), got[:, 1].reshape(flat)
    n1, n2 = swap(oth, 6), swap(n0, 2)
    n3 = swap(n1, 2)

    part = down.shape[0]

    def hidden(ins, micros):
        blocks = len(ins)
        (out,) = call(
            lambda *refs: hidden_kernel(*refs, blocks=blocks),
            (shape((blocks * slots, 2 * part), F32),),
            "v" * (blocks + 3),
            [pltpu.VMEM((blocks * slots, width), BF16)],
            "hidden", micros * MICRO, 14,
        )(*ins, perm_t, down, down_s)
        return out

    def expert(ins, hg, micros):
        blocks = len(ins)
        return call(
            lambda *refs: expert_kernel(*refs, blocks=blocks),
            (shape(flat, BF16),) * blocks,
            "v" * (blocks + 5) + "aa",
            [
                pltpu.VMEM((blocks * slots, width), BF16),
                pltpu.VMEM((4, blocks * slots, part), BF16),
                pltpu.VMEM((blocks * slots, width), F32),
                pltpu.VMEM((2, width, part), BF16),
                pltpu.SemaphoreType.DMA((2,)),
            ],
            "expert", micros * MICRO, 20,
        )(*ins, hg, perm, perm_t, gate, up, gate_s, up_s)

    hidden_own = hidden((g0,), 4)
    hidden_near = hidden((g1, g2), 5)
    (p0,) = expert((n0,), hidden_own, 9)
    p0, g3 = barrier((p0, g3))
    hidden_far = hidden((g3,), 4)
    hidden_far, n1, n2 = barrier((hidden_far, n1, n2))
    p1, p2 = expert((n1, n2), hidden_near, 11)
    (p3,) = expert((n3,), hidden_far, 9)
    h1, h2 = swap(p1, 6), swap(p2, 2)
    h3 = swap(p3, 4)
    own = (p0.astype(F32) + h2.astype(F32)).reshape(columns, 1, CELL, piece)
    oth = (h1.astype(F32) + h3.astype(F32)).reshape(columns, 1, CELL, piece)
    home = exchange(jnp.concatenate([own, oth], axis=1).astype(BF16))

    k_own, v_own, to_left, to_right = call(
        lambda *refs: backward_kernel(*refs, total_tiles=total_tiles),
        (shape((count, width), F32), shape((count, width), F32), shape(pair, BF16), shape(pair, BF16)),
        "ss" + "v" * 13,
        [
            pltpu.VMEM((3 * count, width), BF16),
            pltpu.VMEM((2 * slots, width), BF16),
            pltpu.VMEM((count, width), BF16),
            pltpu.VMEM((3 * count, width), F32),
            pltpu.VMEM((3 * count, width), F32),
        ],
        "attention_grad", 10 * MICRO, 24,
    )(seq, offsets, ids_t, gates_t, home, grad, unit, inv, gain, perm_t, q, vl, v, vr, wts)
    from_right = lax.ppermute(to_left, "seq", down_by).astype(F32)
    from_left = lax.ppermute(to_right, "seq", up_by).astype(F32)

    def finish(own_part, i):
        return (own_part + from_right[i] + from_left[i]).astype(BF16)[None]

    return (finish(k_own, 0), finish(v_own, 1))


def solution(mesh):
    rows = P("exp", "seq", None)
    weights = P("exp", "seq", None, None)
    return jax.shard_map(
        on_device,
        mesh=mesh,
        in_specs=(rows, rows, rows, rows, P(), rows, rows, rows, weights, weights, weights),
        out_specs=(rows, rows),
        check_vma=False,
    )
```
